32 devices in a mesh: grp: 4 (over y, x), wide: 8 (over z, core).
Axes of the slice: x: 2, y: 2, z: 4, core: 2. Of those that a mesh axis runs over, the one named last changes fastest.
Arguments:
- fine_pop: float32 [64, 19, 4096], P(('grp', 'wide')), may hold values from 0 to 1, as said below
- coarse_pop: float32 [19, 32, 8, 1024], P(None, 'grp', None, 'wide'), may hold values from 0 to 1, as said below
- new_slot: int32 [64], replicated, may hold values from 0 to 63, each once
Outputs:
- fine_out: float32 [64, 19, 4096], P(('grp', 'wide'))
- coarse_out: float32 [19, 32, 8, 1024], P(None, 'grp', None, 'wide')
The draws below stay inside these ranges and needn't reach their ends.
Inputs may be any that keep to these rules, and one draw needn't show every extreme that they name: A permutation: fine block b moves to slot new_slot[b]. `fine_pop`: positive populations near equilibrium, densities of order one, speeds under 0.25. `coarse_pop`: positive populations near equilibrium, densities of order one, speeds under 0.25.
All inputs are finite; a program needn't handle non-finite values.
Results may differ from the reference program's by a relative error of at most 0.00002.
Values sent between devices are 32-bit elements; how exact they have to be, the bound alone decides.
No kernel may reach another device: no remote copies, remote signals or barrier semaphores. Data moves between devices by JAX's collectives and lax.ppermute only.
A program may use at most 128 MiB of HBM per device.

```python
import jax
import jax.numpy as jnp
from jax import lax

B = 16
FB_DEV = 2
CY = 128
FINE_BLOCKS = 64
COARSE_X = 32
COARSE_Y = 1024
N_GRP = 4
N_WIDE = 8


VELOCITIES = ((0, 0, 0), (1, 0, 0), (-1, 0, 0), (0, 1, 0), (0, -1, 0), (0, 0, 1), (0, 0, -1), (1, 1, 0), (-1, -1, 0), (1, -1, 0), (-1, 1, 0), (1, 0, 1), (-1, 0, -1), (1, 0, -1), (-1, 0, 1), (0, 1, 1), (0, -1, -1), (0, 1, -1), (0, -1, 1))


WEIGHTS = (1.0 / 3.0,) + (1.0 / 18.0,) * 6 + (1.0 / 36.0,) * 12


def draw_state(key, leading, cell_count):
    subkeys = jax.random.split(key, 5)
    density = jax.random.uniform(subkeys[1], (leading, cell_count), jnp.float32, minval=0.5, maxval=1.5)
    motion = jnp.zeros((leading, 3, 1), jnp.float32)
    velocity = jnp.clip(0.04 * jax.random.normal(subkeys[2], (leading, 3, cell_count), jnp.float32) + motion, -0.12, 0.12)
    jitter = jnp.clip(0.1 * jax.random.normal(subkeys[3], (leading, 19, cell_count), jnp.float32), -0.3, 0.3)
    squared = velocity[:, 0] * velocity[:, 0] + velocity[:, 1] * velocity[:, 1] + velocity[:, 2] * velocity[:, 2]
    entries = []
    for direction in range(19):
        offset = VELOCITIES[direction]
        projected = offset[0] * velocity[:, 0] + offset[1] * velocity[:, 1] + offset[2] * velocity[:, 2]
        entries.append(WEIGHTS[direction] * density * (1.0 + 3.0 * projected + 4.5 * projected * projected - 1.5 * squared))
    return jnp.stack(entries, axis=1) * (1.0 + jitter)


def draw_fine_pop(key, part):
    return draw_state(key, FINE_BLOCKS, B ** 3)


def draw_coarse_pop(key, part):
    values = draw_state(key, COARSE_X, B // 2 * COARSE_Y)
    return values.transpose(1, 0, 2).reshape(19, COARSE_X, B // 2, COARSE_Y)


def setup_inputs(seed: int = 0) -> dict:
    keys = jax.random.split(jax.random.key(seed), 4)
    fine_pop = draw_fine_pop(jax.random.fold_in(keys[3], 71), 0)
    coarse_pop = draw_coarse_pop(jax.random.fold_in(keys[3], 71), 0)
    new_slot = jax.random.permutation(keys[2], FINE_BLOCKS).astype(jnp.int32)
    return dict(fine_pop=fine_pop, coarse_pop=coarse_pop, new_slot=new_slot)


VELOCITIES = ((0, 0, 0), (1, 0, 0), (-1, 0, 0), (0, 1, 0), (0, -1, 0), (0, 0, 1), (0, 0, -1),
              (1, 1, 0), (-1, -1, 0), (1, -1, 0), (-1, 1, 0), (1, 0, 1), (-1, 0, -1), (1, 0, -1),
              (-1, 0, 1), (0, 1, 1), (0, -1, -1), (0, 1, -1), (0, -1, 1))
WEIGHTS = (1.0 / 3.0,) + (1.0 / 18.0,) * 6 + (1.0 / 36.0,) * 12
COUPLING = -5.0
FINE_TAU = 1.1
COARSE_TAU = 0.8
TO_COARSE = 2.0 * COARSE_TAU / FINE_TAU
TO_FINE = FINE_TAU / (2.0 * COARSE_TAU)


def moments(state):
    density = state[0]
    momentum = [jnp.zeros_like(state[0]), jnp.zeros_like(state[0]), jnp.zeros_like(state[0])]
    for direction in range(1, 19):
        offset = VELOCITIES[direction]
        density = density + state[direction]
        for component in range(3):
            if offset[component] != 0:
                momentum[component] = momentum[component] + offset[component] * state[direction]
    return density, momentum


def equilibrium(density, velocity):
    squared = velocity[0] * velocity[0] + velocity[1] * velocity[1] + velocity[2] * velocity[2]
    entries = []
    for direction in range(19):
        offset = VELOCITIES[direction]
        projected = jnp.zeros_like(density)
        for component in range(3):
            if offset[component] != 0:
                projected = projected + offset[component] * velocity[component]
        entries.append(WEIGHTS[direction] * density * (1.0 + 3.0 * projected + 4.5 * projected * projected - 1.5 * squared))
    return jnp.stack(entries)


def rescale(state, factor):
    density, momentum = moments(state)
    velocity = []
    for component in range(3):
        velocity.append(momentum[component] / density)
    balance = equilibrium(density, velocity)
    return balance + factor * (state - balance)


def restrict(layers):
    extent_x = layers.shape[1]
    extent_z = layers.shape[2]
    grouped = layers.reshape(layers.shape[0], extent_x // 2, 2, extent_z // 2, 2, 2)
    return 0.125 * jnp.sum(grouped, axis=(2, 4, 5))


def upsample(boundary):
    return jnp.repeat(jnp.repeat(boundary, 2, axis=-2), 2, axis=-1)


def window(padded, shift_x, shift_y, shift_z):
    extent_x = padded.shape[-3] - 2
    extent_z = padded.shape[-2] - 2
    extent_y = padded.shape[-1] - 2
    return padded[..., 1 + shift_x:1 + shift_x + extent_x, 1 + shift_z:1 + shift_z + extent_z, 1 + shift_y:1 + shift_y + extent_y]


def collide(state, density, momentum, potential, padded_potential, relaxation):
    gradient = [jnp.zeros_like(density), jnp.zeros_like(density), jnp.zeros_like(density)]
    for direction in range(1, 19):
        offset = VELOCITIES[direction]
        neighbor = window(padded_potential, offset[0], offset[1], offset[2])
        for component in range(3):
            if offset[component] != 0:
                gradient[component] = gradient[component] + (WEIGHTS[direction] * offset[component]) * neighbor
    velocity = []
    for component in range(3):
        velocity.append((momentum[component] - relaxation * COUPLING * potential * gradient[component]) / density)
    balance = equilibrium(density, velocity)
    return state + (balance - state) / relaxation


def propagate(padded_post):
    entries = []
    for direction in range(19):
        offset = VELOCITIES[direction]
        entries.append(window(padded_post[direction], -offset[0], -offset[1], -offset[2]))
    return jnp.stack(entries)


def lattice_step(state, relaxation, ghosts):
    potential_low, potential_high, post_low, post_high = ghosts
    density, momentum = moments(state)
    potential = 1.0 - jnp.exp(-density)
    padded_potential = pad_slab(potential[None], potential_low[None], potential_high[None])[0]
    post = collide(state, density, momentum, potential, padded_potential, relaxation)
    return propagate(pad_slab(post, post_low, post_high))


def coarse_ghosts(restricted):
    density, momentum = moments(restricted)
    return 1.0 - jnp.exp(-density), rescale(restricted, TO_COARSE)


def fine_ghosts(boundary):
    density, momentum = moments(boundary)
    return upsample(1.0 - jnp.exp(-density)), upsample(rescale(boundary, TO_FINE))


def pad_slab(state, ghost_low, ghost_high):
    with_rows = jnp.concatenate([ghost_low[..., None], state, ghost_high[..., None]], axis=3)
    with_sides = jnp.concatenate([with_rows[:, -1:], with_rows, with_rows[:, :1]], axis=1)
    return jnp.concatenate([with_sides[:, :, -1:], with_sides, with_sides[:, :, :1]], axis=2)


def slab_update(items):
    fine_slab, coarse_slab, next_first, previous_last = items
    low_potential, low_post = coarse_ghosts(restrict(fine_slab[..., -2:]))
    high_potential, high_post = coarse_ghosts(restrict(next_first))
    coarse_new = lattice_step(coarse_slab, COARSE_TAU, (low_potential, high_potential, low_post, high_post))
    fine_low_potential, fine_low_post = fine_ghosts(previous_last)
    fine_high_potential, fine_high_post = fine_ghosts(coarse_slab[..., 0])
    ghosts = (fine_low_potential, fine_high_potential, fine_low_post, fine_high_post)
    for substep in range(2):
        fine_slab = lattice_step(fine_slab, FINE_TAU, ghosts)
    return fine_slab, coarse_new


def reference(fine_pop, coarse_pop, new_slot):
    block_count = new_slot.shape[0]
    inverse = jnp.zeros((block_count,), jnp.int32).at[new_slot].set(jnp.arange(block_count, dtype=jnp.int32))
    arranged = fine_pop[inverse]
    fine_slabs = arranged.reshape(N_GRP, N_WIDE, FB_DEV, 19, B, B, B).transpose(1, 3, 0, 4, 5, 2, 6)
    fine_slabs = fine_slabs.reshape(N_WIDE, 19, N_GRP * B, B, FB_DEV * B)
    coarse_slabs = coarse_pop.reshape(19, COARSE_X, B // 2, N_WIDE, CY).transpose(3, 0, 1, 2, 4)
    next_first = jnp.roll(fine_slabs[..., :2], -1, axis=0)
    previous_last = jnp.roll(coarse_slabs[..., -1], 1, axis=0)
    fine_new, coarse_new = lax.map(slab_update, (fine_slabs, coarse_slabs, next_first, previous_last))
    fine_out = fine_new.reshape(N_WIDE, 19, N_GRP, B, B, FB_DEV, B).transpose(2, 0, 5, 1, 3, 4, 6)
    fine_out = fine_out.reshape(block_count, 19, B ** 3)
    coarse_out = coarse_new.transpose(1, 2, 3, 0, 4).reshape(19, COARSE_X, B // 2, N_WIDE * CY)
    return fine_out, coarse_out
```

```python
import functools

import jax
import jax.numpy as jnp
from jax import lax
from jax.experimental import pallas as pl
from jax.experimental.pallas import tpu as pltpu
from jax.sharding import PartitionSpec as P

B = 16
LANES = 128
SUB = 8
HALO = 4
PAD = 8

VELOCITIES = (
    (0, 0, 0),
    (1, 0, 0),
    (-1, 0, 0),
    (0, 1, 0),
    (0, -1, 0),
    (0, 0, 1),
    (0, 0, -1),
    (1, 1, 0),
    (-1, -1, 0),
    (1, -1, 0),
    (-1, 1, 0),
    (1, 0, 1),
    (-1, 0, -1),
    (1, 0, -1),
    (-1, 0, 1),
    (0, 1, 1),
    (0, -1, -1),
    (0, 1, -1),
    (0, -1, 1),
)
Q = len(VELOCITIES)
WEIGHTS = (1.0 / 3.0,) + (1.0 / 18.0,) * 6 + (1.0 / 36.0,) * 12
W_AXIS = WEIGHTS[1]
W_DIAG = WEIGHTS[7]
COUPLING = -5.0
FINE_TAU = 1.1
COARSE_TAU = 0.8
TO_COARSE = 2.0 * COARSE_TAU / FINE_TAU
TO_FINE = FINE_TAU / (2.0 * COARSE_TAU)
UP = tuple(i for i in range(Q) if VELOCITIES[i][1] == 1)
DOWN = tuple(i for i in range(Q) if VELOCITIES[i][1] == -1)
NG = len(UP) + 1

VMEM = pl.BlockSpec(memory_space=pltpu.VMEM)
SMEM = pl.BlockSpec(memory_space=pltpu.SMEM)


def call(body, outs, specs, scratch=(), flops=10**6, moved=10**6):
    return pl.pallas_call(
        body,
        out_shape=outs,
        in_specs=specs,
        out_specs=jax.tree.map(lambda _: VMEM, outs),
        scratch_shapes=list(scratch),
        cost_estimate=pl.CostEstimate(flops=flops, bytes_accessed=moved, transcendentals=0),
    )


def f32(*shape):
    return jax.ShapeDtypeStruct(shape, jnp.float32)


def moments(f):
    density = f[0]
    momentum = [None, None, None]
    for i in range(1, Q, 2):
        density = density + (f[i] + f[i + 1])
        odd = f[i] - f[i + 1]
        for j in range(3):
            c = VELOCITIES[i][j]
            if c:
                term = odd if c > 0 else -odd
                if momentum[j] is None:
                    momentum[j] = term
                else:
                    momentum[j] = momentum[j] + odd if c > 0 else momentum[j] - odd
    return density, momentum


def balances(density, u, scale):
    base = 1.0 - 1.5 * (u[0] * u[0] + u[1] * u[1] + u[2] * u[2])
    scaled = {w: density * (w * scale) for w in set(WEIGHTS)}
    yield 0, scaled[WEIGHTS[0]] * base
    for i in range(1, Q, 2):
        along = None
        for j in range(3):
            c = VELOCITIES[i][j]
            if c:
                if along is None:
                    along = u[j] if c > 0 else -u[j]
                else:
                    along = along + u[j] if c > 0 else along - u[j]
        weight = scaled[WEIGHTS[i]]
        even = weight * (base + 4.5 * (along * along))
        odd = weight * (3.0 * along)
        yield i, even + odd
        yield i + 1, even - odd


def rescaled(f, factor, wanted):
    density, momentum = moments(f)
    inverse = 1.0 / density
    u = [m * inverse for m in momentum]
    found = {}
    for i, balance in balances(density, u, 1.0):
        if i in wanted:
            found[i] = balance + factor * (f[i] - balance)
    return 1.0 - jnp.exp(-density), found


def gradient_parts(p, shift_y, shift_z):
    above = shift_y(p, -1, "p")
    below = shift_y(p, 1, "p")
    front = shift_z(p, -1)
    back = shift_z(p, 1)
    n = range(len(p))
    dy = [above[q] - below[q] for q in n]
    sy = [above[q] + below[q] for q in n]
    dz = [front[q] - back[q] for q in n]
    tx = [W_AXIS * p[q] + W_DIAG * (sy[q] + (front[q] + back[q])) for q in n]
    mixed = [W_AXIS * p[q] + W_DIAG * sy[q] for q in n]
    mixed_front = shift_z(mixed, -1)
    mixed_back = shift_z(mixed, 1)
    dy_front = shift_z(dy, -1)
    dy_back = shift_z(dy, 1)
    gy = [W_AXIS * dy[q] + W_DIAG * (dy_front[q] + dy_back[q]) for q in n]
    gz = [mixed_front[q] - mixed_back[q] for q in n]
    return tx, [W_DIAG * v for v in dy], [W_DIAG * v for v in dz], gy, gz


def velocity_of(density, momentum, potential, pull, tau):
    inverse = 1.0 / density
    force = (-tau * COUPLING) * potential
    return [(momentum[j] + force * pull[j]) * inverse for j in range(3)]


def regroup_body(blocks, k_blocks, rows, slot_ref, in_ref, out_ref):
    def step(b, carry):
        s = slot_ref[b]
        source = (b // k_blocks) * (rows * k_blocks) + b % k_blocks
        target = (s // k_blocks) * (rows * k_blocks) + s % k_blocks
        out_ref[pl.ds(target, rows, stride=k_blocks), :] = in_ref[
            pl.ds(source, rows, stride=k_blocks), :
        ]
        return carry

    lax.fori_loop(0, blocks, step, 0, unroll=4)


def lane_ids():
    lane = lax.broadcasted_iota(jnp.int32, (SUB, LANES), 1)
    return lane % B, lane // B


def fine_shifts(ch_count, k_count, ghost):
    y, z = lane_ids()
    first_y, last_y = y == 0, y == B - 1
    first_z, last_z = z == 0, z == LANES // B - 1

    def shift_y(v, c, which):
        out = []
        for ch in range(ch_count):
            for k in range(k_count):
                q = ch * k_count + k
                if c > 0:
                    own = pltpu.roll(v[q], 1, 1)
                    carry = (
                        ghost(0, which, ch) if k == 0 else pltpu.roll(v[q - 1], LANES - (B - 1), 1)
                    )
                    out.append(jnp.where(first_y, carry, own))
                else:
                    own = pltpu.roll(v[q], LANES - 1, 1)
                    carry = (
                        ghost(1, which, ch)
                        if k == k_count - 1
                        else pltpu.roll(v[q + 1], B - 1, 1)
                    )
                    out.append(jnp.where(last_y, carry, own))
        return out

    def shift_z(v, c):
        rolled = [pltpu.roll(x, B if c > 0 else LANES - B, 1) for x in v]
        edge = first_z if c > 0 else last_z
        out = []
        for ch in range(ch_count):
            other = (ch - c) % ch_count
            for k in range(k_count):
                q = ch * k_count + k
                out.append(jnp.where(edge, rolled[other * k_count + k], rolled[q]))
        return out

    return shift_y, shift_z


def fine_step(src, offset, dst, ghosts, parts, ch_count, k_count, chunks):
    nq = ch_count * k_count
    qs = range(nq)
    for chunk in range(chunks):
        r = chunk * SUB
        f = [[src[i, q, pl.ds(offset + r, SUB), :] for i in range(Q)] for q in qs]
        moved = [moments(f[q]) for q in qs]
        p = [1.0 - jnp.exp(-moved[q][0]) for q in qs]

        def ghost(side, which, ch, r=r):
            return ghosts[side, NG - 1, ch, pl.ds(r, SUB), :]

        shift_y, shift_z = fine_shifts(ch_count, k_count, ghost)
        tx, dy, dz, gy, gz = gradient_parts(p, shift_y, shift_z)
        for q in qs:
            values = (tx[q], dy[q], dz[q], gy[q], gz[q], p[q], moved[q][0], *moved[q][1])
            for n, v in enumerate(values):
                parts[n, q, pl.ds(PAD + r, SUB), :] = v
    for chunk in range(chunks):
        r = chunk * SUB

        def ghost(side, which, ch, r=r):
            place = (UP if side == 0 else DOWN).index(which)
            return ghosts[side, place, ch, pl.ds(r, SUB), :]

        shift_y, shift_z = fine_shifts(ch_count, k_count, ghost)
        density, streams = [], []
        for q in qs:
            low = [parts[n, q, pl.ds(PAD + r - 1, SUB), :] for n in range(3)]
            high = [parts[n, q, pl.ds(PAD + r + 1, SUB), :] for n in range(3)]
            gy, gz, p, rho, mx, my, mz = (
                parts[n, q, pl.ds(PAD + r, SUB), :] for n in range(3, 10)
            )
            pull = [high[0] - low[0], gy + (high[1] + low[1]), gz + (high[2] + low[2])]
            u = velocity_of(rho, (mx, my, mz), p, pull, FINE_TAU)
            streams.append(balances(rho, u, 1.0 / FINE_TAU))
        for i in range(Q):
            cx, cy, cz = VELOCITIES[i]
            post = []
            for q in qs:
                _, balance = next(streams[q])
                h = src[i, q, pl.ds(offset + r, SUB), :]
                post.append(h * (1.0 - 1.0 / FINE_TAU) + balance)
            if cy:
                post = shift_y(post, cy, i)
            if cz:
                post = shift_z(post, cz)
            for q in qs:
                dst[i, q, pl.ds(PAD + r + cx, SUB), :] = post[q]


def fine_body(ch_count, k_count, own, left, right, ghosts, out, first, second, third, parts):
    nq = ch_count * k_count

    def gather(i, carry):
        for q in range(nq):
            first[i, q, pl.ds(0, HALO), :] = left[pl.ds(i * (HALO * nq) + q, HALO, stride=nq), :]
            first[i, q, pl.ds(HALO, B), :] = own[pl.ds(i * (B * nq) + q, B, stride=nq), :]
            first[i, q, pl.ds(HALO + B, HALO), :] = right[
                pl.ds(i * (HALO * nq) + q, HALO, stride=nq), :
            ]
        return carry

    lax.fori_loop(0, Q, gather, 0)
    chunks = (B + 2 * HALO) // SUB
    fine_step(first, 0, second, ghosts, parts, ch_count, k_count, chunks)
    fine_step(second, PAD, third, ghosts, parts, ch_count, k_count, chunks)

    def scatter(i, carry):
        for q in range(nq):
            out[pl.ds(i * (B * nq) + q, B, stride=nq), :] = third[i, q, pl.ds(PAD + HALO, B), :]
        return carry

    lax.fori_loop(0, Q, scatter, 0)


def fine_ghost_body(ch_count, rows, layers, spread, out, wide):
    for side in range(2):
        wide[...] = jnp.dot(
            layers[side],
            spread[...],
            precision=lax.Precision.HIGHEST,
            preferred_element_type=jnp.float32,
        )
        wanted = UP if side == 0 else DOWN
        for ch in range(ch_count):
            for r in range(0, rows, SUB):
                f = [
                    wide[pl.ds(i * rows + r, SUB), pl.ds(ch * LANES, LANES)] for i in range(Q)
                ]
                potential, found = rescaled(f, TO_FINE, wanted)
                for n, i in enumerate(wanted):
                    out[side, n, ch, pl.ds(r, SUB), :] = found[i]
                out[side, NG - 1, ch, pl.ds(r, SUB), :] = potential


STRIDE = 32
PER = LANES // STRIDE


def restrict_body(ch_count, k_count, own, left, right, out, buffer):
    nq = ch_count * k_count
    row = lax.broadcasted_iota(jnp.int32, (LANES, LANES), 0)
    col = lax.broadcasted_iota(jnp.int32, (LANES, LANES), 1)
    for side in range(2):
        k = k_count - 1 if side == 0 else 0
        y = row % B
        picked = (y >= B - 2) if side == 0 else (y < 2)
        total = None
        for ch in range(ch_count):
            q = ch * k_count + k

            def gather(i, carry, ch=ch, q=q):
                at = i * STRIDE
                buffer[ch, pl.ds(at, HALO), :] = left[
                    pl.ds(i * (HALO * nq) + q, HALO, stride=nq), :
                ]
                buffer[ch, pl.ds(at + HALO, B), :] = own[pl.ds(i * (B * nq) + q, B, stride=nq), :]
                buffer[ch, pl.ds(at + HALO + B, HALO), :] = right[
                    pl.ds(i * (HALO * nq) + q, HALO, stride=nq), :
                ]
                buffer[ch, pl.ds(at + 2 * HALO + B, STRIDE - 2 * HALO - B), :] = jnp.zeros(
                    (STRIDE - 2 * HALO - B, LANES), jnp.float32
                )
                return carry

            lax.fori_loop(0, Q, gather, 0)
            coarse_z = ch * (LANES // B // 2) + row // (2 * B)
            select = jnp.where(picked & (coarse_z == col), 0.125, 0.0).astype(jnp.float32)
            part = jnp.dot(
                buffer[ch, pl.ds(0, Q * STRIDE), :],
                select,
                precision=lax.Precision.HIGHEST,
                preferred_element_type=jnp.float32,
            )
            total = part if total is None else total + part
        for n in range(pl.cdiv(Q, PER)):
            count = min(PER, Q - n * PER) * STRIDE
            block = total[n * LANES : n * LANES + count]
            if count < LANES:
                block = jnp.concatenate(
                    [block, jnp.zeros((LANES - count, LANES), jnp.float32)], axis=0
                )
            out[side, n] = block.T[:SUB]


def coarse_body(planes, state, low, high, out, ghosts, parts):
    lane = lax.broadcasted_iota(jnp.int32, (SUB, LANES), 1)
    first_y, last_y = lane == 0, lane == LANES - 1

    for side, ref in enumerate((low, high)):
        paired = []
        for n in range(pl.cdiv(Q, PER)):
            v = ref[n]
            paired.append(v + pltpu.roll(v, LANES - 1, 1))
        f = []
        for i in range(Q):
            s = (i % PER) * STRIDE
            f.append(paired[i // PER] if s == 0 else pltpu.roll(paired[i // PER], LANES - s, 1))
        wanted = UP if side == 0 else DOWN
        potential, found = rescaled(f, TO_COARSE, wanted)
        for n, v in enumerate([found[i] for i in wanted] + [potential]):
            for x in range(planes):
                ghosts[side, n, x] = jnp.broadcast_to(v[:, 2 * x : 2 * x + 1], (SUB, LANES))

    def shifts(x):
        def shift_y(v, c, which):
            side = 0 if c > 0 else 1
            place = NG - 1 if which == "p" else (UP if c > 0 else DOWN).index(which)
            carry = ghosts[side, place, x]
            own = pltpu.roll(v[0], 1 if c > 0 else LANES - 1, 1)
            return [jnp.where(first_y if c > 0 else last_y, carry, own)]

        def shift_z(v, c):
            return [pltpu.roll(v[0], 1 if c > 0 else SUB - 1, 0)]

        return shift_y, shift_z

    def prepare(x, carry):
        density, momentum = moments([state[i, x] for i in range(Q)])
        p = 1.0 - jnp.exp(-density)
        values = gradient_parts([p], *shifts(x))
        values = [v[0] for v in values] + [p, density, *momentum]
        for n, v in enumerate(values):
            parts[n, x] = v
        return carry

    lax.fori_loop(0, planes, prepare, 0, unroll=2)

    inner = planes - 2 * (HALO // 2)
    base = HALO // 2

    def update(x, carry):
        shift_y, shift_z = shifts(x)
        lower = [parts[n, x - 1] for n in range(3)]
        upper = [parts[n, x + 1] for n in range(3)]
        gy, gz, p, rho, mx, my, mz = (parts[n, x] for n in range(3, 10))
        pull = [upper[0] - lower[0], gy + (upper[1] + lower[1]), gz + (upper[2] + lower[2])]
        u = velocity_of(rho, (mx, my, mz), p, pull, COARSE_TAU)
        for i, balance in balances(rho, u, 1.0 / COARSE_TAU):
            cx, cy, cz = VELOCITIES[i]
            post = [state[i, x] * (1.0 - 1.0 / COARSE_TAU) + balance]
            if cy:
                post = shift_y(post, cy, i)
            if cz:
                post = shift_z(post, cz)
            out[i, x + cx] = post[0]
        return carry

    lax.fori_loop(base - 1, base + inner + 1, update, 0, unroll=2)


def ring(axis, count, step):
    return [(i, (i + step) % count) for i in range(count)]


def local(fine_pop, coarse_pop, new_slot):
    k_count, q_count, cells = fine_pop.shape
    blocks = new_slot.shape[0]
    devices = blocks // k_count
    tiles = cells // LANES
    ch_count = tiles // B
    nq = ch_count * k_count
    axes = ("grp", "wide")
    n_grp, n_wide = lax.axis_size("grp"), lax.axis_size("wide")
    _, cx, cz, cy = coarse_pop.shape
    planes = cx + HALO
    fine_rows = B + 2 * HALO

    rows = pl.cdiv(Q * tiles, devices)
    pieces = fine_pop.reshape(k_count, Q, tiles, LANES).transpose(1, 2, 0, 3)
    pieces = pieces.reshape(Q * tiles, k_count, LANES)
    if rows * devices != Q * tiles:
        pieces = jnp.pad(pieces, ((0, rows * devices - Q * tiles), (0, 0), (0, 0)))
    pieces = pieces.reshape(devices, rows, k_count, LANES)
    spread = lax.all_to_all(pieces, axes, 0, 0, tiled=True)
    total = devices * rows * k_count
    regroup = call(
        functools.partial(regroup_body, blocks, k_count, rows),
        f32(total, LANES),
        [SMEM, VMEM],
        moved=8 * total * LANES,
    )
    outgoing = regroup(new_slot, spread.reshape(total, LANES))
    arrived = lax.all_to_all(
        outgoing.reshape(devices, rows, k_count, LANES), axes, 0, 0, tiled=True
    )
    own = arrived.reshape(total, LANES)[: Q * tiles * k_count]

    edge = HALO // 2
    coarse_left = lax.ppermute(coarse_pop[:, cx - edge :], "grp", ring("grp", n_grp, 1))
    coarse_right = lax.ppermute(coarse_pop[:, :edge], "grp", ring("grp", n_grp, -1))
    coarse = jnp.concatenate([coarse_left, coarse_pop, coarse_right], axis=1)
    below = lax.ppermute(coarse[..., -1], "wide", ring("wide", n_wide, 1))
    layers = jnp.repeat(jnp.stack([below, coarse[..., 0]]), 2, axis=2)
    layers = layers.reshape(2, Q * fine_rows, cz)
    lane = jnp.arange(ch_count * LANES) // (2 * B)
    one_hot = (jnp.arange(cz)[:, None] == lane[None, :]).astype(jnp.float32)
    fine_ghosts = call(
        functools.partial(fine_ghost_body, ch_count, fine_rows),
        f32(2, NG, ch_count, fine_rows, LANES),
        [VMEM, VMEM],
        [pltpu.VMEM((Q * fine_rows, ch_count * LANES), jnp.float32)],
    )(layers, one_hot)

    by_x = own.reshape(Q, B * nq, LANES)
    width = HALO * nq
    left = lax.ppermute(by_x[:, -width:], "grp", ring("grp", n_grp, 1)).reshape(Q * width, LANES)
    right = lax.ppermute(by_x[:, :width], "grp", ring("grp", n_grp, -1)).reshape(Q * width, LANES)

    groups = pl.cdiv(Q, PER)
    restricted = call(
        functools.partial(restrict_body, ch_count, k_count),
        f32(2, groups, SUB, LANES),
        [VMEM, VMEM, VMEM],
        [pltpu.VMEM((ch_count, Q * STRIDE, LANES), jnp.float32)],
    )(own, left, right)
    high = lax.ppermute(restricted[1], "wide", ring("wide", n_wide, -1))

    padded = PAD + fine_rows + PAD
    fine = call(
        functools.partial(fine_body, ch_count, k_count),
        f32(Q * B * nq, LANES),
        [VMEM] * 4,
        [
            pltpu.VMEM((Q, nq, fine_rows, LANES), jnp.float32),
            pltpu.VMEM((Q, nq, padded, LANES), jnp.float32),
            pltpu.VMEM((Q, nq, padded, LANES), jnp.float32),
            pltpu.VMEM((10, nq, padded, LANES), jnp.float32),
        ],
        flops=10**7,
    )(own, left, right, fine_ghosts)

    coarse_new = call(
        functools.partial(coarse_body, planes),
        f32(Q, planes, cz, cy),
        [VMEM] * 3,
        [
            pltpu.VMEM((2, NG, planes, SUB, LANES), jnp.float32),
            pltpu.VMEM((10, planes, SUB, LANES), jnp.float32),
        ],
        flops=10**7,
    )(coarse, restricted[0], high)
    coarse_out = coarse_new[:, edge : edge + cx]

    fine_out = fine.reshape(Q, tiles, k_count, LANES).transpose(2, 0, 1, 3)
    fine_out = fine_out.reshape(k_count, q_count, cells)
    return fine_out, coarse_out


def solution(mesh):
    return jax.shard_map(
        local,
        mesh=mesh,
        in_specs=(P(("grp", "wide"), None, None), P(None, "grp", None, "wide"), P()),
        out_specs=(P(("grp", "wide"), None, None), P(None, "grp", None, "wide")),
        check_vma=False,
    )
```

```python
import functools

import jax
import jax.numpy as jnp
from jax import lax
from jax.experimental import pallas as pl
from jax.experimental.layout import Layout, with_layout_constraint
from jax.experimental.pallas import tpu as pltpu
from jax.sharding import PartitionSpec as P

B = 16
LANES = 128
SUB = 8
HALO = 4
PAD = 8
GRANT = 24 << 20

VELOCITIES = (
    (0, 0, 0),
    (1, 0, 0),
    (-1, 0, 0),
    (0, 1, 0),
    (0, -1, 0),
    (0, 0, 1),
    (0, 0, -1),
    (1, 1, 0),
    (-1, -1, 0),
    (1, -1, 0),
    (-1, 1, 0),
    (1, 0, 1),
    (-1, 0, -1),
    (1, 0, -1),
    (-1, 0, 1),
    (0, 1, 1),
    (0, -1, -1),
    (0, 1, -1),
    (0, -1, 1),
)
Q = len(VELOCITIES)
WEIGHTS = (1.0 / 3.0,) + (1.0 / 18.0,) * 6 + (1.0 / 36.0,) * 12
W_AXIS = WEIGHTS[1]
W_DIAG = WEIGHTS[7]
COUPLING = -5.0
FINE_TAU = 1.1
COARSE_TAU = 0.8
TO_COARSE = 2.0 * COARSE_TAU / FINE_TAU
TO_FINE = FINE_TAU / (2.0 * COARSE_TAU)
UP = tuple(i for i in range(Q) if VELOCITIES[i][1] == 1)
DOWN = tuple(i for i in range(Q) if VELOCITIES[i][1] == -1)
NG = len(UP) + 1

VMEM = pl.BlockSpec(memory_space=pltpu.VMEM)
SMEM = pl.BlockSpec(memory_space=pltpu.SMEM)


def call(body, outs, specs, scratch=(), flops=10**6, moved=10**6):
    return pl.pallas_call(
        body,
        out_shape=outs,
        in_specs=specs,
        out_specs=jax.tree.map(lambda _: VMEM, outs),
        scratch_shapes=list(scratch),
        cost_estimate=pl.CostEstimate(flops=flops, bytes_accessed=moved, transcendentals=0),
        compiler_params=pltpu.CompilerParams(vmem_limit_bytes=GRANT),
    )


def f32(*shape):
    return jax.ShapeDtypeStruct(shape, jnp.float32)


def moments(f):
    density = f[0]
    momentum = [None, None, None]
    for i in range(1, Q, 2):
        density = density + (f[i] + f[i + 1])
        odd = f[i] - f[i + 1]
        for j in range(3):
            c = VELOCITIES[i][j]
            if c:
                term = odd if c > 0 else -odd
                if momentum[j] is None:
                    momentum[j] = term
                else:
                    momentum[j] = momentum[j] + odd if c > 0 else momentum[j] - odd
    return density, momentum


def balances(density, u, scale):
    base = 1.0 - 1.5 * (u[0] * u[0] + u[1] * u[1] + u[2] * u[2])
    scaled = {w: density * (w * scale) for w in set(WEIGHTS)}
    yield 0, scaled[WEIGHTS[0]] * base
    for i in range(1, Q, 2):
        along = None
        for j in range(3):
            c = VELOCITIES[i][j]
            if c:
                if along is None:
                    along = u[j] if c > 0 else -u[j]
                else:
                    along = along + u[j] if c > 0 else along - u[j]
        weight = scaled[WEIGHTS[i]]
        even = weight * (base + 4.5 * (along * along))
        odd = weight * (3.0 * along)
        yield i, even + odd
        yield i + 1, even - odd


def rescaled(f, factor, wanted):
    density, momentum = moments(f)
    inverse = 1.0 / density
    u = [m * inverse for m in momentum]
    found = {}
    for i, balance in balances(density, u, 1.0):
        if i in wanted:
            found[i] = balance + factor * (f[i] - balance)
    return 1.0 - jnp.exp(-density), found


def gradient_parts(p, shift_y, shift_z):
    above = shift_y(p, -1, "p")
    below = shift_y(p, 1, "p")
    front = shift_z(p, -1)
    back = shift_z(p, 1)
    n = range(len(p))
    dy = [above[q] - below[q] for q in n]
    sy = [above[q] + below[q] for q in n]
    dz = [front[q] - back[q] for q in n]
    tx = [W_AXIS * p[q] + W_DIAG * (sy[q] + (front[q] + back[q])) for q in n]
    mixed = [W_AXIS * p[q] + W_DIAG * sy[q] for q in n]
    mixed_front = shift_z(mixed, -1)
    mixed_back = shift_z(mixed, 1)
    dy_front = shift_z(dy, -1)
    dy_back = shift_z(dy, 1)
    gy = [W_AXIS * dy[q] + W_DIAG * (dy_front[q] + dy_back[q]) for q in n]
    gz = [mixed_front[q] - mixed_back[q] for q in n]
    return tx, [W_DIAG * v for v in dy], [W_DIAG * v for v in dz], gy, gz


def velocity_of(density, momentum, potential, pull, tau):
    inverse = 1.0 / density
    force = (-tau * COUPLING) * potential
    return [(momentum[j] + force * pull[j]) * inverse for j in range(3)]


def regroup_body(blocks, k_blocks, rows, slot_ref, in_ref, out_ref):
    def step(b, carry):
        s = slot_ref[b]
        source = (b // k_blocks) * (rows * k_blocks) + b % k_blocks
        target = (s // k_blocks) * (rows * k_blocks) + s % k_blocks
        out_ref[pl.ds(target, rows, stride=k_blocks), :] = in_ref[
            pl.ds(source, rows, stride=k_blocks), :
        ]
        return carry

    lax.fori_loop(0, blocks, step, 0, unroll=4)


def lane_ids():
    lane = lax.broadcasted_iota(jnp.int32, (SUB, LANES), 1)
    return lane % B, lane // B


def fine_shifts(ch_count, k_count, ghost):
    y, z = lane_ids()
    first_y, last_y = y == 0, y == B - 1
    first_z, last_z = z == 0, z == LANES // B - 1

    def shift_y(v, c, which):
        out = []
        for ch in range(ch_count):
            for k in range(k_count):
                q = ch * k_count + k
                if c > 0:
                    own = pltpu.roll(v[q], 1, 1)
                    carry = (
                        ghost(0, which, ch) if k == 0 else pltpu.roll(v[q - 1], LANES - (B - 1), 1)
                    )
                    out.append(jnp.where(first_y, carry, own))
                else:
                    own = pltpu.roll(v[q], LANES - 1, 1)
                    carry = (
                        ghost(1, which, ch)
                        if k == k_count - 1
                        else pltpu.roll(v[q + 1], B - 1, 1)
                    )
                    out.append(jnp.where(last_y, carry, own))
        return out

    def shift_z(v, c):
        rolled = [pltpu.roll(x, B if c > 0 else LANES - B, 1) for x in v]
        edge = first_z if c > 0 else last_z
        out = []
        for ch in range(ch_count):
            other = (ch - c) % ch_count
            for k in range(k_count):
                q = ch * k_count + k
                out.append(jnp.where(edge, rolled[other * k_count + k], rolled[q]))
        return out

    return shift_y, shift_z


def fine_step(src, offset, dst, ghosts, parts, ch_count, k_count, chunks):
    nq = ch_count * k_count
    qs = range(nq)
    for chunk in range(chunks):
        r = chunk * SUB
        f = [[src[i, q, pl.ds(offset + r, SUB), :] for i in range(Q)] for q in qs]
        moved = [moments(f[q]) for q in qs]
        p = [1.0 - jnp.exp(-moved[q][0]) for q in qs]

        def ghost(side, which, ch, r=r):
            return ghosts[side, NG - 1, ch, pl.ds(r, SUB), :]

        shift_y, shift_z = fine_shifts(ch_count, k_count, ghost)
        tx, dy, dz, gy, gz = gradient_parts(p, shift_y, shift_z)
        for q in qs:
            values = (tx[q], dy[q], dz[q], gy[q], gz[q], p[q], moved[q][0], *moved[q][1])
            for n, v in enumerate(values):
                parts[n, q, pl.ds(PAD + r, SUB), :] = v
    for chunk in range(chunks):
        r = chunk * SUB

        def ghost(side, which, ch, r=r):
            place = (UP if side == 0 else DOWN).index(which)
            return ghosts[side, place, ch, pl.ds(r, SUB), :]

        shift_y, shift_z = fine_shifts(ch_count, k_count, ghost)
        density, streams = [], []
        for q in qs:
            low = [parts[n, q, pl.ds(PAD + r - 1, SUB), :] for n in range(3)]
            high = [parts[n, q, pl.ds(PAD + r + 1, SUB), :] for n in range(3)]
            gy, gz, p, rho, mx, my, mz = (
                parts[n, q, pl.ds(PAD + r, SUB), :] for n in range(3, 10)
            )
            pull = [high[0] - low[0], gy + (high[1] + low[1]), gz + (high[2] + low[2])]
            u = velocity_of(rho, (mx, my, mz), p, pull, FINE_TAU)
            streams.append(balances(rho, u, 1.0 / FINE_TAU))
        for i in range(Q):
            cx, cy, cz = VELOCITIES[i]
            post = []
            for q in qs:
                _, balance = next(streams[q])
                h = src[i, q, pl.ds(offset + r, SUB), :]
                post.append(h * (1.0 - 1.0 / FINE_TAU) + balance)
            if cy:
                post = shift_y(post, cy, i)
            if cz:
                post = shift_z(post, cz)
            for q in qs:
                dst[i, q, pl.ds(PAD + r + cx, SUB), :] = post[q]


def fine_body(ch_count, k_count, own, left, right, ghosts, out, first, second, third, parts):
    nq = ch_count * k_count

    def gather(i, carry):
        for q in range(nq):
            first[i, q, pl.ds(0, HALO), :] = left[pl.ds(i * (HALO * nq) + q, HALO, stride=nq), :]
            first[i, q, pl.ds(HALO, B), :] = own[pl.ds(i * (B * nq) + q, B, stride=nq), :]
            first[i, q, pl.ds(HALO + B, HALO), :] = right[
                pl.ds(i * (HALO * nq) + q, HALO, stride=nq), :
            ]
        return carry

    lax.fori_loop(0, Q, gather, 0)
    chunks = (B + 2 * HALO) // SUB
    fine_step(first, 0, second, ghosts, parts, ch_count, k_count, chunks)
    fine_step(second, PAD, third, ghosts, parts, ch_count, k_count, chunks)

    def scatter(i, carry):
        for q in range(nq):
            out[pl.ds(i * (B * nq) + q, B, stride=nq), :] = third[i, q, pl.ds(PAD + HALO, B), :]
        return carry

    lax.fori_loop(0, Q, scatter, 0)


def fine_ghost_body(ch_count, rows, layers, spread, out, wide):
    for side in range(2):
        wide[...] = jnp.dot(
            layers[side],
            spread[...],
            precision=lax.Precision.HIGHEST,
            preferred_element_type=jnp.float32,
        )
        wanted = UP if side == 0 else DOWN
        for ch in range(ch_count):
            for r in range(0, rows, SUB):
                f = [
                    wide[pl.ds(i * rows + r, SUB), pl.ds(ch * LANES, LANES)] for i in range(Q)
                ]
                potential, found = rescaled(f, TO_FINE, wanted)
                for n, i in enumerate(wanted):
                    out[side, n, ch, pl.ds(r, SUB), :] = found[i]
                out[side, NG - 1, ch, pl.ds(r, SUB), :] = potential


STRIDE = 32
PER = LANES // STRIDE


def restrict_body(ch_count, k_count, own, left, right, out_low, out_high, buffer):
    nq = ch_count * k_count
    row = lax.broadcasted_iota(jnp.int32, (LANES, LANES), 0)
    col = lax.broadcasted_iota(jnp.int32, (LANES, LANES), 1)
    for side in range(2):
        k = k_count - 1 if side == 0 else 0
        y = row % B
        picked = (y >= B - 2) if side == 0 else (y < 2)
        total = None
        for ch in range(ch_count):
            q = ch * k_count + k

            def gather(i, carry, ch=ch, q=q):
                at = i * STRIDE
                buffer[ch, pl.ds(at, HALO), :] = left[
                    pl.ds(i * (HALO * nq) + q, HALO, stride=nq), :
                ]
                buffer[ch, pl.ds(at + HALO, B), :] = own[pl.ds(i * (B * nq) + q, B, stride=nq), :]
                buffer[ch, pl.ds(at + HALO + B, HALO), :] = right[
                    pl.ds(i * (HALO * nq) + q, HALO, stride=nq), :
                ]
                buffer[ch, pl.ds(at + 2 * HALO + B, STRIDE - 2 * HALO - B), :] = jnp.zeros(
                    (STRIDE - 2 * HALO - B, LANES), jnp.float32
                )
                return carry

            lax.fori_loop(0, Q, gather, 0)
            coarse_z = ch * (LANES // B // 2) + row // (2 * B)
            select = jnp.where(picked & (coarse_z == col), 0.125, 0.0).astype(jnp.float32)
            part = jnp.dot(
                buffer[ch, pl.ds(0, Q * STRIDE), :],
                select,
                precision=lax.Precision.HIGHEST,
                preferred_element_type=jnp.float32,
            )
            total = part if total is None else total + part
        for n in range(pl.cdiv(Q, PER)):
            count = min(PER, Q - n * PER) * STRIDE
            block = total[n * LANES : n * LANES + count]
            if count < LANES:
                block = jnp.concatenate(
                    [block, jnp.zeros((LANES - count, LANES), jnp.float32)], axis=0
                )
            (out_low, out_high)[side][n] = block.T[:SUB]


def coarse_body(planes, state, low, high, out, ghosts, parts, out_pad):
    lane = lax.broadcasted_iota(jnp.int32, (SUB, LANES), 1)
    first_y, last_y = lane == 0, lane == LANES - 1

    for side, ref in enumerate((low, high)):
        paired = []
        for n in range(pl.cdiv(Q, PER)):
            v = ref[n]
            paired.append(v + pltpu.roll(v, LANES - 1, 1))
        f = []
        for i in range(Q):
            s = (i % PER) * STRIDE
            f.append(paired[i // PER] if s == 0 else pltpu.roll(paired[i // PER], LANES - s, 1))
        wanted = UP if side == 0 else DOWN
        potential, found = rescaled(f, TO_COARSE, wanted)
        for n, v in enumerate([found[i] for i in wanted] + [potential]):
            for x in range(planes):
                ghosts[side, n, x] = jnp.broadcast_to(v[:, 2 * x : 2 * x + 1], (SUB, LANES))

    def shifts(x):
        def shift_y(v, c, which):
            side = 0 if c > 0 else 1
            place = NG - 1 if which == "p" else (UP if c > 0 else DOWN).index(which)
            carry = ghosts[side, place, x]
            own = pltpu.roll(v[0], 1 if c > 0 else LANES - 1, 1)
            return [jnp.where(first_y if c > 0 else last_y, carry, own)]

        def shift_z(v, c):
            return [pltpu.roll(v[0], 1 if c > 0 else SUB - 1, 0)]

        return shift_y, shift_z

    def prepare(x, carry):
        density, momentum = moments([state[i, x] for i in range(Q)])
        p = 1.0 - jnp.exp(-density)
        values = gradient_parts([p], *shifts(x))
        values = [v[0] for v in values] + [p, density, *momentum]
        for n, v in enumerate(values):
            parts[n, x] = v
        return carry

    lax.fori_loop(0, planes, prepare, 0, unroll=2)

    inner = planes - 2 * (HALO // 2)
    base = HALO // 2

    def update(x, carry):
        shift_y, shift_z = shifts(x)
        lower = [parts[n, x - 1] for n in range(3)]
        upper = [parts[n, x + 1] for n in range(3)]
        gy, gz, p, rho, mx, my, mz = (parts[n, x] for n in range(3, 10))
        pull = [upper[0] - lower[0], gy + (upper[1] + lower[1]), gz + (upper[2] + lower[2])]
        u = velocity_of(rho, (mx, my, mz), p, pull, COARSE_TAU)
        for i, balance in balances(rho, u, 1.0 / COARSE_TAU):
            cx, cy, cz = VELOCITIES[i]
            post = [state[i, x] * (1.0 - 1.0 / COARSE_TAU) + balance]
            if cy:
                post = shift_y(post, cy, i)
            if cz:
                post = shift_z(post, cz)
            inside = x + cx - base
            spare = jnp.where((inside >= 0) & (inside < inner), inside, inner)
            out_pad[i, spare] = post[0]
        return carry

    lax.fori_loop(base - 1, base + inner + 1, update, 0, unroll=2)
    out[...] = out_pad[:, :inner]


def ring(axis, count, step):
    return [(i, (i + step) % count) for i in range(count)]


def local(fine_pop, coarse_pop, new_slot):
    k_count, q_count, cells = fine_pop.shape
    blocks = new_slot.shape[0]
    devices = blocks // k_count
    tiles = cells // LANES
    ch_count = tiles // B
    nq = ch_count * k_count
    axes = ("grp", "wide")
    n_grp, n_wide = lax.axis_size("grp"), lax.axis_size("wide")
    _, cx, cz, cy = coarse_pop.shape
    planes = cx + HALO
    fine_rows = B + 2 * HALO

    rows = pl.cdiv(Q * tiles, devices)
    pieces = fine_pop.reshape(k_count, Q, tiles, LANES)
    pieces = with_layout_constraint(pieces, Layout(major_to_minor=(1, 2, 0, 3)))
    pieces = pieces.transpose(1, 2, 0, 3)
    pieces = pieces.reshape(Q * tiles, k_count, LANES)
    if rows * devices != Q * tiles:
        pieces = jnp.pad(pieces, ((0, rows * devices - Q * tiles), (0, 0), (0, 0)))
    pieces = pieces.reshape(devices, rows, k_count, LANES)
    spread = lax.all_to_all(pieces, axes, 0, 0, tiled=True)
    edge = HALO // 2
    coarse_left = lax.ppermute(coarse_pop[:, cx - edge :], "grp", ring("grp", n_grp, 1))
    coarse_right = lax.ppermute(coarse_pop[:, :edge], "grp", ring("grp", n_grp, -1))
    coarse = jnp.concatenate([coarse_left, coarse_pop, coarse_right], axis=1)
    below = lax.ppermute(coarse[..., -1], "wide", ring("wide", n_wide, 1))
    spread, coarse, below = lax.optimization_barrier((spread, coarse, below))
    total = devices * rows * k_count
    regroup = call(
        functools.partial(regroup_body, blocks, k_count, rows),
        f32(total, LANES),
        [SMEM, VMEM],
        moved=8 * total * LANES,
    )
    outgoing = regroup(new_slot, spread.reshape(total, LANES))
    arrived = lax.all_to_all(
        outgoing.reshape(devices, rows, k_count, LANES), axes, 0, 0, tiled=True
    )
    layers = jnp.repeat(jnp.stack([below, coarse[..., 0]]), 2, axis=2)
    layers = layers.reshape(2, Q * fine_rows, cz)
    lane = jnp.arange(ch_count * LANES) // (2 * B)
    one_hot = (jnp.arange(cz)[:, None] == lane[None, :]).astype(jnp.float32)
    fine_ghosts = call(
        functools.partial(fine_ghost_body, ch_count, fine_rows),
        f32(2, NG, ch_count, fine_rows, LANES),
        [VMEM, VMEM],
        [pltpu.VMEM((Q * fine_rows, ch_count * LANES), jnp.float32)],
    )(layers, one_hot)
    arrived, fine_ghosts = lax.optimization_barrier((arrived, fine_ghosts))
    own = arrived.reshape(total, LANES)[: Q * tiles * k_count]

    by_x = own.reshape(Q, B * nq, LANES)
    width = HALO * nq
    left = lax.ppermute(by_x[:, -width:], "grp", ring("grp", n_grp, 1)).reshape(Q * width, LANES)
    right = lax.ppermute(by_x[:, :width], "grp", ring("grp", n_grp, -1)).reshape(Q * width, LANES)

    groups = pl.cdiv(Q, PER)
    restricted = call(
        functools.partial(restrict_body, ch_count, k_count),
        [f32(groups, SUB, LANES)] * 2,
        [VMEM, VMEM, VMEM],
        [pltpu.VMEM((ch_count, Q * STRIDE, LANES), jnp.float32)],
    )(own, left, right)
    high = lax.ppermute(restricted[1], "wide", ring("wide", n_wide, -1))

    padded = PAD + fine_rows + PAD
    fine = call(
        functools.partial(fine_body, ch_count, k_count),
        f32(Q * B * nq, LANES),
        [VMEM] * 4,
        [
            pltpu.VMEM((Q, nq, fine_rows, LANES), jnp.float32),
            pltpu.VMEM((Q, nq, padded, LANES), jnp.float32),
            pltpu.VMEM((Q, nq, padded, LANES), jnp.float32),
            pltpu.VMEM((10, nq, padded, LANES), jnp.float32),
        ],
        flops=10**7,
    )(own, left, right, fine_ghosts)

    coarse_out = call(
        functools.partial(coarse_body, planes),
        f32(Q, cx, cz, cy),
        [VMEM] * 3,
        [
            pltpu.VMEM((2, NG, planes, SUB, LANES), jnp.float32),
            pltpu.VMEM((10, planes, SUB, LANES), jnp.float32),
            pltpu.VMEM((Q, cx + 1, SUB, LANES), jnp.float32),
        ],
        flops=10**7,
    )(coarse, restricted[0], high)

    fine_out = fine.reshape(Q, tiles, k_count, LANES).transpose(2, 0, 1, 3)
    fine_out = fine_out.reshape(k_count, q_count, cells)
    return fine_out, coarse_out


def solution(mesh):
    return jax.shard_map(
        local,
        mesh=mesh,
        in_specs=(P(("grp", "wide"), None, None), P(None, "grp", None, "wide"), P()),
        out_specs=(P(("grp", "wide"), None, None), P(None, "grp", None, "wide")),
        check_vma=False,
    )
```

```python
import functools

import jax
import jax.numpy as jnp
from jax import lax
from jax.experimental import pallas as pl
from jax.experimental.layout import Layout, with_layout_constraint
from jax.experimental.pallas import tpu as pltpu
from jax.sharding import PartitionSpec as P

B = 16
LANES = 128
SUB = 8
HALO = 4
PAD = 8
GRANT = 24 << 20

VELOCITIES = (
    (0, 0, 0),
    (1, 0, 0),
    (-1, 0, 0),
    (0, 1, 0),
    (0, -1, 0),
    (0, 0, 1),
    (0, 0, -1),
    (1, 1, 0),
    (-1, -1, 0),
    (1, -1, 0),
    (-1, 1, 0),
    (1, 0, 1),
    (-1, 0, -1),
    (1, 0, -1),
    (-1, 0, 1),
    (0, 1, 1),
    (0, -1, -1),
    (0, 1, -1),
    (0, -1, 1),
)
Q = len(VELOCITIES)
WEIGHTS = (1.0 / 3.0,) + (1.0 / 18.0,) * 6 + (1.0 / 36.0,) * 12
W_AXIS = WEIGHTS[1]
W_DIAG = WEIGHTS[7]
COUPLING = -5.0
FINE_TAU = 1.1
COARSE_TAU = 0.8
TO_COARSE = 2.0 * COARSE_TAU / FINE_TAU
TO_FINE = FINE_TAU / (2.0 * COARSE_TAU)
UP = tuple(i for i in range(Q) if VELOCITIES[i][1] == 1)
DOWN = tuple(i for i in range(Q) if VELOCITIES[i][1] == -1)
NG = len(UP) + 1

VMEM = pl.BlockSpec(memory_space=pltpu.VMEM)
SMEM = pl.BlockSpec(memory_space=pltpu.SMEM)


def call(body, outs, specs, scratch=(), flops=10**6, moved=10**6):
    return pl.pallas_call(
        body,
        out_shape=outs,
        in_specs=specs,
        out_specs=jax.tree.map(lambda _: VMEM, outs),
        scratch_shapes=list(scratch),
        cost_estimate=pl.CostEstimate(flops=flops, bytes_accessed=moved, transcendentals=0),
        compiler_params=pltpu.CompilerParams(vmem_limit_bytes=GRANT),
    )


def f32(*shape):
    return jax.ShapeDtypeStruct(shape, jnp.float32)


def moments(f):
    density = f[0]
    momentum = [None, None, None]
    for i in range(1, Q, 2):
        density = density + (f[i] + f[i + 1])
        odd = f[i] - f[i + 1]
        for j in range(3):
            c = VELOCITIES[i][j]
            if c:
                term = odd if c > 0 else -odd
                if momentum[j] is None:
                    momentum[j] = term
                else:
                    momentum[j] = momentum[j] + odd if c > 0 else momentum[j] - odd
    return density, momentum


def balances(density, u, scale):
    base = 1.0 - 1.5 * (u[0] * u[0] + u[1] * u[1] + u[2] * u[2])
    scaled = {w: density * (w * scale) for w in set(WEIGHTS)}
    yield 0, scaled[WEIGHTS[0]] * base
    for i in range(1, Q, 2):
        along = None
        for j in range(3):
            c = VELOCITIES[i][j]
            if c:
                if along is None:
                    along = u[j] if c > 0 else -u[j]
                else:
                    along = along + u[j] if c > 0 else along - u[j]
        weight = scaled[WEIGHTS[i]]
        even = weight * (base + 4.5 * (along * along))
        odd = weight * (3.0 * along)
        yield i, even + odd
        yield i + 1, even - odd


def rescaled(f, factor, wanted):
    density, momentum = moments(f)
    inverse = 1.0 / density
    u = [m * inverse for m in momentum]
    found = {}
    for i, balance in balances(density, u, 1.0):
        if i in wanted:
            found[i] = balance + factor * (f[i] - balance)
    return 1.0 - jnp.exp(-density), found


def gradient_parts(p, shift_y, shift_z):
    above = shift_y(p, -1, "p")
    below = shift_y(p, 1, "p")
    front = shift_z(p, -1)
    back = shift_z(p, 1)
    n = range(len(p))
    dy = [above[q] - below[q] for q in n]
    sy = [above[q] + below[q] for q in n]
    dz = [front[q] - back[q] for q in n]
    tx = [W_AXIS * p[q] + W_DIAG * (sy[q] + (front[q] + back[q])) for q in n]
    mixed = [W_AXIS * p[q] + W_DIAG * sy[q] for q in n]
    mixed_front = shift_z(mixed, -1)
    mixed_back = shift_z(mixed, 1)
    dy_front = shift_z(dy, -1)
    dy_back = shift_z(dy, 1)
    gy = [W_AXIS * dy[q] + W_DIAG * (dy_front[q] + dy_back[q]) for q in n]
    gz = [mixed_front[q] - mixed_back[q] for q in n]
    return tx, [W_DIAG * v for v in dy], [W_DIAG * v for v in dz], gy, gz


def velocity_of(density, momentum, potential, pull, tau):
    inverse = 1.0 / density
    force = (-tau * COUPLING) * potential
    return [(momentum[j] + force * pull[j]) * inverse for j in range(3)]


def regroup_body(blocks, k_blocks, rows, slot_ref, in_ref, out_ref):
    def step(b, carry):
        s = slot_ref[b]
        source = (b // k_blocks) * (rows * k_blocks) + b % k_blocks
        target = (s // k_blocks) * (rows * k_blocks) + s % k_blocks
        out_ref[pl.ds(target, rows, stride=k_blocks), :] = in_ref[
            pl.ds(source, rows, stride=k_blocks), :
        ]
        return carry

    lax.fori_loop(0, blocks, step, 0, unroll=4)


def lane_ids():
    lane = lax.broadcasted_iota(jnp.int32, (SUB, LANES), 1)
    return lane % B, lane // B


def fine_shifts(ch_count, k_count, ghost):
    y, z = lane_ids()
    first_y, last_y = y == 0, y == B - 1
    first_z, last_z = z == 0, z == LANES // B - 1

    def shift_y(v, c, which):
        out = []
        for ch in range(ch_count):
            for k in range(k_count):
                q = ch * k_count + k
                if c > 0:
                    own = pltpu.roll(v[q], 1, 1)
                    carry = (
                        ghost(0, which, ch) if k == 0 else pltpu.roll(v[q - 1], LANES - (B - 1), 1)
                    )
                    out.append(jnp.where(first_y, carry, own))
                else:
                    own = pltpu.roll(v[q], LANES - 1, 1)
                    carry = (
                        ghost(1, which, ch)
                        if k == k_count - 1
                        else pltpu.roll(v[q + 1], B - 1, 1)
                    )
                    out.append(jnp.where(last_y, carry, own))
        return out

    def shift_z(v, c):
        rolled = [pltpu.roll(x, B if c > 0 else LANES - B, 1) for x in v]
        edge = first_z if c > 0 else last_z
        out = []
        for ch in range(ch_count):
            other = (ch - c) % ch_count
            for k in range(k_count):
                q = ch * k_count + k
                out.append(jnp.where(edge, rolled[other * k_count + k], rolled[q]))
        return out

    return shift_y, shift_z


def fine_step(src, offset, dst, ghosts, parts, ch_count, k_count, chunks):
    nq = ch_count * k_count
    qs = range(nq)
    for chunk in range(chunks):
        r = chunk * SUB
        f = [[src[i, q, pl.ds(offset + r, SUB), :] for i in range(Q)] for q in qs]
        moved = [moments(f[q]) for q in qs]
        p = [1.0 - jnp.exp(-moved[q][0]) for q in qs]

        def ghost(side, which, ch, r=r):
            return ghosts[side, NG - 1, ch, pl.ds(r, SUB), :]

        shift_y, shift_z = fine_shifts(ch_count, k_count, ghost)
        tx, dy, dz, gy, gz = gradient_parts(p, shift_y, shift_z)
        for q in qs:
            values = (tx[q], dy[q], dz[q], gy[q], gz[q], p[q], moved[q][0], *moved[q][1])
            for n, v in enumerate(values):
                parts[n, q, pl.ds(PAD + r, SUB), :] = v
    for chunk in range(chunks):
        r = chunk * SUB

        def ghost(side, which, ch, r=r):
            place = (UP if side == 0 else DOWN).index(which)
            return ghosts[side, place, ch, pl.ds(r, SUB), :]

        shift_y, shift_z = fine_shifts(ch_count, k_count, ghost)
        density, streams = [], []
        for q in qs:
            low = [parts[n, q, pl.ds(PAD + r - 1, SUB), :] for n in range(3)]
            high = [parts[n, q, pl.ds(PAD + r + 1, SUB), :] for n in range(3)]
            gy, gz, p, rho, mx, my, mz = (
                parts[n, q, pl.ds(PAD + r, SUB), :] for n in range(3, 10)
            )
            pull = [high[0] - low[0], gy + (high[1] + low[1]), gz + (high[2] + low[2])]
            u = velocity_of(rho, (mx, my, mz), p, pull, FINE_TAU)
            streams.append(balances(rho, u, 1.0 / FINE_TAU))
        for i in range(Q):
            cx, cy, cz = VELOCITIES[i]
            post = []
            for q in qs:
                _, balance = next(streams[q])
                h = src[i, q, pl.ds(offset + r, SUB), :]
                post.append(h * (1.0 - 1.0 / FINE_TAU) + balance)
            if cy:
                post = shift_y(post, cy, i)
            if cz:
                post = shift_z(post, cz)
            for q in qs:
                dst[i, q, pl.ds(PAD + r + cx, SUB), :] = post[q]


def fine_body(ch_count, k_count, own, left, right, ghosts, out, first, second, third, parts):
    nq = ch_count * k_count

    def gather(i, carry):
        for q in range(nq):
            first[i, q, pl.ds(0, HALO), :] = left[pl.ds(i * (HALO * nq) + q, HALO, stride=nq), :]
            first[i, q, pl.ds(HALO, B), :] = own[pl.ds(i * (B * nq) + q, B, stride=nq), :]
            first[i, q, pl.ds(HALO + B, HALO), :] = right[
                pl.ds(i * (HALO * nq) + q, HALO, stride=nq), :
            ]
        return carry

    lax.fori_loop(0, Q, gather, 0)
    chunks = (B + 2 * HALO) // SUB
    fine_step(first, 0, second, ghosts, parts, ch_count, k_count, chunks)
    fine_step(second, PAD, third, ghosts, parts, ch_count, k_count, chunks)

    def scatter(i, carry):
        for q in range(nq):
            out[pl.ds(i * (B * nq) + q, B, stride=nq), :] = third[i, q, pl.ds(PAD + HALO, B), :]
        return carry

    lax.fori_loop(0, Q, scatter, 0)


def fine_ghost_body(ch_count, rows, layers, spread, out, wide):
    for side in range(2):
        wide[...] = jnp.dot(
            layers[side],
            spread[...],
            precision=lax.Precision.HIGHEST,
            preferred_element_type=jnp.float32,
        )
        wanted = UP if side == 0 else DOWN
        for ch in range(ch_count):
            for r in range(0, rows, SUB):
                f = [
                    wide[pl.ds(i * rows + r, SUB), pl.ds(ch * LANES, LANES)] for i in range(Q)
                ]
                potential, found = rescaled(f, TO_FINE, wanted)
                for n, i in enumerate(wanted):
                    out[side, n, ch, pl.ds(r, SUB), :] = found[i]
                out[side, NG - 1, ch, pl.ds(r, SUB), :] = potential


GROUP = 16
STEP = 32
PLANES = -(-Q // GROUP)


def pack(load, ch_count, k_count, side):
    lane = lax.broadcasted_iota(jnp.int32, (SUB, LANES), 1)
    offset = B - 2 if side == 0 else 0
    kept = lane % STEP == offset
    k = k_count - 1 if side == 0 else 0
    planes = [None] * PLANES
    for i in range(Q):
        for ch in range(ch_count):
            q = ch * k_count + k
            v = load(i, q, 0) + load(i, q, 1)
            v = v + pltpu.roll(v, LANES - 1, 1)
            v = v + pltpu.roll(v, LANES - B, 1)
            v = jnp.where(kept, v, 0.0)
            shift = (2 * (i % GROUP) + ch - offset) % LANES
            if shift:
                v = pltpu.roll(v, shift, 1)
            n = i // GROUP
            planes[n] = v if planes[n] is None else planes[n] + v
    return planes


def restrict_body(ch_count, k_count, own, low, high):
    nq = ch_count * k_count

    def load(i, q, half):
        return own[pl.ds(i * (B * nq) + half * nq + q, SUB, stride=2 * nq), :]

    for side, out in enumerate((low, high)):
        for n, plane in enumerate(pack(load, ch_count, k_count, side)):
            out[n] = plane


def coarse_body(planes, state, out, packed, near, parts, out_pad):
    lane = lax.broadcasted_iota(jnp.int32, (SUB, LANES), 1)

    def shift_y(v, c, which):
        return [pltpu.roll(v[0], 1 if c > 0 else LANES - 1, 1)]

    def shift_z(v, c):
        return [pltpu.roll(v[0], 1 if c > 0 else SUB - 1, 0)]

    def prepare(x, carry):
        density, momentum = moments([state[i, x] for i in range(Q)])
        p = 1.0 - jnp.exp(-density)
        values = gradient_parts([p], shift_y, shift_z)
        values = [v[0] for v in values] + [p, density, *momentum]
        for n, v in enumerate(values):
            parts[n, x] = v
        return carry

    lax.fori_loop(0, planes, prepare, 0, unroll=2)

    inner = planes - HALO
    base = HALO // 2

    def update(x, carry):
        lower = [parts[n, x - 1] for n in range(3)]
        upper = [parts[n, x + 1] for n in range(3)]
        gy, gz, p, rho, mx, my, mz = (parts[n, x] for n in range(3, 10))
        pull = [upper[0] - lower[0], gy + (upper[1] + lower[1]), gz + (upper[2] + lower[2])]
        u = velocity_of(rho, (mx, my, mz), p, pull, COARSE_TAU)
        for i, balance in balances(rho, u, 1.0 / COARSE_TAU):
            cx, cy, cz = VELOCITIES[i]
            post = [state[i, x] * (1.0 - 1.0 / COARSE_TAU) + balance]
            if cy:
                post = shift_y(post, cy, i)
            if cz:
                post = shift_z(post, cz)
            inside = x + cx - base
            spare = jnp.where((inside >= 0) & (inside < inner), inside, inner)
            out_pad[i, spare] = post[0]
        return carry

    lax.fori_loop(base - 1, base + inner + 1, update, 0, unroll=2)
    out[...] = out_pad[:, :inner]

    def gather(i, carry):
        total = jnp.zeros((SUB, LANES), jnp.float32)
        for x in range(planes):
            here = (lane == 2 * x + 1) | (lane == 2 * x + 2)
            total = jnp.where(here, pltpu.roll(state[i, x], 2 * x + 2, 1), total)
        packed[i] = total
        return carry

    lax.fori_loop(0, Q, gather, 0)
    total = jnp.zeros((SUB, LANES), jnp.float32)
    for x in range(planes):
        p = parts[5, x]
        total = jnp.where(lane == 2 * x + 2, pltpu.roll(p, 2 * x + 1, 1), total)
        total = jnp.where(lane == 2 * x + 1, pltpu.roll(p, 2 * x + 3, 1), total)
    near[...] = total


def edges_body(
    ch_count, k_count, planes, left, right, low, high, high_left, high_right, packed, near, step,
    out, halo, rows, columns, ghost,
):
    nq = ch_count * k_count
    edge = HALO // 2
    inner = planes - HALO
    lane = lax.broadcasted_iota(jnp.int32, (SUB, LANES), 1)
    sided = lane % 2 == 0

    halo[...] = jnp.zeros_like(halo)

    def load(i, q, half):
        for at, ref in ((0, left), (edge, right)):
            start = i * (HALO * nq) + half * nq + q
            halo[i % 2, q, half, pl.ds(at, edge), :] = ref[pl.ds(start, edge, stride=2 * nq), :]
        return halo[i % 2, q, half]

    beside = pack(load, ch_count, k_count, 0)
    for n in range(PLANES):
        own_x = 2 * edge
        rows[n, pl.ds(2 + own_x, inner, stride=2), :] = low[n]
        rows[n, pl.ds(2, edge, stride=2), :] = beside[n][:edge]
        rows[n, pl.ds(2 + 2 * (edge + inner), edge, stride=2), :] = beside[n][edge : 2 * edge]
        rows[n, pl.ds(1 + own_x, inner, stride=2), :] = high[n]
        rows[n, pl.ds(1, edge, stride=2), :] = high_left[n, pl.ds(inner - edge, edge), :]
        rows[n, pl.ds(1 + 2 * (edge + inner), edge, stride=2), :] = high_right[
            n, pl.ds(0, edge), :
        ]
        columns[n] = rows[n].T
    per = LANES // STEP
    for i in range(Q):
        for ch in range(ch_count):
            ghost[i, pl.ds(ch * per, per), :] = (
                0.125 * columns[i // GROUP, pl.ds(2 * (i % GROUP) + ch, per, stride=STEP), :]
            )

    beyond, entering = rescaled([ghost[i] for i in range(Q)], TO_COARSE, UP + DOWN)
    density, momentum = moments([packed[i] for i in range(Q)])
    p = 1.0 - jnp.exp(-density)
    inside = near[...]
    above = jnp.where(sided, inside, beyond)
    below = jnp.where(sided, beyond, inside)

    def shift_y(v, c, which):
        return [below if c > 0 else above]

    def shift_z(v, c):
        return [pltpu.roll(v[0], 1 if c > 0 else SUB - 1, 0)]

    def shift_x(v, c):
        return pltpu.roll(v, 2 if c > 0 else LANES - 2, 1) if c else v

    tx, dy, dz, gy, gz = (v[0] for v in gradient_parts([p], shift_y, shift_z))
    pull = [
        shift_x(tx, -1) - shift_x(tx, 1),
        gy + (shift_x(dy, -1) + shift_x(dy, 1)),
        gz + (shift_x(dz, -1) + shift_x(dz, 1)),
    ]
    u = velocity_of(density, momentum, p, pull, COARSE_TAU)
    for i, balance in balances(density, u, 1.0 / COARSE_TAU):
        cx, cy, cz = VELOCITIES[i]
        v = packed[i] * (1.0 - 1.0 / COARSE_TAU) + balance
        if cy > 0:
            v = jnp.where(sided, entering[i], pltpu.roll(v, 1, 1))
            touched = lane < 2
        elif cy < 0:
            v = jnp.where(sided, pltpu.roll(v, LANES - 1, 1), entering[i])
            touched = lane >= LANES - 2
        else:
            touched = (lane == 0) | (lane == LANES - 1)
        v = shift_x(v, cx)
        if cz:
            v = shift_z([v], cz)[0]
        for x in range(inner):
            column = pltpu.roll(v, LANES - (2 * (x + edge) + 2), 1)
            out[i, x] = jnp.where(touched, column, step[i, x])


def ring(axis, count, step):
    return [(i, (i + step) % count) for i in range(count)]


def local(fine_pop, coarse_pop, new_slot):
    k_count, q_count, cells = fine_pop.shape
    blocks = new_slot.shape[0]
    devices = blocks // k_count
    tiles = cells // LANES
    ch_count = tiles // B
    nq = ch_count * k_count
    axes = ("grp", "wide")
    n_grp, n_wide = lax.axis_size("grp"), lax.axis_size("wide")
    _, cx, cz, cy = coarse_pop.shape
    planes = cx + HALO
    fine_rows = B + 2 * HALO

    rows = pl.cdiv(Q * tiles, devices)
    pieces = fine_pop.reshape(k_count, Q, tiles, LANES)
    pieces = with_layout_constraint(pieces, Layout(major_to_minor=(1, 2, 0, 3)))
    pieces = pieces.transpose(1, 2, 0, 3)
    pieces = pieces.reshape(Q * tiles, k_count, LANES)
    if rows * devices != Q * tiles:
        pieces = jnp.pad(pieces, ((0, rows * devices - Q * tiles), (0, 0), (0, 0)))
    pieces = pieces.reshape(devices, rows, k_count, LANES)
    spread = lax.all_to_all(pieces, axes, 0, 0, tiled=True)
    edge = HALO // 2
    coarse_left = lax.ppermute(coarse_pop[:, cx - edge :], "grp", ring("grp", n_grp, 1))
    coarse_right = lax.ppermute(coarse_pop[:, :edge], "grp", ring("grp", n_grp, -1))
    coarse = jnp.concatenate([coarse_left, coarse_pop, coarse_right], axis=1)
    spread, coarse = lax.optimization_barrier((spread, coarse))
    total = devices * rows * k_count
    regroup = call(
        functools.partial(regroup_body, blocks, k_count, rows),
        f32(total, LANES),
        [SMEM, VMEM],
        moved=8 * total * LANES,
    )
    outgoing = regroup(new_slot, spread.reshape(total, LANES))
    arrived = lax.all_to_all(
        outgoing.reshape(devices, rows, k_count, LANES), axes, 0, 0, tiled=True
    )
    below = lax.ppermute(coarse[..., -1], "wide", ring("wide", n_wide, 1))
    layers = jnp.repeat(jnp.stack([below, coarse[..., 0]]), 2, axis=2)
    layers = layers.reshape(2, Q * fine_rows, cz)
    lane = jnp.arange(ch_count * LANES) // (2 * B)
    one_hot = (jnp.arange(cz)[:, None] == lane[None, :]).astype(jnp.float32)
    fine_ghosts = call(
        functools.partial(fine_ghost_body, ch_count, fine_rows),
        f32(2, NG, ch_count, fine_rows, LANES),
        [VMEM, VMEM],
        [pltpu.VMEM((Q * fine_rows, ch_count * LANES), jnp.float32)],
    )(layers, one_hot)
    coarse_step, packed, near = call(
        functools.partial(coarse_body, planes),
        [f32(Q, cx, cz, cy), f32(Q, SUB, LANES), f32(SUB, LANES)],
        [VMEM],
        [
            pltpu.VMEM((10, planes, SUB, LANES), jnp.float32),
            pltpu.VMEM((Q, cx + 1, SUB, LANES), jnp.float32),
        ],
        flops=10**7,
    )(coarse)
    arrived, fine_ghosts, coarse_step, packed, near = lax.optimization_barrier(
        (arrived, fine_ghosts, coarse_step, packed, near)
    )
    own = arrived.reshape(total, LANES)[: Q * tiles * k_count]

    by_x = own.reshape(Q, B * nq, LANES)
    width = HALO * nq
    left = lax.ppermute(by_x[:, -width:], "grp", ring("grp", n_grp, 1)).reshape(Q * width, LANES)
    right = lax.ppermute(by_x[:, :width], "grp", ring("grp", n_grp, -1)).reshape(Q * width, LANES)

    low, first = call(
        functools.partial(restrict_body, ch_count, k_count),
        [f32(PLANES, SUB, LANES)] * 2,
        [VMEM],
    )(own)
    highs = []
    for across in (0, 1, -1):
        pairs = [
            (g * n_wide + (w + 1) % n_wide, (g + across) % n_grp * n_wide + w)
            for g in range(n_grp)
            for w in range(n_wide)
        ]
        highs.append(lax.ppermute(first, axes, pairs))

    padded = PAD + fine_rows + PAD
    fine = call(
        functools.partial(fine_body, ch_count, k_count),
        f32(Q * B * nq, LANES),
        [VMEM] * 4,
        [
            pltpu.VMEM((Q, nq, fine_rows, LANES), jnp.float32),
            pltpu.VMEM((Q, nq, padded, LANES), jnp.float32),
            pltpu.VMEM((Q, nq, padded, LANES), jnp.float32),
            pltpu.VMEM((10, nq, padded, LANES), jnp.float32),
        ],
        flops=10**7,
    )(own, left, right, fine_ghosts)

    coarse_out = call(
        functools.partial(edges_body, ch_count, k_count, planes),
        f32(Q, cx, cz, cy),
        [VMEM] * 9,
        [
            pltpu.VMEM((2, nq, 2, SUB, LANES), jnp.float32),
            pltpu.VMEM((PLANES, LANES, LANES), jnp.float32),
            pltpu.VMEM((PLANES, LANES, LANES), jnp.float32),
            pltpu.VMEM((Q, SUB, LANES), jnp.float32),
        ],
    )(left, right, low, *highs, packed, near, coarse_step)

    fine_out = fine.reshape(Q, tiles, k_count, LANES).transpose(2, 0, 1, 3)
    fine_out = fine_out.reshape(k_count, q_count, cells)
    return fine_out, coarse_out


def solution(mesh):
    return jax.shard_map(
        local,
        mesh=mesh,
        in_specs=(P(("grp", "wide"), None, None), P(None, "grp", None, "wide"), P()),
        out_specs=(P(("grp", "wide"), None, None), P(None, "grp", None, "wide")),
        check_vma=False,
    )
```

```python
import functools

import jax
import jax.numpy as jnp
from jax import lax
from jax.experimental import pallas as pl
from jax.experimental.layout import Layout, with_layout_constraint
from jax.experimental.pallas import tpu as pltpu
from jax.sharding import PartitionSpec as P


B = 16
LANES = 128
SUB = 8
HALO = 4
PAD = 8
GRANT = 24 << 20

VELOCITIES = (
    (0, 0, 0),
    (1, 0, 0),
    (-1, 0, 0),
    (0, 1, 0),
    (0, -1, 0),
    (0, 0, 1),
    (0, 0, -1),
    (1, 1, 0),
    (-1, -1, 0),
    (1, -1, 0),
    (-1, 1, 0),
    (1, 0, 1),
    (-1, 0, -1),
    (1, 0, -1),
    (-1, 0, 1),
    (0, 1, 1),
    (0, -1, -1),
    (0, 1, -1),
    (0, -1, 1),
)
Q = len(VELOCITIES)
WEIGHTS = (1.0 / 3.0,) + (1.0 / 18.0,) * 6 + (1.0 / 36.0,) * 12
W_AXIS = WEIGHTS[1]
W_DIAG = WEIGHTS[7]
COUPLING = -5.0
FINE_TAU = 1.1
COARSE_TAU = 0.8
TO_COARSE = 2.0 * COARSE_TAU / FINE_TAU
TO_FINE = FINE_TAU / (2.0 * COARSE_TAU)
UP = tuple(i for i in range(Q) if VELOCITIES[i][1] == 1)
DOWN = tuple(i for i in range(Q) if VELOCITIES[i][1] == -1)
NG = len(UP) + 1

VMEM = pl.BlockSpec(memory_space=pltpu.VMEM)
SMEM = pl.BlockSpec(memory_space=pltpu.SMEM)


def call(body, outs, specs, scratch=(), flops=10**6, moved=10**6):
    return pl.pallas_call(
        body,
        out_shape=outs,
        in_specs=specs,
        out_specs=jax.tree.map(lambda _: VMEM, outs),
        scratch_shapes=list(scratch),
        cost_estimate=pl.CostEstimate(flops=flops, bytes_accessed=moved, transcendentals=0),
        compiler_params=pltpu.CompilerParams(vmem_limit_bytes=GRANT),
    )


def f32(*shape):
    return jax.ShapeDtypeStruct(shape, jnp.float32)


def moments(f):
    density = f[0]
    momentum = [None, None, None]
    for i in range(1, Q, 2):
        density = density + (f[i] + f[i + 1])
        odd = f[i] - f[i + 1]
        for j in range(3):
            c = VELOCITIES[i][j]
            if c:
                term = odd if c > 0 else -odd
                if momentum[j] is None:
                    momentum[j] = term
                else:
                    momentum[j] = momentum[j] + odd if c > 0 else momentum[j] - odd
    return density, momentum


def balances(density, u, scale):
    base = 1.0 - 1.5 * (u[0] * u[0] + u[1] * u[1] + u[2] * u[2])
    scaled = {w: density * (w * scale) for w in set(WEIGHTS)}
    yield 0, scaled[WEIGHTS[0]] * base
    for i in range(1, Q, 2):
        along = None
        for j in range(3):
            c = VELOCITIES[i][j]
            if c:
                if along is None:
                    along = u[j] if c > 0 else -u[j]
                else:
                    along = along + u[j] if c > 0 else along - u[j]
        weight = scaled[WEIGHTS[i]]
        even = weight * (base + 4.5 * (along * along))
        odd = weight * (3.0 * along)
        yield i, even + odd
        yield i + 1, even - odd


def rescaled(f, factor, wanted):
    density, momentum = moments(f)
    inverse = 1.0 / density
    u = [m * inverse for m in momentum]
    found = {}
    for i, balance in balances(density, u, 1.0):
        if i in wanted:
            found[i] = balance + factor * (f[i] - balance)
    return 1.0 - jnp.exp(-density), found


def gradient_parts(p, shift_y, shift_z):
    above = shift_y(p, -1, "p")
    below = shift_y(p, 1, "p")
    front = shift_z(p, -1)
    back = shift_z(p, 1)
    n = range(len(p))
    dy = [above[q] - below[q] for q in n]
    sy = [above[q] + below[q] for q in n]
    dz = [front[q] - back[q] for q in n]
    tx = [W_AXIS * p[q] + W_DIAG * (sy[q] + (front[q] + back[q])) for q in n]
    mixed = [W_AXIS * p[q] + W_DIAG * sy[q] for q in n]
    mixed_front = shift_z(mixed, -1)
    mixed_back = shift_z(mixed, 1)
    dy_front = shift_z(dy, -1)
    dy_back = shift_z(dy, 1)
    gy = [W_AXIS * dy[q] + W_DIAG * (dy_front[q] + dy_back[q]) for q in n]
    gz = [mixed_front[q] - mixed_back[q] for q in n]
    return tx, [W_DIAG * v for v in dy], [W_DIAG * v for v in dz], gy, gz


def velocity_of(density, momentum, potential, pull, tau):
    inverse = 1.0 / density
    force = (-tau * COUPLING) * potential
    return [(momentum[j] + force * pull[j]) * inverse for j in range(3)]


def regroup_body(blocks, k_blocks, rows, slot_ref, in_ref, out_ref):
    for b in range(blocks):
        s = slot_ref[b]
        source = (b // k_blocks) * (rows * k_blocks) + b % k_blocks
        owner = lax.div(s, k_blocks)
        target = owner * (rows * k_blocks) + (s - owner * k_blocks)
        out_ref[pl.ds(target, rows, stride=k_blocks), :] = in_ref[
            pl.ds(source, rows, stride=k_blocks), :
        ]


def lane_ids():
    lane = lax.broadcasted_iota(jnp.int32, (SUB, LANES), 1)
    return lane % B, lane // B


def fine_shifts(ch_count, k_count, ghost):
    y, z = lane_ids()
    first_y, last_y = y == 0, y == B - 1
    first_z, last_z = z == 0, z == LANES // B - 1

    def shift_y(v, c, which):
        out = []
        for ch in range(ch_count):
            for k in range(k_count):
                q = ch * k_count + k
                if c > 0:
                    own = pltpu.roll(v[q], 1, 1)
                    carry = (
                        ghost(0, which, ch) if k == 0 else pltpu.roll(v[q - 1], LANES - (B - 1), 1)
                    )
                    out.append(jnp.where(first_y, carry, own))
                else:
                    own = pltpu.roll(v[q], LANES - 1, 1)
                    carry = (
                        ghost(1, which, ch)
                        if k == k_count - 1
                        else pltpu.roll(v[q + 1], B - 1, 1)
                    )
                    out.append(jnp.where(last_y, carry, own))
        return out

    def shift_z(v, c):
        rolled = [pltpu.roll(x, B if c > 0 else LANES - B, 1) for x in v]
        edge = first_z if c > 0 else last_z
        out = []
        for ch in range(ch_count):
            other = (ch - c) % ch_count
            for k in range(k_count):
                q = ch * k_count + k
                out.append(jnp.where(edge, rolled[other * k_count + k], rolled[q]))
        return out

    return shift_y, shift_z


def fine_step(src, offset, dst, ghosts, parts, ch_count, k_count, chunks):
    nq = ch_count * k_count
    qs = range(nq)
    for chunk in range(chunks):
        r = chunk * SUB
        f = [[src[i, q, pl.ds(offset + r, SUB), :] for i in range(Q)] for q in qs]
        moved = [moments(f[q]) for q in qs]
        p = [1.0 - jnp.exp(-moved[q][0]) for q in qs]

        def ghost(side, which, ch, r=r):
            return ghosts[side, NG - 1, ch, pl.ds(r, SUB), :]

        shift_y, shift_z = fine_shifts(ch_count, k_count, ghost)
        tx, dy, dz, gy, gz = gradient_parts(p, shift_y, shift_z)
        for q in qs:
            values = (tx[q], dy[q], dz[q], gy[q], gz[q], p[q], moved[q][0], *moved[q][1])
            for n, v in enumerate(values):
                parts[n, q, pl.ds(PAD + r, SUB), :] = v
    for chunk in range(chunks):
        r = chunk * SUB

        def ghost(side, which, ch, r=r):
            place = (UP if side == 0 else DOWN).index(which)
            return ghosts[side, place, ch, pl.ds(r, SUB), :]

        shift_y, shift_z = fine_shifts(ch_count, k_count, ghost)
        streams = []
        for q in qs:
            low = [parts[n, q, pl.ds(PAD + r - 1, SUB), :] for n in range(3)]
            high = [parts[n, q, pl.ds(PAD + r + 1, SUB), :] for n in range(3)]
            gy, gz, p, rho, mx, my, mz = (
                parts[n, q, pl.ds(PAD + r, SUB), :] for n in range(3, 10)
            )
            pull = [high[0] - low[0], gy + (high[1] + low[1]), gz + (high[2] + low[2])]
            u = velocity_of(rho, (mx, my, mz), p, pull, FINE_TAU)
            streams.append(balances(rho, u, 1.0 / FINE_TAU))
        for i in range(Q):
            cx, cy, cz = VELOCITIES[i]
            post = []
            for q in qs:
                _, balance = next(streams[q])
                h = src[i, q, pl.ds(offset + r, SUB), :]
                post.append(h * (1.0 - 1.0 / FINE_TAU) + balance)
            if cy:
                post = shift_y(post, cy, i)
            if cz:
                post = shift_z(post, cz)
            for q in qs:
                dst[i, q, pl.ds(PAD + r + cx, SUB), :] = post[q]


def fine_body(ch_count, k_count, own, left, right, ghosts, out, first, second, third, parts):
    nq = ch_count * k_count

    def gather(i, carry):
        for q in range(nq):
            first[i, q, pl.ds(0, HALO), :] = left[pl.ds(i * (HALO * nq) + q, HALO, stride=nq), :]
            first[i, q, pl.ds(HALO, B), :] = own[pl.ds(i * (B * nq) + q, B, stride=nq), :]
            first[i, q, pl.ds(HALO + B, HALO), :] = right[
                pl.ds(i * (HALO * nq) + q, HALO, stride=nq), :
            ]
        return carry

    lax.fori_loop(0, Q, gather, 0)
    chunks = (B + 2 * HALO) // SUB
    fine_step(first, 0, second, ghosts, parts, ch_count, k_count, chunks)
    fine_step(second, PAD, third, ghosts, parts, ch_count, k_count, chunks)

    def scatter(i, carry):
        for q in range(nq):
            out[pl.ds(i * (B * nq) + q, B, stride=nq), :] = third[i, q, pl.ds(PAD + HALO, B), :]
        return carry

    lax.fori_loop(0, Q, scatter, 0)


def fine_ghost_body(ch_count, rows, layers, spread, out, wide):
    for side in range(2):
        wide[...] = jnp.dot(
            layers[side],
            spread[...],
            precision=lax.Precision.HIGHEST,
            preferred_element_type=jnp.float32,
        )
        wanted = UP if side == 0 else DOWN
        for ch in range(ch_count):
            for r in range(0, rows, SUB):
                f = [
                    wide[pl.ds(i * rows + r, SUB), pl.ds(ch * LANES, LANES)] for i in range(Q)
                ]
                potential, found = rescaled(f, TO_FINE, wanted)
                for n, i in enumerate(wanted):
                    out[side, n, ch, pl.ds(r, SUB), :] = found[i]
                out[side, NG - 1, ch, pl.ds(r, SUB), :] = potential


GROUP = 16
STEP = 32
PLANES = -(-Q // GROUP)


def pack(load, ch_count, k_count, side):
    lane = lax.broadcasted_iota(jnp.int32, (SUB, LANES), 1)
    offset = B - 2 if side == 0 else 0
    kept = lane % STEP == offset
    k = k_count - 1 if side == 0 else 0
    planes = [None] * PLANES
    for i in range(Q):
        for ch in range(ch_count):
            q = ch * k_count + k
            v = load(i, q, 0) + load(i, q, 1)
            v = v + pltpu.roll(v, LANES - 1, 1)
            v = v + pltpu.roll(v, LANES - B, 1)
            v = jnp.where(kept, v, 0.0)
            shift = (2 * (i % GROUP) + ch - offset) % LANES
            if shift:
                v = pltpu.roll(v, shift, 1)
            n = i // GROUP
            planes[n] = v if planes[n] is None else planes[n] + v
    return planes


def restrict_body(ch_count, k_count, own, low, high):
    nq = ch_count * k_count

    def load(i, q, half):
        return own[pl.ds(i * (B * nq) + half * nq + q, SUB, stride=2 * nq), :]

    for side, out in enumerate((low, high)):
        for n, plane in enumerate(pack(load, ch_count, k_count, side)):
            out[n] = plane


def coarse_body(planes, state, out, packed, near, parts, out_pad):
    lane = lax.broadcasted_iota(jnp.int32, (SUB, LANES), 1)

    def shift_y(v, c, which):
        return [pltpu.roll(v[0], 1 if c > 0 else LANES - 1, 1)]

    def shift_z(v, c):
        return [pltpu.roll(v[0], 1 if c > 0 else SUB - 1, 0)]

    def prepare(x, carry):
        density, momentum = moments([state[i, x] for i in range(Q)])
        p = 1.0 - jnp.exp(-density)
        values = gradient_parts([p], shift_y, shift_z)
        values = [v[0] for v in values] + [p, density, *momentum]
        for n, v in enumerate(values):
            parts[n, x] = v
        return carry

    lax.fori_loop(0, planes, prepare, 0, unroll=2)

    inner = planes - HALO
    base = HALO // 2

    def update(x, carry):
        lower = [parts[n, x - 1] for n in range(3)]
        upper = [parts[n, x + 1] for n in range(3)]
        gy, gz, p, rho, mx, my, mz = (parts[n, x] for n in range(3, 10))
        pull = [upper[0] - lower[0], gy + (upper[1] + lower[1]), gz + (upper[2] + lower[2])]
        u = velocity_of(rho, (mx, my, mz), p, pull, COARSE_TAU)
        for i, balance in balances(rho, u, 1.0 / COARSE_TAU):
            cx, cy, cz = VELOCITIES[i]
            post = [state[i, x] * (1.0 - 1.0 / COARSE_TAU) + balance]
            if cy:
                post = shift_y(post, cy, i)
            if cz:
                post = shift_z(post, cz)
            inside = x + cx - base
            spare = jnp.where((inside >= 0) & (inside < inner), inside, inner)
            out_pad[i, spare] = post[0]
        return carry

    lax.fori_loop(base - 1, base + inner + 1, update, 0, unroll=2)
    out[...] = out_pad[:, :inner]

    def gather(i, carry):
        total = jnp.zeros((SUB, LANES), jnp.float32)
        for x in range(planes):
            here = (lane == 2 * x + 1) | (lane == 2 * x + 2)
            total = jnp.where(here, pltpu.roll(state[i, x], 2 * x + 2, 1), total)
        packed[i] = total
        return carry

    lax.fori_loop(0, Q, gather, 0)
    total = jnp.zeros((SUB, LANES), jnp.float32)
    for x in range(planes):
        p = parts[5, x]
        total = jnp.where(lane == 2 * x + 2, pltpu.roll(p, 2 * x + 1, 1), total)
        total = jnp.where(lane == 2 * x + 1, pltpu.roll(p, 2 * x + 3, 1), total)
    near[...] = total


def edges_body(
    ch_count, k_count, planes, left, right, low, high, high_left, high_right, packed, near, step,
    out, halo, rows, columns, ghost,
):
    nq = ch_count * k_count
    edge = HALO // 2
    inner = planes - HALO
    lane = lax.broadcasted_iota(jnp.int32, (SUB, LANES), 1)
    sided = lane % 2 == 0

    halo[...] = jnp.zeros_like(halo)

    def load(i, q, half):
        for at, ref in ((0, left), (edge, right)):
            start = i * (HALO * nq) + half * nq + q
            halo[i % 2, q, half, pl.ds(at, edge), :] = ref[pl.ds(start, edge, stride=2 * nq), :]
        return halo[i % 2, q, half]

    beside = pack(load, ch_count, k_count, 0)
    for n in range(PLANES):
        own_x = 2 * edge
        rows[n, pl.ds(2 + own_x, inner, stride=2), :] = low[n]
        rows[n, pl.ds(2, edge, stride=2), :] = beside[n][:edge]
        rows[n, pl.ds(2 + 2 * (edge + inner), edge, stride=2), :] = beside[n][edge : 2 * edge]
        rows[n, pl.ds(1 + own_x, inner, stride=2), :] = high[n]
        rows[n, pl.ds(1, edge, stride=2), :] = high_left[n, pl.ds(inner - edge, edge), :]
        rows[n, pl.ds(1 + 2 * (edge + inner), edge, stride=2), :] = high_right[
            n, pl.ds(0, edge), :
        ]
        columns[n] = rows[n].T
    per = LANES // STEP
    for i in range(Q):
        for ch in range(ch_count):
            ghost[i, pl.ds(ch * per, per), :] = (
                0.125 * columns[i // GROUP, pl.ds(2 * (i % GROUP) + ch, per, stride=STEP), :]
            )

    beyond, entering = rescaled([ghost[i] for i in range(Q)], TO_COARSE, UP + DOWN)
    density, momentum = moments([packed[i] for i in range(Q)])
    p = 1.0 - jnp.exp(-density)
    inside = near[...]
    above = jnp.where(sided, inside, beyond)
    below = jnp.where(sided, beyond, inside)

    def shift_y(v, c, which):
        return [below if c > 0 else above]

    def shift_z(v, c):
        return [pltpu.roll(v[0], 1 if c > 0 else SUB - 1, 0)]

    def shift_x(v, c):
        return pltpu.roll(v, 2 if c > 0 else LANES - 2, 1) if c else v

    tx, dy, dz, gy, gz = (v[0] for v in gradient_parts([p], shift_y, shift_z))
    pull = [
        shift_x(tx, -1) - shift_x(tx, 1),
        gy + (shift_x(dy, -1) + shift_x(dy, 1)),
        gz + (shift_x(dz, -1) + shift_x(dz, 1)),
    ]
    u = velocity_of(density, momentum, p, pull, COARSE_TAU)
    for i, balance in balances(density, u, 1.0 / COARSE_TAU):
        cx, cy, cz = VELOCITIES[i]
        v = packed[i] * (1.0 - 1.0 / COARSE_TAU) + balance
        if cy > 0:
            v = jnp.where(sided, entering[i], pltpu.roll(v, 1, 1))
            touched = lane < 2
        elif cy < 0:
            v = jnp.where(sided, pltpu.roll(v, LANES - 1, 1), entering[i])
            touched = lane >= LANES - 2
        else:
            touched = (lane == 0) | (lane == LANES - 1)
        v = shift_x(v, cx)
        if cz:
            v = shift_z([v], cz)[0]
        for x in range(inner):
            column = pltpu.roll(v, LANES - (2 * (x + edge) + 2), 1)
            out[i, x] = jnp.where(touched, column, step[i, x])


def ring(count, step):
    return [(i, (i + step) % count) for i in range(count)]


def slab_pairs(n_grp, n_wide, up, across):
    return [
        (g * n_wide + w, (g + across) % n_grp * n_wide + (w + up) % n_wide)
        for g in range(n_grp)
        for w in range(n_wide)
    ]


def local(fine_pop, coarse_pop, new_slot):
    k_count, q_count, cells = fine_pop.shape
    blocks = new_slot.shape[0]
    devices = blocks // k_count
    tiles = cells // LANES
    ch_count = tiles // B
    nq = ch_count * k_count
    axes = ("grp", "wide")
    n_grp, n_wide = lax.axis_size("grp"), lax.axis_size("wide")
    _, cx, cz, cy = coarse_pop.shape
    planes = cx + HALO
    fine_rows = B + 2 * HALO

    rows = pl.cdiv(Q * tiles, devices)
    pieces = fine_pop.reshape(k_count, Q, tiles, LANES)
    pieces = with_layout_constraint(pieces, Layout(major_to_minor=(1, 2, 0, 3)))
    pieces = pieces.transpose(1, 2, 0, 3)
    pieces = pieces.reshape(Q * tiles, k_count, LANES)
    if rows * devices != Q * tiles:
        pieces = jnp.pad(pieces, ((0, rows * devices - Q * tiles), (0, 0), (0, 0)))
    pieces = pieces.reshape(devices, rows, k_count, LANES)
    spread = lax.all_to_all(pieces, axes, 0, 0, tiled=True)
    edge = HALO // 2
    coarse_left = lax.ppermute(coarse_pop[:, cx - edge :], "grp", ring(n_grp, 1))
    coarse_right = lax.ppermute(coarse_pop[:, :edge], "grp", ring(n_grp, -1))
    last = coarse_pop[..., -1]
    below = []
    for part, across in ((last[:, cx - edge :], 1), (last, 0), (last[:, :edge], -1)):
        below.append(lax.ppermute(part, axes, slab_pairs(n_grp, n_wide, 1, across)))
    total = devices * rows * k_count
    regroup = call(
        functools.partial(regroup_body, blocks, k_count, rows),
        f32(total, LANES),
        [SMEM, VMEM],
        moved=8 * total * LANES,
    )
    outgoing = regroup(new_slot, spread.reshape(total, LANES))
    arrived = lax.all_to_all(
        outgoing.reshape(devices, rows, k_count, LANES), axes, 0, 0, tiled=True
    )
    coarse = jnp.concatenate([coarse_left, coarse_pop, coarse_right], axis=1)
    below = jnp.concatenate(below, axis=1)
    layers = jnp.repeat(jnp.stack([below, coarse[..., 0]]), 2, axis=2)
    layers = layers.reshape(2, Q * fine_rows, cz)
    lane = jnp.arange(ch_count * LANES) // (2 * B)
    one_hot = (jnp.arange(cz)[:, None] == lane[None, :]).astype(jnp.float32)
    fine_ghosts = call(
        functools.partial(fine_ghost_body, ch_count, fine_rows),
        f32(2, NG, ch_count, fine_rows, LANES),
        [VMEM, VMEM],
        [pltpu.VMEM((Q * fine_rows, ch_count * LANES), jnp.float32)],
    )(layers, one_hot)
    coarse_step, packed, near = call(
        functools.partial(coarse_body, planes),
        [f32(Q, cx, cz, cy), f32(Q, SUB, LANES), f32(SUB, LANES)],
        [VMEM],
        [
            pltpu.VMEM((10, planes, SUB, LANES), jnp.float32),
            pltpu.VMEM((Q, cx + 1, SUB, LANES), jnp.float32),
        ],
        flops=10**7,
    )(coarse)
    arrived, fine_ghosts, coarse_step, packed, near = lax.optimization_barrier(
        (arrived, fine_ghosts, coarse_step, packed, near)
    )
    own = arrived.reshape(total, LANES)[: Q * tiles * k_count]

    by_x = own.reshape(Q, B * nq, LANES)
    width = HALO * nq
    left = lax.ppermute(by_x[:, -width:], "grp", ring(n_grp, 1)).reshape(Q * width, LANES)
    right = lax.ppermute(by_x[:, :width], "grp", ring(n_grp, -1)).reshape(Q * width, LANES)

    low, first = call(
        functools.partial(restrict_body, ch_count, k_count),
        [f32(PLANES, SUB, LANES)] * 2,
        [VMEM],
    )(own)
    highs = []
    for across in (0, 1, -1):
        highs.append(lax.ppermute(first, axes, slab_pairs(n_grp, n_wide, -1, across)))

    padded = PAD + fine_rows + PAD
    fine = call(
        functools.partial(fine_body, ch_count, k_count),
        f32(Q * B * nq, LANES),
        [VMEM] * 4,
        [
            pltpu.VMEM((Q, nq, fine_rows, LANES), jnp.float32),
            pltpu.VMEM((Q, nq, padded, LANES), jnp.float32),
            pltpu.VMEM((Q, nq, padded, LANES), jnp.float32),
            pltpu.VMEM((10, nq, padded, LANES), jnp.float32),
        ],
        flops=10**7,
    )(own, left, right, fine_ghosts)

    coarse_out = call(
        functools.partial(edges_body, ch_count, k_count, planes),
        f32(Q, cx, cz, cy),
        [VMEM] * 9,
        [
            pltpu.VMEM((2, nq, 2, SUB, LANES), jnp.float32),
            pltpu.VMEM((PLANES, LANES, LANES), jnp.float32),
            pltpu.VMEM((PLANES, LANES, LANES), jnp.float32),
            pltpu.VMEM((Q, SUB, LANES), jnp.float32),
        ],
    )(left, right, low, *highs, packed, near, coarse_step)

    fine_out = fine.reshape(Q, tiles, k_count, LANES).transpose(2, 0, 1, 3)
    fine_out = fine_out.reshape(k_count, q_count, cells)
    return fine_out, coarse_out


def solution(mesh):
    return jax.shard_map(
        local,
        mesh=mesh,
        in_specs=(P(("grp", "wide"), None, None), P(None, "grp", None, "wide"), P()),
        out_specs=(P(("grp", "wide"), None, None), P(None, "grp", None, "wide")),
        check_vma=False,
    )
```

```python
import functools

import jax
import jax.numpy as jnp
from jax import lax
from jax.experimental import pallas as pl
from jax.experimental.layout import Layout, with_layout_constraint
from jax.experimental.pallas import tpu as pltpu
from jax.sharding import PartitionSpec as P


B = 16
LANES = 128
SUB = 8
HALO = 4
PAD = 8
GRANT = 24 << 20

VELOCITIES = (
    (0, 0, 0),
    (1, 0, 0),
    (-1, 0, 0),
    (0, 1, 0),
    (0, -1, 0),
    (0, 0, 1),
    (0, 0, -1),
    (1, 1, 0),
    (-1, -1, 0),
    (1, -1, 0),
    (-1, 1, 0),
    (1, 0, 1),
    (-1, 0, -1),
    (1, 0, -1),
    (-1, 0, 1),
    (0, 1, 1),
    (0, -1, -1),
    (0, 1, -1),
    (0, -1, 1),
)
Q = len(VELOCITIES)
WEIGHTS = (1.0 / 3.0,) + (1.0 / 18.0,) * 6 + (1.0 / 36.0,) * 12
W_DIAG = WEIGHTS[7]
COUPLING = -5.0
FINE_TAU = 1.1
COARSE_TAU = 0.8
TO_COARSE = 2.0 * COARSE_TAU / FINE_TAU
TO_FINE = FINE_TAU / (2.0 * COARSE_TAU)
UP = tuple(i for i in range(Q) if VELOCITIES[i][1] == 1)
DOWN = tuple(i for i in range(Q) if VELOCITIES[i][1] == -1)
NG = len(UP) + 1

VMEM = pl.BlockSpec(memory_space=pltpu.VMEM)
SMEM = pl.BlockSpec(memory_space=pltpu.SMEM)


def call(body, outs, specs, scratch=(), flops=10**6, moved=10**6):
    return pl.pallas_call(
        body,
        out_shape=outs,
        in_specs=specs,
        out_specs=jax.tree.map(lambda _: VMEM, outs),
        scratch_shapes=list(scratch),
        cost_estimate=pl.CostEstimate(flops=flops, bytes_accessed=moved, transcendentals=0),
        compiler_params=pltpu.CompilerParams(vmem_limit_bytes=GRANT),
    )


def f32(*shape):
    return jax.ShapeDtypeStruct(shape, jnp.float32)


def moments(f):
    density = f[0]
    momentum = [None, None, None]
    for i in range(1, Q, 2):
        density = density + (f[i] + f[i + 1])
        odd = f[i] - f[i + 1]
        for j in range(3):
            c = VELOCITIES[i][j]
            if c:
                term = odd if c > 0 else -odd
                if momentum[j] is None:
                    momentum[j] = term
                else:
                    momentum[j] = momentum[j] + odd if c > 0 else momentum[j] - odd
    return density, momentum


def balances(density, flux, scale):
    w = density * (W_DIAG * scale)
    half = 1.5 / density
    v = [x * half for x in flux]
    g = [x * (3.0 * W_DIAG * scale) for x in flux]
    g2 = [x + x for x in g]
    h = [g[j] * v[j] for j in range(3)]
    total = h[0] + h[1] + h[2]
    base = w - total * (1.0 / 3.0)
    base2 = base + base
    yield 0, base2 * (0.5 * WEIGHTS[0] / W_DIAG)
    for j in range(3):
        even = base2 + (h[j] + h[j])
        yield 2 * j + 1, even + g2[j]
        yield 2 * j + 2, even - g2[j]
    all_h = base + total
    i = 7
    for a, b, c in ((0, 1, 2), (0, 2, 1), (1, 2, 0)):
        even = all_h - h[c]
        cross = g2[a] * v[b]
        for sign in (1, -1):
            side = even + cross if sign > 0 else even - cross
            odd = g[a] + g[b] if sign > 0 else g[a] - g[b]
            yield i, side + odd
            yield i + 1, side - odd
            i += 2


def rescaled(f, factor, wanted):
    density, momentum = moments(f)
    found = {}
    for i, balance in balances(density, momentum, 1.0):
        if i in wanted:
            found[i] = balance + factor * (f[i] - balance)
    return 1.0 - jnp.exp(-density), found


def gradient_parts(p, shift_y, shift_z):
    above = shift_y(p, -1, "p")
    below = shift_y(p, 1, "p")
    front = shift_z(p, -1)
    back = shift_z(p, 1)
    n = range(len(p))
    dy = [above[q] - below[q] for q in n]
    dz = [front[q] - back[q] for q in n]
    mixed = [(p[q] + p[q]) + (above[q] + below[q]) for q in n]
    tx = [mixed[q] + (front[q] + back[q]) for q in n]
    mixed_front = shift_z(mixed, -1)
    mixed_back = shift_z(mixed, 1)
    dy_front = shift_z(dy, -1)
    dy_back = shift_z(dy, 1)
    gy = [(dy[q] + dy[q]) + (dy_front[q] + dy_back[q]) for q in n]
    gz = [mixed_front[q] - mixed_back[q] for q in n]
    return tx, dy, dz, gy, gz


def flux_of(momentum, potential, pull, tau):
    force = (-tau * COUPLING * W_DIAG) * potential
    return [momentum[j] + force * pull[j] for j in range(3)]


def regroup_body(blocks, k_blocks, rows, slot_ref, in_ref, out_ref):
    for b in range(blocks):
        s = slot_ref[b]
        source = (b // k_blocks) * (rows * k_blocks) + b % k_blocks
        owner = lax.div(s, k_blocks)
        target = owner * (rows * k_blocks) + (s - owner * k_blocks)
        out_ref[pl.ds(target, rows, stride=k_blocks), :] = in_ref[
            pl.ds(source, rows, stride=k_blocks), :
        ]


def lane_ids():
    lane = lax.broadcasted_iota(jnp.int32, (SUB, LANES), 1)
    return lane % B, lane // B


def fine_shifts(ch_count, k_count, ghost):
    y, z = lane_ids()
    first_y, last_y = y == 0, y == B - 1
    first_z, last_z = z == 0, z == LANES // B - 1

    def shift_y(v, c, which):
        out = []
        for ch in range(ch_count):
            for k in range(k_count):
                q = ch * k_count + k
                if c > 0:
                    own = pltpu.roll(v[q], 1, 1)
                    carry = (
                        ghost(0, which, ch) if k == 0 else pltpu.roll(v[q - 1], LANES - (B - 1), 1)
                    )
                    out.append(jnp.where(first_y, carry, own))
                else:
                    own = pltpu.roll(v[q], LANES - 1, 1)
                    carry = (
                        ghost(1, which, ch)
                        if k == k_count - 1
                        else pltpu.roll(v[q + 1], B - 1, 1)
                    )
                    out.append(jnp.where(last_y, carry, own))
        return out

    def shift_z(v, c):
        rolled = [pltpu.roll(x, B if c > 0 else LANES - B, 1) for x in v]
        edge = first_z if c > 0 else last_z
        out = []
        for ch in range(ch_count):
            other = (ch - c) % ch_count
            for k in range(k_count):
                q = ch * k_count + k
                out.append(jnp.where(edge, rolled[other * k_count + k], rolled[q]))
        return out

    return shift_y, shift_z


def substep(load, store, ghosts, start, parts, ch_count, k_count, chunks, density_of=None):
    qs = range(ch_count * k_count)
    for chunk in range(chunks):
        r = chunk * SUB

        def ghost(side, which, ch, r=r):
            return ghosts[side, NG - 1, ch, pl.ds(start + r, SUB), :]

        moved = [moments([load(i, q, r) for i in range(Q)]) for q in qs]
        density = [moved[q][0] for q in qs]
        if density_of is not None:
            density = [density_of(q, r, density[q]) for q in qs]
        p = [1.0 - jnp.exp(-density[q]) for q in qs]
        shift_y, shift_z = fine_shifts(ch_count, k_count, ghost)
        tx, dy, dz, gy, gz = gradient_parts(p, shift_y, shift_z)
        for q in qs:
            values = (tx[q], dy[q], dz[q], gy[q], gz[q], p[q], density[q], *moved[q][1])
            for n, v in enumerate(values):
                parts[n, q, pl.ds(PAD + r, SUB), :] = v
    for chunk in range(chunks):
        r = chunk * SUB

        def ghost(side, which, ch, r=r):
            place = (UP if side == 0 else DOWN).index(which)
            return ghosts[side, place, ch, pl.ds(start + r, SUB), :]

        shift_y, shift_z = fine_shifts(ch_count, k_count, ghost)
        streams = []
        for q in qs:
            low = [parts[n, q, pl.ds(PAD + r - 1, SUB), :] for n in range(3)]
            high = [parts[n, q, pl.ds(PAD + r + 1, SUB), :] for n in range(3)]
            gy, gz, p, rho, mx, my, mz = (
                parts[n, q, pl.ds(PAD + r, SUB), :] for n in range(3, 10)
            )
            pull = [high[0] - low[0], gy + (high[1] + low[1]), gz + (high[2] + low[2])]
            flux = flux_of((mx, my, mz), p, pull, FINE_TAU)
            streams.append(balances(rho, flux, 1.0 / FINE_TAU))
        for i in range(Q):
            cx, cy, cz = VELOCITIES[i]
            post = []
            for q in qs:
                _, balance = next(streams[q])
                post.append(load(i, q, r) * (1.0 - 1.0 / FINE_TAU) + balance)
            if cy:
                post = shift_y(post, cy, i)
            if cz:
                post = shift_z(post, cz)
            for q in qs:
                store(i, q, r, cx, post[q])


CROSS = 5
FROM_DENSITY = Q
FROM_ENTER = Q + 1
FROM_PARTIAL = Q + 1 + CROSS
SENT = Q + 2 + CROSS


def edge_rows(nq):
    return SENT * nq + PLANES * (HALO // 2)


def sent_rows(nq):
    return -(-edge_rows(nq) // SUB) * SUB


def along(c):
    return [i for i in range(Q) if VELOCITIES[i][0] == c]


def send_body(
    ch_count, k_count, own, ghosts, to_left, to_right, low, high, rim, moved, parts
):
    nq = ch_count * k_count
    per = B * nq
    edge = HALO // 2

    for i in range(Q):
        for q in range(nq):
            rim[i, q, pl.ds(0, HALO), :] = own[pl.ds(i * per + q, HALO, stride=nq), :]
            rim[i, q, pl.ds(HALO, HALO), :] = own[
                pl.ds(i * per + (B - HALO) * nq + q, HALO, stride=nq), :
            ]

    def load(i, q, r):
        return rim[i, q]

    def store(i, q, r, cx, v):
        moved[i, q, pl.ds(PAD + cx, SUB), :] = v

    substep(load, store, ghosts, 0, parts, ch_count, k_count, 1)

    def restricted(i, q, half):
        return own[pl.ds(i * per + half * nq + q, SUB, stride=2 * nq), :]

    lows = pack(restricted, ch_count, k_count, 0)
    for n, plane in enumerate(lows):
        low[n] = plane
    for n, plane in enumerate(pack(restricted, ch_count, k_count, 1)):
        high[n] = plane

    for c, out, outer in ((1, to_right, B - 1), (-1, to_left, 0)):
        first = PAD + (SUB - 1 if c > 0 else 0)
        second = first - c
        for i in range(Q):
            out[pl.ds(i * nq, nq), :] = own[pl.ds(i * per + outer * nq, nq), :]
        for q in range(nq):
            out[pl.ds(FROM_DENSITY * nq + q, 1), :] = parts[6, q, pl.ds(second, 1), :]
            for n, i in enumerate(along(c)):
                out[pl.ds((FROM_ENTER + n) * nq + q, 1), :] = moved[i, q, pl.ds(first, 1), :]
            total = None
            for i in along(0) + along(c):
                v = moved[i, q, pl.ds(second, 1), :]
                total = v if total is None else total + v
            out[pl.ds(FROM_PARTIAL * nq + q, 1), :] = total
        for n in range(PLANES):
            x = SUB - edge if c > 0 else 0
            out[pl.ds(SENT * nq + n * edge, edge), :] = lows[n][x : x + edge]
        spare = sent_rows(nq) - edge_rows(nq)
        if spare:
            out[pl.ds(edge_rows(nq), spare), :] = jnp.zeros((spare, LANES), jnp.float32)


def inner_body(ch_count, k_count, own, ghosts, out, parts):
    nq = ch_count * k_count

    def load(i, q, r):
        return own[pl.ds(i * (B * nq) + r * nq + q, SUB, stride=nq), :]

    def store(i, q, r, cx, v):
        out[i, q, pl.ds(PAD + r + cx, SUB), :] = v

    substep(load, store, ghosts, HALO, parts, ch_count, k_count, B // SUB)


def fine_body(
    ch_count, k_count, own, left, right, inner, ghosts, rim_ghosts, out, rim, half, third, parts
):
    nq = ch_count * k_count
    per = B * nq
    row = lax.broadcasted_iota(jnp.int32, (SUB, LANES), 0)
    origin = PAD + HALO

    layers = Q * nq
    rim[pl.ds(1, layers, stride=SUB), :] = left[pl.ds(0, layers), :]
    rim[pl.ds(6, layers, stride=SUB), :] = right[pl.ds(0, layers), :]
    for i in range(Q):
        for sub, x in ((2, 0), (3, 1), (4, B - 2), (5, B - 1)):
            rim[pl.ds(i * (nq * SUB) + sub, nq, stride=SUB), :] = own[
                pl.ds(i * per + x * nq, nq), :
            ]

    def spread(ref, plane, q):
        return jnp.broadcast_to(ref[pl.ds(plane * nq + q, 1), :], (SUB, LANES))

    def load_rim(i, q, r):
        return rim[pl.ds((i * nq + q) * SUB, SUB), :]

    def rim_density(q, r, density):
        density = jnp.where(row == 0, spread(left, FROM_DENSITY, q), density)
        return jnp.where(row == SUB - 1, spread(right, FROM_DENSITY, q), density)

    outgoing = {(c, q): None for c in (-1, 1) for q in range(nq)}

    def store_rim(i, q, r, cx, v):
        half[i, q, pl.ds(origin - 2 + cx, SUB), :] = v
        half[i, q, pl.ds(origin + B - 6 + cx, SUB), :] = v
        if cx:
            seen = outgoing[cx, q]
            outgoing[cx, q] = v if seen is None else seen + v

    substep(load_rim, store_rim, rim_ghosts, 0, parts, ch_count, k_count, 1, rim_density)
    for i in range(Q):
        cx = VELOCITIES[i][0]
        for q in range(nq):
            half[i, q, pl.ds(origin + 1 + cx, B - 2), :] = inner[i, q, pl.ds(PAD + 1 + cx, B - 2), :]
            if cx:
                ref = left if cx > 0 else right
                at = origin - 1 if cx > 0 else origin + B
                place = FROM_ENTER + along(cx).index(i)
                half[i, q, pl.ds(at, 1), :] = ref[pl.ds(place * nq + q, 1), :]

    def load(i, q, r):
        return half[i, q, pl.ds(PAD + r, SUB), :]

    def store(i, q, r, cx, v):
        third[i, q, pl.ds(PAD + r + cx, SUB), :] = v

    chunks = (B + 2 * HALO) // SUB

    def density_of(q, r, density):
        if r == 0:
            value = spread(left, FROM_PARTIAL, q) + pltpu.roll(outgoing[-1, q], 1, 0)
            return jnp.where(row == HALO - 2, value, density)
        if r == (chunks - 1) * SUB:
            value = spread(right, FROM_PARTIAL, q) + pltpu.roll(outgoing[1, q], SUB - 1, 0)
            return jnp.where(row == SUB - HALO + 1, value, density)
        return density

    substep(load, store, ghosts, 0, parts, ch_count, k_count, chunks, density_of)

    def scatter(i, carry):
        for q in range(nq):
            out[pl.ds(i * per + q, B, stride=nq), :] = third[i, q, pl.ds(origin, B), :]
        return carry

    lax.fori_loop(0, Q, scatter, 0)


def fine_ghost_body(ch_count, rows, layers, spread, out, send_ghosts, rim_ghosts, wide):
    for side in range(2):
        wide[...] = jnp.dot(
            layers[side],
            spread[...],
            precision=lax.Precision.HIGHEST,
            preferred_element_type=jnp.float32,
        )
        wanted = UP if side == 0 else DOWN
        for ch in range(ch_count):
            for r in range(0, rows, SUB):
                f = [
                    wide[pl.ds(i * rows + r, SUB), pl.ds(ch * LANES, LANES)] for i in range(Q)
                ]
                potential, found = rescaled(f, TO_FINE, wanted)
                for n, i in enumerate(wanted):
                    out[side, n, ch, pl.ds(r, SUB), :] = found[i]
                out[side, NG - 1, ch, pl.ds(r, SUB), :] = potential
            for n in range(NG):
                for ref, lower, upper in (
                    (send_ghosts, HALO, rows - 2 * HALO),
                    (rim_ghosts, 2, rows - HALO - 2),
                ):
                    ref[side, n, ch, pl.ds(0, HALO), :] = out[side, n, ch, pl.ds(lower, HALO), :]
                    ref[side, n, ch, pl.ds(HALO, HALO), :] = out[
                        side, n, ch, pl.ds(upper, HALO), :
                    ]


GROUP = 16
STEP = 32
PLANES = -(-Q // GROUP)


def pack(load, ch_count, k_count, side):
    lane = lax.broadcasted_iota(jnp.int32, (SUB, LANES), 1)
    offset = B - 2 if side == 0 else 0
    kept = lane % STEP == offset
    k = k_count - 1 if side == 0 else 0
    planes = [None] * PLANES
    for i in range(Q):
        for ch in range(ch_count):
            q = ch * k_count + k
            v = load(i, q, 0) + load(i, q, 1)
            v = v + pltpu.roll(v, LANES - 1, 1)
            v = v + pltpu.roll(v, LANES - B, 1)
            v = jnp.where(kept, v, 0.0)
            shift = (2 * (i % GROUP) + ch - offset) % LANES
            if shift:
                v = pltpu.roll(v, shift, 1)
            n = i // GROUP
            planes[n] = v if planes[n] is None else planes[n] + v
    return planes


def coarse_body(planes, state, out, packed, near, parts, out_pad):
    lane = lax.broadcasted_iota(jnp.int32, (SUB, LANES), 1)

    def shift_y(v, c, which):
        return [pltpu.roll(v[0], 1 if c > 0 else LANES - 1, 1)]

    def shift_z(v, c):
        return [pltpu.roll(v[0], 1 if c > 0 else SUB - 1, 0)]

    def prepare(x, carry):
        density, momentum = moments([state[i, x] for i in range(Q)])
        p = 1.0 - jnp.exp(-density)
        values = gradient_parts([p], shift_y, shift_z)
        values = [v[0] for v in values] + [p, density, *momentum]
        for n, v in enumerate(values):
            parts[n, x] = v
        return carry

    lax.fori_loop(0, planes, prepare, 0, unroll=2)

    inner = planes - HALO
    base = HALO // 2

    def update(x, carry):
        lower = [parts[n, x - 1] for n in range(3)]
        upper = [parts[n, x + 1] for n in range(3)]
        gy, gz, p, rho, mx, my, mz = (parts[n, x] for n in range(3, 10))
        pull = [upper[0] - lower[0], gy + (upper[1] + lower[1]), gz + (upper[2] + lower[2])]
        flux = flux_of((mx, my, mz), p, pull, COARSE_TAU)
        for i, balance in balances(rho, flux, 1.0 / COARSE_TAU):
            cx, cy, cz = VELOCITIES[i]
            post = [state[i, x] * (1.0 - 1.0 / COARSE_TAU) + balance]
            if cy:
                post = shift_y(post, cy, i)
            if cz:
                post = shift_z(post, cz)
            inside = x + cx - base
            spare = jnp.where((inside >= 0) & (inside < inner), inside, inner)
            out_pad[i, spare] = post[0]
        return carry

    lax.fori_loop(base - 1, base + inner + 1, update, 0, unroll=2)
    out[...] = out_pad[:, :inner]

    def gather(i, carry):
        total = jnp.zeros((SUB, LANES), jnp.float32)
        for x in range(planes):
            here = (lane == 2 * x + 1) | (lane == 2 * x + 2)
            total = jnp.where(here, pltpu.roll(state[i, x], 2 * x + 2, 1), total)
        packed[i] = total
        return carry

    lax.fori_loop(0, Q, gather, 0)
    total = jnp.zeros((SUB, LANES), jnp.float32)
    for x in range(planes):
        p = parts[5, x]
        total = jnp.where(lane == 2 * x + 2, pltpu.roll(p, 2 * x + 1, 1), total)
        total = jnp.where(lane == 2 * x + 1, pltpu.roll(p, 2 * x + 3, 1), total)
    near[...] = total


def edges_body(
    ch_count, k_count, planes, left, right, low, high, high_left, high_right, packed, near, step,
    out, rows, columns, ghost,
):
    nq = ch_count * k_count
    edge = HALO // 2
    inner = planes - HALO
    lane = lax.broadcasted_iota(jnp.int32, (SUB, LANES), 1)
    sided = lane % 2 == 0

    for n in range(PLANES):
        own_x = 2 * edge
        rows[n, pl.ds(2 + own_x, inner, stride=2), :] = low[n]
        beside = SENT * nq + n * edge
        rows[n, pl.ds(2, edge, stride=2), :] = left[pl.ds(beside, edge), :]
        rows[n, pl.ds(2 + 2 * (edge + inner), edge, stride=2), :] = right[
            pl.ds(beside, edge), :
        ]
        rows[n, pl.ds(1 + own_x, inner, stride=2), :] = high[n]
        rows[n, pl.ds(1, edge, stride=2), :] = high_left[n, pl.ds(inner - edge, edge), :]
        rows[n, pl.ds(1 + 2 * (edge + inner), edge, stride=2), :] = high_right[
            n, pl.ds(0, edge), :
        ]
        columns[n] = rows[n].T
    per = LANES // STEP
    for i in range(Q):
        for ch in range(ch_count):
            ghost[i, pl.ds(ch * per, per), :] = (
                0.125 * columns[i // GROUP, pl.ds(2 * (i % GROUP) + ch, per, stride=STEP), :]
            )

    beyond, entering = rescaled([ghost[i] for i in range(Q)], TO_COARSE, UP + DOWN)
    density, momentum = moments([packed[i] for i in range(Q)])
    p = 1.0 - jnp.exp(-density)
    inside = near[...]
    above = jnp.where(sided, inside, beyond)
    below = jnp.where(sided, beyond, inside)

    def shift_y(v, c, which):
        return [below if c > 0 else above]

    def shift_z(v, c):
        return [pltpu.roll(v[0], 1 if c > 0 else SUB - 1, 0)]

    def shift_x(v, c):
        return pltpu.roll(v, 2 if c > 0 else LANES - 2, 1) if c else v

    tx, dy, dz, gy, gz = (v[0] for v in gradient_parts([p], shift_y, shift_z))
    pull = [
        shift_x(tx, -1) - shift_x(tx, 1),
        gy + (shift_x(dy, -1) + shift_x(dy, 1)),
        gz + (shift_x(dz, -1) + shift_x(dz, 1)),
    ]
    flux = flux_of(momentum, p, pull, COARSE_TAU)
    for i, balance in balances(density, flux, 1.0 / COARSE_TAU):
        cx, cy, cz = VELOCITIES[i]
        v = packed[i] * (1.0 - 1.0 / COARSE_TAU) + balance
        if cy > 0:
            v = jnp.where(sided, entering[i], pltpu.roll(v, 1, 1))
            touched = lane < 2
        elif cy < 0:
            v = jnp.where(sided, pltpu.roll(v, LANES - 1, 1), entering[i])
            touched = lane >= LANES - 2
        else:
            touched = (lane == 0) | (lane == LANES - 1)
        v = shift_x(v, cx)
        if cz:
            v = shift_z([v], cz)[0]
        for x in range(inner):
            column = pltpu.roll(v, LANES - (2 * (x + edge) + 2), 1)
            out[i, x] = jnp.where(touched, column, step[i, x])


def ring(count, step):
    return [(i, (i + step) % count) for i in range(count)]


def slab_pairs(n_grp, n_wide, up, across):
    return [
        (g * n_wide + w, (g + across) % n_grp * n_wide + (w + up) % n_wide)
        for g in range(n_grp)
        for w in range(n_wide)
    ]


def local(fine_pop, coarse_pop, new_slot):
    k_count, q_count, cells = fine_pop.shape
    blocks = new_slot.shape[0]
    devices = blocks // k_count
    tiles = cells // LANES
    ch_count = tiles // B
    nq = ch_count * k_count
    axes = ("grp", "wide")
    n_grp, n_wide = lax.axis_size("grp"), lax.axis_size("wide")
    _, cx, cz, cy = coarse_pop.shape
    planes = cx + HALO
    fine_rows = B + 2 * HALO

    rows = pl.cdiv(Q * tiles, devices)
    pieces = fine_pop.reshape(k_count, Q, tiles, LANES)
    pieces = with_layout_constraint(pieces, Layout(major_to_minor=(1, 2, 0, 3)))
    pieces = pieces.transpose(1, 2, 0, 3)
    pieces = pieces.reshape(Q * tiles, k_count, LANES)
    if rows * devices != Q * tiles:
        pieces = jnp.pad(pieces, ((0, rows * devices - Q * tiles), (0, 0), (0, 0)))
    pieces = pieces.reshape(devices, rows, k_count, LANES)
    spread = lax.all_to_all(pieces, axes, 0, 0, tiled=True)
    edge = HALO // 2
    coarse_left = lax.ppermute(coarse_pop[:, cx - edge :], "grp", ring(n_grp, 1))
    coarse_right = lax.ppermute(coarse_pop[:, :edge], "grp", ring(n_grp, -1))
    last = coarse_pop[..., -1]
    below = []
    for part, across in ((last[:, cx - edge :], 1), (last, 0), (last[:, :edge], -1)):
        below.append(lax.ppermute(part, axes, slab_pairs(n_grp, n_wide, 1, across)))
    total = devices * rows * k_count
    regroup = call(
        functools.partial(regroup_body, blocks, k_count, rows),
        f32(total, LANES),
        [SMEM, VMEM],
        moved=8 * total * LANES,
    )
    outgoing = regroup(new_slot, spread.reshape(total, LANES))
    arrived = lax.all_to_all(
        outgoing.reshape(devices, rows, k_count, LANES), axes, 0, 0, tiled=True
    )
    coarse = jnp.concatenate([coarse_left, coarse_pop, coarse_right], axis=1)
    below = jnp.concatenate(below, axis=1)
    layers = jnp.repeat(jnp.stack([below, coarse[..., 0]]), 2, axis=2)
    layers = layers.reshape(2, Q * fine_rows, cz)
    lane = jnp.arange(ch_count * LANES) // (2 * B)
    one_hot = (jnp.arange(cz)[:, None] == lane[None, :]).astype(jnp.float32)
    fine_ghosts, send_ghosts, rim_ghosts = call(
        functools.partial(fine_ghost_body, ch_count, fine_rows),
        [f32(2, NG, ch_count, n, LANES) for n in (fine_rows, SUB, SUB)],
        [VMEM, VMEM],
        [pltpu.VMEM((Q * fine_rows, ch_count * LANES), jnp.float32)],
    )(layers, one_hot)
    coarse_step, packed, near = call(
        functools.partial(coarse_body, planes),
        [f32(Q, cx, cz, cy), f32(Q, SUB, LANES), f32(SUB, LANES)],
        [VMEM],
        [
            pltpu.VMEM((10, planes, SUB, LANES), jnp.float32),
            pltpu.VMEM((Q, cx + 1, SUB, LANES), jnp.float32),
        ],
        flops=10**7,
    )(coarse)
    hidden = (fine_ghosts, send_ghosts, rim_ghosts, coarse_step, packed, near)
    arrived, hidden = lax.optimization_barrier((arrived, hidden))
    fine_ghosts, send_ghosts, rim_ghosts, coarse_step, packed, near = hidden
    own = arrived.reshape(total, LANES)[: Q * tiles * k_count]

    padded = PAD + fine_rows + PAD
    to_left, to_right, low, first = call(
        functools.partial(send_body, ch_count, k_count),
        [f32(sent_rows(nq), LANES)] * 2 + [f32(PLANES, SUB, LANES)] * 2,
        [VMEM] * 2,
        [
            pltpu.VMEM((Q, nq, SUB, LANES), jnp.float32),
            pltpu.VMEM((Q, nq, 3 * PAD, LANES), jnp.float32),
            pltpu.VMEM((10, nq, 3 * PAD, LANES), jnp.float32),
        ],
    )(own, send_ghosts)
    left = lax.ppermute(to_right, "grp", ring(n_grp, 1))
    right = lax.ppermute(to_left, "grp", ring(n_grp, -1))
    inner = call(
        functools.partial(inner_body, ch_count, k_count),
        f32(Q, nq, PAD + B + PAD, LANES),
        [VMEM] * 2,
        [pltpu.VMEM((10, nq, PAD + B + PAD, LANES), jnp.float32)],
        flops=10**7,
    )(own, fine_ghosts)
    highs = []
    for across in (0, 1, -1):
        highs.append(lax.ppermute(first, axes, slab_pairs(n_grp, n_wide, -1, across)))

    fine = call(
        functools.partial(fine_body, ch_count, k_count),
        f32(Q * B * nq, LANES),
        [VMEM] * 6,
        [
            pltpu.VMEM((Q * nq * SUB, LANES), jnp.float32),
            pltpu.VMEM((Q, nq, padded, LANES), jnp.float32),
            pltpu.VMEM((Q, nq, padded, LANES), jnp.float32),
            pltpu.VMEM((10, nq, padded, LANES), jnp.float32),
        ],
        flops=10**7,
    )(own, left, right, inner, fine_ghosts, rim_ghosts)

    coarse_out = call(
        functools.partial(edges_body, ch_count, k_count, planes),
        f32(Q, cx, cz, cy),
        [VMEM] * 9,
        [
            pltpu.VMEM((PLANES, LANES, LANES), jnp.float32),
            pltpu.VMEM((PLANES, LANES, LANES), jnp.float32),
            pltpu.VMEM((Q, SUB, LANES), jnp.float32),
        ],
    )(left, right, low, *highs, packed, near, coarse_step)

    fine_out = fine.reshape(Q, tiles, k_count, LANES).transpose(2, 0, 1, 3)
    fine_out = fine_out.reshape(k_count, q_count, cells)
    return fine_out, coarse_out


def solution(mesh):
    return jax.shard_map(
        local,
        mesh=mesh,
        in_specs=(P(("grp", "wide"), None, None), P(None, "grp", None, "wide"), P()),
        out_specs=(P(("grp", "wide"), None, None), P(None, "grp", None, "wide")),
        check_vma=False,
    )
```

```python
import functools

import jax
import jax.numpy as jnp
from jax import lax
from jax.experimental import pallas as pl
from jax.experimental.layout import Layout, with_layout_constraint
from jax.experimental.pallas import tpu as pltpu
from jax.sharding import PartitionSpec as P


B = 16
LANES = 128
SUB = 8
HALO = 4
PAD = 8
GRANT = 24 << 20
PIECES = 8

VELOCITIES = (
    (0, 0, 0),
    (1, 0, 0),
    (-1, 0, 0),
    (0, 1, 0),
    (0, -1, 0),
    (0, 0, 1),
    (0, 0, -1),
    (1, 1, 0),
    (-1, -1, 0),
    (1, -1, 0),
    (-1, 1, 0),
    (1, 0, 1),
    (-1, 0, -1),
    (1, 0, -1),
    (-1, 0, 1),
    (0, 1, 1),
    (0, -1, -1),
    (0, 1, -1),
    (0, -1, 1),
)
Q = len(VELOCITIES)
WEIGHTS = (1.0 / 3.0,) + (1.0 / 18.0,) * 6 + (1.0 / 36.0,) * 12
W_DIAG = WEIGHTS[7]
COUPLING = -5.0
FINE_TAU = 1.1
COARSE_TAU = 0.8
TO_COARSE = 2.0 * COARSE_TAU / FINE_TAU
TO_FINE = FINE_TAU / (2.0 * COARSE_TAU)
UP = tuple(i for i in range(Q) if VELOCITIES[i][1] == 1)
DOWN = tuple(i for i in range(Q) if VELOCITIES[i][1] == -1)
NG = len(UP) + 1

VMEM = pl.BlockSpec(memory_space=pltpu.VMEM)
SMEM = pl.BlockSpec(memory_space=pltpu.SMEM)
HBM = pl.BlockSpec(memory_space=pl.ANY)


def call(body, outs, specs, scratch=(), flops=10**6, moved=10**6, place=VMEM):
    return pl.pallas_call(
        body,
        out_shape=outs,
        in_specs=specs,
        out_specs=jax.tree.map(lambda _: place, outs),
        scratch_shapes=list(scratch),
        cost_estimate=pl.CostEstimate(flops=flops, bytes_accessed=moved, transcendentals=0),
        compiler_params=pltpu.CompilerParams(vmem_limit_bytes=GRANT),
    )


def f32(*shape):
    return jax.ShapeDtypeStruct(shape, jnp.float32)


def moments(f):
    density = f[0]
    momentum = [None, None, None]
    for i in range(1, Q, 2):
        density = density + (f[i] + f[i + 1])
        odd = f[i] - f[i + 1]
        for j in range(3):
            c = VELOCITIES[i][j]
            if c:
                term = odd if c > 0 else -odd
                if momentum[j] is None:
                    momentum[j] = term
                else:
                    momentum[j] = momentum[j] + odd if c > 0 else momentum[j] - odd
    return density, momentum


def balances(density, flux, scale):
    w = density * (W_DIAG * scale)
    half = 1.5 / density
    v = [x * half for x in flux]
    g = [x * (3.0 * W_DIAG * scale) for x in flux]
    g2 = [x + x for x in g]
    h = [g[j] * v[j] for j in range(3)]
    total = h[0] + h[1] + h[2]
    base = w - total * (1.0 / 3.0)
    base2 = base + base
    yield 0, base2 * (0.5 * WEIGHTS[0] / W_DIAG)
    for j in range(3):
        even = base2 + (h[j] + h[j])
        yield 2 * j + 1, even + g2[j]
        yield 2 * j + 2, even - g2[j]
    all_h = base + total
    i = 7
    for a, b, c in ((0, 1, 2), (0, 2, 1), (1, 2, 0)):
        even = all_h - h[c]
        cross = g2[a] * v[b]
        for sign in (1, -1):
            side = even + cross if sign > 0 else even - cross
            odd = g[a] + g[b] if sign > 0 else g[a] - g[b]
            yield i, side + odd
            yield i + 1, side - odd
            i += 2


def rescaled(f, factor, wanted):
    density, momentum = moments(f)
    found = {}
    for i, balance in balances(density, momentum, 1.0):
        if i in wanted:
            found[i] = balance + factor * (f[i] - balance)
    return 1.0 - jnp.exp(-density), found


def gradient_parts(p, shift_y, shift_z):
    above = shift_y(p, -1, "p")
    below = shift_y(p, 1, "p")
    front = shift_z(p, -1)
    back = shift_z(p, 1)
    n = range(len(p))
    dy = [above[q] - below[q] for q in n]
    dz = [front[q] - back[q] for q in n]
    mixed = [(p[q] + p[q]) + (above[q] + below[q]) for q in n]
    tx = [mixed[q] + (front[q] + back[q]) for q in n]
    mixed_front = shift_z(mixed, -1)
    mixed_back = shift_z(mixed, 1)
    dy_front = shift_z(dy, -1)
    dy_back = shift_z(dy, 1)
    gy = [(dy[q] + dy[q]) + (dy_front[q] + dy_back[q]) for q in n]
    gz = [mixed_front[q] - mixed_back[q] for q in n]
    return tx, dy, dz, gy, gz


def flux_of(momentum, potential, pull, tau):
    force = (-tau * COUPLING * W_DIAG) * potential
    return [momentum[j] + force * pull[j] for j in range(3)]


def regroup_body(blocks, k_blocks, rows, target_ref, in_ref, out_ref):
    for b in range(blocks):
        source = (b // k_blocks) * (rows * k_blocks) + b % k_blocks
        out_ref[pl.ds(target_ref[b], rows, stride=k_blocks), :] = in_ref[
            pl.ds(source, rows, stride=k_blocks), :
        ]


def lane_ids():
    lane = lax.broadcasted_iota(jnp.int32, (SUB, LANES), 1)
    return lane % B, lane // B


def fine_shifts(ch_count, k_count, ghost):
    y, z = lane_ids()
    first_y, last_y = y == 0, y == B - 1
    first_z, last_z = z == 0, z == LANES // B - 1

    def shift_y(v, c, which):
        out = []
        for ch in range(ch_count):
            for k in range(k_count):
                q = ch * k_count + k
                if c > 0:
                    own = pltpu.roll(v[q], 1, 1)
                    carry = (
                        ghost(0, which, ch) if k == 0 else pltpu.roll(v[q - 1], LANES - (B - 1), 1)
                    )
                    out.append(jnp.where(first_y, carry, own))
                else:
                    own = pltpu.roll(v[q], LANES - 1, 1)
                    carry = (
                        ghost(1, which, ch)
                        if k == k_count - 1
                        else pltpu.roll(v[q + 1], B - 1, 1)
                    )
                    out.append(jnp.where(last_y, carry, own))
        return out

    def shift_z(v, c):
        rolled = [pltpu.roll(x, B if c > 0 else LANES - B, 1) for x in v]
        edge = first_z if c > 0 else last_z
        out = []
        for ch in range(ch_count):
            other = (ch - c) % ch_count
            for k in range(k_count):
                q = ch * k_count + k
                out.append(jnp.where(edge, rolled[other * k_count + k], rolled[q]))
        return out

    return shift_y, shift_z


def substep(load, store, ghosts, start, parts, ch_count, k_count, chunks, density_of=None):
    qs = range(ch_count * k_count)
    for chunk in range(chunks):
        r = chunk * SUB

        def ghost(side, which, ch, r=r):
            return ghosts[side, NG - 1, ch, pl.ds(start + r, SUB), :]

        moved = [moments([load(i, q, r) for i in range(Q)]) for q in qs]
        density = [moved[q][0] for q in qs]
        if density_of is not None:
            density = [density_of(q, r, density[q]) for q in qs]
        p = [1.0 - jnp.exp(-density[q]) for q in qs]
        shift_y, shift_z = fine_shifts(ch_count, k_count, ghost)
        tx, dy, dz, gy, gz = gradient_parts(p, shift_y, shift_z)
        for q in qs:
            values = (tx[q], dy[q], dz[q], gy[q], gz[q], p[q], density[q], *moved[q][1])
            for n, v in enumerate(values):
                parts[n, q, pl.ds(PAD + r, SUB), :] = v
    for chunk in range(chunks):
        r = chunk * SUB

        def ghost(side, which, ch, r=r):
            place = (UP if side == 0 else DOWN).index(which)
            return ghosts[side, place, ch, pl.ds(start + r, SUB), :]

        shift_y, shift_z = fine_shifts(ch_count, k_count, ghost)
        streams = []
        for q in qs:
            low = [parts[n, q, pl.ds(PAD + r - 1, SUB), :] for n in range(3)]
            high = [parts[n, q, pl.ds(PAD + r + 1, SUB), :] for n in range(3)]
            gy, gz, p, rho, mx, my, mz = (
                parts[n, q, pl.ds(PAD + r, SUB), :] for n in range(3, 10)
            )
            pull = [high[0] - low[0], gy + (high[1] + low[1]), gz + (high[2] + low[2])]
            flux = flux_of((mx, my, mz), p, pull, FINE_TAU)
            streams.append(balances(rho, flux, 1.0 / FINE_TAU))
        for i in range(Q):
            cx, cy, cz = VELOCITIES[i]
            post = []
            for q in qs:
                _, balance = next(streams[q])
                post.append(load(i, q, r) * (1.0 - 1.0 / FINE_TAU) + balance)
            if cy:
                post = shift_y(post, cy, i)
            if cz:
                post = shift_z(post, cz)
            for q in qs:
                store(i, q, r, cx, post[q])


CROSS = 5
FROM_DENSITY = Q
FROM_ENTER = Q + 1
FROM_PARTIAL = Q + 1 + CROSS
SENT = Q + 2 + CROSS


def edge_rows(nq):
    return SENT * nq + PLANES * (HALO // 2)


def sent_rows(nq):
    return -(-edge_rows(nq) // SUB) * SUB


def parts_of(count, pieces):
    cuts = [count * n // pieces for n in range(pieces + 1)]
    return list(zip(cuts[:-1], cuts[1:]))


def along(c):
    return [i for i in range(Q) if VELOCITIES[i][0] == c]


def restrict_body(ch_count, k_count, own, low, high):
    nq = ch_count * k_count

    def restricted(i, q, half):
        return own[pl.ds(i * (B * nq) + half * nq + q, SUB, stride=2 * nq), :]

    for side, out in enumerate((low, high)):
        for n, plane in enumerate(pack(restricted, ch_count, k_count, side)):
            out[n] = plane


def send_body(ch_count, k_count, own, ghosts, low, to_left, to_right, rim, moved, parts):
    nq = ch_count * k_count
    per = B * nq
    edge = HALO // 2

    for i in range(Q):
        for q in range(nq):
            rim[i, q, pl.ds(0, HALO), :] = own[pl.ds(i * per + q, HALO, stride=nq), :]
            rim[i, q, pl.ds(HALO, HALO), :] = own[
                pl.ds(i * per + (B - HALO) * nq + q, HALO, stride=nq), :
            ]

    def load(i, q, r):
        return rim[i, q]

    def store(i, q, r, cx, v):
        moved[i, q, pl.ds(PAD + cx, SUB), :] = v

    substep(load, store, ghosts, 0, parts, ch_count, k_count, 1)

    for c, out, outer in ((1, to_right, B - 1), (-1, to_left, 0)):
        first = PAD + (SUB - 1 if c > 0 else 0)
        second = first - c
        for i in range(Q):
            out[pl.ds(i * nq, nq), :] = own[pl.ds(i * per + outer * nq, nq), :]
        for q in range(nq):
            out[pl.ds(FROM_DENSITY * nq + q, 1), :] = parts[6, q, pl.ds(second, 1), :]
            for n, i in enumerate(along(c)):
                out[pl.ds((FROM_ENTER + n) * nq + q, 1), :] = moved[i, q, pl.ds(first, 1), :]
            total = None
            for i in along(0) + along(c):
                v = moved[i, q, pl.ds(second, 1), :]
                total = v if total is None else total + v
            out[pl.ds(FROM_PARTIAL * nq + q, 1), :] = total
        for n in range(PLANES):
            x = SUB - edge if c > 0 else 0
            out[pl.ds(SENT * nq + n * edge, edge), :] = low[n, pl.ds(x, edge), :]
        spare = sent_rows(nq) - edge_rows(nq)
        if spare:
            out[pl.ds(edge_rows(nq), spare), :] = jnp.zeros((spare, LANES), jnp.float32)


def inner_body(ch_count, k_count, own, ghosts, out, parts):
    nq = ch_count * k_count

    def load(i, q, r):
        return own[pl.ds(i * (B * nq) + r * nq + q, SUB, stride=nq), :]

    def store(i, q, r, cx, v):
        out[i, q, pl.ds(PAD + r + cx, SUB), :] = v

    substep(load, store, ghosts, HALO, parts, ch_count, k_count, B // SUB)


def fine_body(
    ch_count, k_count, own, left, right, inner, ghosts, rim_ghosts, out, rim, half, third, parts, held, sems
):
    nq = ch_count * k_count
    per = B * nq
    row = lax.broadcasted_iota(jnp.int32, (SUB, LANES), 0)
    origin = PAD + HALO

    layers = Q * nq
    rim[pl.ds(1, layers, stride=SUB), :] = left[pl.ds(0, layers), :]
    rim[pl.ds(6, layers, stride=SUB), :] = right[pl.ds(0, layers), :]
    for i in range(Q):
        for sub, x in ((2, 0), (3, 1), (4, B - 2), (5, B - 1)):
            rim[pl.ds(i * (nq * SUB) + sub, nq, stride=SUB), :] = own[
                pl.ds(i * per + x * nq, nq), :
            ]

    def spread(ref, plane, q):
        return jnp.broadcast_to(ref[pl.ds(plane * nq + q, 1), :], (SUB, LANES))

    def load_rim(i, q, r):
        return rim[pl.ds((i * nq + q) * SUB, SUB), :]

    def rim_density(q, r, density):
        density = jnp.where(row == 0, spread(left, FROM_DENSITY, q), density)
        return jnp.where(row == SUB - 1, spread(right, FROM_DENSITY, q), density)

    outgoing = {(c, q): None for c in (-1, 1) for q in range(nq)}

    def store_rim(i, q, r, cx, v):
        half[i, q, pl.ds(origin - 2 + cx, SUB), :] = v
        half[i, q, pl.ds(origin + B - 6 + cx, SUB), :] = v
        if cx:
            seen = outgoing[cx, q]
            outgoing[cx, q] = v if seen is None else seen + v

    substep(load_rim, store_rim, rim_ghosts, 0, parts, ch_count, k_count, 1, rim_density)
    for i in range(Q):
        cx = VELOCITIES[i][0]
        for q in range(nq):
            half[i, q, pl.ds(origin + 1 + cx, B - 2), :] = inner[i, q, pl.ds(PAD + 1 + cx, B - 2), :]
            if cx:
                ref = left if cx > 0 else right
                at = origin - 1 if cx > 0 else origin + B
                place = FROM_ENTER + along(cx).index(i)
                half[i, q, pl.ds(at, 1), :] = ref[pl.ds(place * nq + q, 1), :]

    def load(i, q, r):
        return half[i, q, pl.ds(PAD + r, SUB), :]

    def store(i, q, r, cx, v):
        third[i, q, pl.ds(PAD + r + cx, SUB), :] = v

    chunks = (B + 2 * HALO) // SUB

    def density_of(q, r, density):
        if r == 0:
            value = spread(left, FROM_PARTIAL, q) + pltpu.roll(outgoing[-1, q], 1, 0)
            return jnp.where(row == HALO - 2, value, density)
        if r == (chunks - 1) * SUB:
            value = spread(right, FROM_PARTIAL, q) + pltpu.roll(outgoing[1, q], SUB - 1, 0)
            return jnp.where(row == SUB - HALO + 1, value, density)
        return density

    substep(load, store, ghosts, 0, parts, ch_count, k_count, chunks, density_of)

    copies = []
    for n, (i0, i1) in enumerate(parts_of(Q, PIECES)):
        for i in range(i0, i1):
            for q in range(nq):
                held[pl.ds(i * per + q, B, stride=nq), :] = third[i, q, pl.ds(origin, B), :]
        part = pl.ds(i0 * per, (i1 - i0) * per)
        copies.append(pltpu.make_async_copy(held.at[part], out.at[part], sems.at[n]))
        copies[-1].start()
    for copy in copies:
        copy.wait()


def fine_ghost_body(ch_count, rows, layers, spread, out, send_ghosts, rim_ghosts, wide):
    for side in range(2):
        wide[...] = jnp.dot(
            layers[side],
            spread[...],
            precision=lax.Precision.HIGHEST,
            preferred_element_type=jnp.float32,
        )
        wanted = UP if side == 0 else DOWN
        for ch in range(ch_count):
            for r in range(0, rows, SUB):
                f = [
                    wide[pl.ds(i * rows + r, SUB), pl.ds(ch * LANES, LANES)] for i in range(Q)
                ]
                potential, found = rescaled(f, TO_FINE, wanted)
                for n, i in enumerate(wanted):
                    out[side, n, ch, pl.ds(r, SUB), :] = found[i]
                out[side, NG - 1, ch, pl.ds(r, SUB), :] = potential
            for n in range(NG):
                for ref, lower, upper in (
                    (send_ghosts, HALO, rows - 2 * HALO),
                    (rim_ghosts, 2, rows - HALO - 2),
                ):
                    ref[side, n, ch, pl.ds(0, HALO), :] = out[side, n, ch, pl.ds(lower, HALO), :]
                    ref[side, n, ch, pl.ds(HALO, HALO), :] = out[
                        side, n, ch, pl.ds(upper, HALO), :
                    ]


GROUP = 16
STEP = 32
PLANES = -(-Q // GROUP)


def pack(load, ch_count, k_count, side):
    lane = lax.broadcasted_iota(jnp.int32, (SUB, LANES), 1)
    offset = B - 2 if side == 0 else 0
    kept = lane % STEP == offset
    k = k_count - 1 if side == 0 else 0
    planes = [None] * PLANES
    for i in range(Q):
        for ch in range(ch_count):
            q = ch * k_count + k
            v = load(i, q, 0) + load(i, q, 1)
            v = v + pltpu.roll(v, LANES - 1, 1)
            v = v + pltpu.roll(v, LANES - B, 1)
            v = jnp.where(kept, v, 0.0)
            shift = (2 * (i % GROUP) + ch - offset) % LANES
            if shift:
                v = pltpu.roll(v, shift, 1)
            n = i // GROUP
            planes[n] = v if planes[n] is None else planes[n] + v
    return planes


def coarse_body(planes, state, out, packed, near, parts, out_pad):
    lane = lax.broadcasted_iota(jnp.int32, (SUB, LANES), 1)

    def shift_y(v, c, which):
        return [pltpu.roll(v[0], 1 if c > 0 else LANES - 1, 1)]

    def shift_z(v, c):
        return [pltpu.roll(v[0], 1 if c > 0 else SUB - 1, 0)]

    def prepare(x, carry):
        density, momentum = moments([state[i, x] for i in range(Q)])
        p = 1.0 - jnp.exp(-density)
        values = gradient_parts([p], shift_y, shift_z)
        values = [v[0] for v in values] + [p, density, *momentum]
        for n, v in enumerate(values):
            parts[n, x] = v
        return carry

    lax.fori_loop(0, planes, prepare, 0, unroll=2)

    inner = planes - HALO
    base = HALO // 2

    def update(x, carry):
        lower = [parts[n, x - 1] for n in range(3)]
        upper = [parts[n, x + 1] for n in range(3)]
        gy, gz, p, rho, mx, my, mz = (parts[n, x] for n in range(3, 10))
        pull = [upper[0] - lower[0], gy + (upper[1] + lower[1]), gz + (upper[2] + lower[2])]
        flux = flux_of((mx, my, mz), p, pull, COARSE_TAU)
        for i, balance in balances(rho, flux, 1.0 / COARSE_TAU):
            cx, cy, cz = VELOCITIES[i]
            post = [state[i, x] * (1.0 - 1.0 / COARSE_TAU) + balance]
            if cy:
                post = shift_y(post, cy, i)
            if cz:
                post = shift_z(post, cz)
            inside = x + cx - base
            spare = jnp.where((inside >= 0) & (inside < inner), inside, inner)
            out_pad[i, spare] = post[0]
        return carry

    lax.fori_loop(base - 1, base + inner + 1, update, 0, unroll=2)
    out[...] = out_pad[:, :inner]

    def gather(i, carry):
        total = jnp.zeros((SUB, LANES), jnp.float32)
        for x in range(planes):
            here = (lane == 2 * x + 1) | (lane == 2 * x + 2)
            total = jnp.where(here, pltpu.roll(state[i, x], 2 * x + 2, 1), total)
        packed[i] = total
        return carry

    lax.fori_loop(0, Q, gather, 0)
    total = jnp.zeros((SUB, LANES), jnp.float32)
    for x in range(planes):
        p = parts[5, x]
        total = jnp.where(lane == 2 * x + 2, pltpu.roll(p, 2 * x + 1, 1), total)
        total = jnp.where(lane == 2 * x + 1, pltpu.roll(p, 2 * x + 3, 1), total)
    near[...] = total


def edges_body(
    ch_count, k_count, planes, left, right, low, high, high_left, high_right, packed, near, step,
    out, rows, columns, ghost, held, sems,
):
    nq = ch_count * k_count
    edge = HALO // 2
    inner = planes - HALO
    lane = lax.broadcasted_iota(jnp.int32, (SUB, LANES), 1)
    sided = lane % 2 == 0

    for n in range(PLANES):
        own_x = 2 * edge
        rows[n, pl.ds(2 + own_x, inner, stride=2), :] = low[n]
        beside = SENT * nq + n * edge
        rows[n, pl.ds(2, edge, stride=2), :] = left[pl.ds(beside, edge), :]
        rows[n, pl.ds(2 + 2 * (edge + inner), edge, stride=2), :] = right[
            pl.ds(beside, edge), :
        ]
        rows[n, pl.ds(1 + own_x, inner, stride=2), :] = high[n]
        rows[n, pl.ds(1, edge, stride=2), :] = high_left[n, pl.ds(inner - edge, edge), :]
        rows[n, pl.ds(1 + 2 * (edge + inner), edge, stride=2), :] = high_right[
            n, pl.ds(0, edge), :
        ]
        columns[n, :, pl.ds(0, STEP)] = rows[n, pl.ds(0, STEP), :].T
    per = LANES // STEP
    for i in range(Q):
        for ch in range(ch_count):
            ghost[i, pl.ds(ch * per, per), :] = (
                0.125 * columns[i // GROUP, pl.ds(2 * (i % GROUP) + ch, per, stride=STEP), :]
            )

    beyond, entering = rescaled([ghost[i] for i in range(Q)], TO_COARSE, UP + DOWN)
    density, momentum = moments([packed[i] for i in range(Q)])
    p = 1.0 - jnp.exp(-density)
    inside = near[...]
    above = jnp.where(sided, inside, beyond)
    below = jnp.where(sided, beyond, inside)

    def shift_y(v, c, which):
        return [below if c > 0 else above]

    def shift_z(v, c):
        return [pltpu.roll(v[0], 1 if c > 0 else SUB - 1, 0)]

    def shift_x(v, c):
        return pltpu.roll(v, 2 if c > 0 else LANES - 2, 1) if c else v

    tx, dy, dz, gy, gz = (v[0] for v in gradient_parts([p], shift_y, shift_z))
    pull = [
        shift_x(tx, -1) - shift_x(tx, 1),
        gy + (shift_x(dy, -1) + shift_x(dy, 1)),
        gz + (shift_x(dz, -1) + shift_x(dz, 1)),
    ]
    flux = flux_of(momentum, p, pull, COARSE_TAU)
    copies = []
    for i, balance in balances(density, flux, 1.0 / COARSE_TAU):
        cx, cy, cz = VELOCITIES[i]
        v = packed[i] * (1.0 - 1.0 / COARSE_TAU) + balance
        if cy > 0:
            v = jnp.where(sided, entering[i], pltpu.roll(v, 1, 1))
            touched = lane < 2
        elif cy < 0:
            v = jnp.where(sided, pltpu.roll(v, LANES - 1, 1), entering[i])
            touched = lane >= LANES - 2
        else:
            touched = (lane == 0) | (lane == LANES - 1)
        v = shift_x(v, cx)
        if cz:
            v = shift_z([v], cz)[0]
        for x in range(inner):
            column = pltpu.roll(v, LANES - (2 * (x + edge) + 2), 1)
            held[i, x] = jnp.where(touched, column, step[i, x])
        for n, (i0, i1) in enumerate(parts_of(Q, PIECES)):
            if i == i1 - 1:
                part = pl.ds(i0, i1 - i0)
                copies.append(pltpu.make_async_copy(held.at[part], out.at[part], sems.at[n]))
                copies[-1].start()
    for copy in copies:
        copy.wait()


def ring(count, step):
    return [(i, (i + step) % count) for i in range(count)]


def slab_pairs(n_grp, n_wide, up, across):
    return [
        (g * n_wide + w, (g + across) % n_grp * n_wide + (w + up) % n_wide)
        for g in range(n_grp)
        for w in range(n_wide)
    ]


def local(fine_pop, coarse_pop, new_slot):
    k_count, q_count, cells = fine_pop.shape
    blocks = new_slot.shape[0]
    devices = blocks // k_count
    tiles = cells // LANES
    ch_count = tiles // B
    nq = ch_count * k_count
    axes = ("grp", "wide")
    n_grp, n_wide = lax.axis_size("grp"), lax.axis_size("wide")
    _, cx, cz, cy = coarse_pop.shape
    planes = cx + HALO
    fine_rows = B + 2 * HALO

    rows = pl.cdiv(Q * tiles, devices)
    pieces = fine_pop.reshape(k_count, Q, tiles, LANES)
    pieces = with_layout_constraint(pieces, Layout(major_to_minor=(1, 2, 0, 3)))
    pieces = pieces.transpose(1, 2, 0, 3)
    pieces = pieces.reshape(Q * tiles, k_count, LANES)
    if rows * devices != Q * tiles:
        pieces = jnp.pad(pieces, ((0, rows * devices - Q * tiles), (0, 0), (0, 0)))
    pieces = pieces.reshape(devices, rows, k_count, LANES)
    spread = lax.all_to_all(pieces, axes, 0, 0, tiled=True)
    edge = HALO // 2
    coarse_left = lax.ppermute(coarse_pop[:, cx - edge :], "grp", ring(n_grp, 1))
    coarse_right = lax.ppermute(coarse_pop[:, :edge], "grp", ring(n_grp, -1))
    last = coarse_pop[..., -1]
    below = []
    for part, across in ((last[:, cx - edge :], 1), (last, 0), (last[:, :edge], -1)):
        below.append(lax.ppermute(part, axes, slab_pairs(n_grp, n_wide, 1, across)))
    total = devices * rows * k_count
    regroup = call(
        functools.partial(regroup_body, blocks, k_count, rows),
        f32(total, LANES),
        [SMEM, VMEM],
        moved=8 * total * LANES,
    )
    targets = rows * new_slot - (rows - 1) * (new_slot % k_count)
    outgoing = regroup(targets, spread.reshape(total, LANES))
    arrived = lax.all_to_all(
        outgoing.reshape(devices, rows, k_count, LANES), axes, 0, 0, tiled=True
    )
    coarse = jnp.concatenate([coarse_left, coarse_pop, coarse_right], axis=1)
    below = jnp.concatenate(below, axis=1)
    layers = jnp.repeat(jnp.stack([below, coarse[..., 0]]), 2, axis=2)
    layers = layers.reshape(2, Q * fine_rows, cz)
    lane = jnp.arange(ch_count * LANES) // (2 * B)
    one_hot = (jnp.arange(cz)[:, None] == lane[None, :]).astype(jnp.float32)
    fine_ghosts, send_ghosts, rim_ghosts = call(
        functools.partial(fine_ghost_body, ch_count, fine_rows),
        [f32(2, NG, ch_count, n, LANES) for n in (fine_rows, SUB, SUB)],
        [VMEM, VMEM],
        [pltpu.VMEM((Q * fine_rows, ch_count * LANES), jnp.float32)],
    )(layers, one_hot)
    coarse_step, packed, near = call(
        functools.partial(coarse_body, planes),
        [f32(Q, cx, cz, cy), f32(Q, SUB, LANES), f32(SUB, LANES)],
        [VMEM],
        [
            pltpu.VMEM((10, planes, SUB, LANES), jnp.float32),
            pltpu.VMEM((Q, cx + 1, SUB, LANES), jnp.float32),
        ],
        flops=10**7,
    )(coarse)
    hidden = (fine_ghosts, send_ghosts, rim_ghosts, coarse_step, packed, near)
    arrived, hidden = lax.optimization_barrier((arrived, hidden))
    fine_ghosts, send_ghosts, rim_ghosts, coarse_step, packed, near = hidden
    own = arrived.reshape(total, LANES)[: Q * tiles * k_count]

    padded = PAD + fine_rows + PAD
    low, first = call(
        functools.partial(restrict_body, ch_count, k_count),
        [f32(PLANES, SUB, LANES)] * 2,
        [VMEM],
    )(own)
    to_left, to_right = call(
        functools.partial(send_body, ch_count, k_count),
        [f32(sent_rows(nq), LANES)] * 2,
        [VMEM] * 3,
        [
            pltpu.VMEM((Q, nq, SUB, LANES), jnp.float32),
            pltpu.VMEM((Q, nq, 3 * PAD, LANES), jnp.float32),
            pltpu.VMEM((10, nq, 3 * PAD, LANES), jnp.float32),
        ],
    )(own, send_ghosts, low)
    left = lax.ppermute(to_right, "grp", ring(n_grp, 1))
    right = lax.ppermute(to_left, "grp", ring(n_grp, -1))
    inner = call(
        functools.partial(inner_body, ch_count, k_count),
        f32(Q, nq, PAD + B + PAD, LANES),
        [VMEM] * 2,
        [pltpu.VMEM((10, nq, PAD + B + PAD, LANES), jnp.float32)],
        flops=10**7,
    )(own, fine_ghosts)
    highs = []
    for across in (0, 1, -1):
        highs.append(lax.ppermute(first, axes, slab_pairs(n_grp, n_wide, -1, across)))

    fine = call(
        functools.partial(fine_body, ch_count, k_count),
        f32(Q * B * nq, LANES),
        [VMEM] * 6,
        [
            pltpu.VMEM((Q * nq * SUB, LANES), jnp.float32),
            pltpu.VMEM((Q, nq, padded, LANES), jnp.float32),
            pltpu.VMEM((Q, nq, padded, LANES), jnp.float32),
            pltpu.VMEM((10, nq, padded, LANES), jnp.float32),
            pltpu.VMEM((Q * B * nq, LANES), jnp.float32),
            pltpu.SemaphoreType.DMA((PIECES,)),
        ],
        flops=10**7,
        place=HBM,
    )(own, left, right, inner, fine_ghosts, rim_ghosts)

    coarse_out = call(
        functools.partial(edges_body, ch_count, k_count, planes),
        f32(Q, cx, cz, cy),
        [VMEM] * 9,
        [
            pltpu.VMEM((PLANES, LANES, LANES), jnp.float32),
            pltpu.VMEM((PLANES, LANES, LANES), jnp.float32),
            pltpu.VMEM((Q, SUB, LANES), jnp.float32),
            pltpu.VMEM((Q, cx, cz, cy), jnp.float32),
            pltpu.SemaphoreType.DMA((PIECES,)),
        ],
        place=HBM,
    )(left, right, low, *highs, packed, near, coarse_step)

    fine_out = fine.reshape(Q, tiles, k_count, LANES).transpose(2, 0, 1, 3)
    fine_out = fine_out.reshape(k_count, q_count, cells)
    return fine_out, coarse_out


def solution(mesh):
    return jax.shard_map(
        local,
        mesh=mesh,
        in_specs=(P(("grp", "wide"), None, None), P(None, "grp", None, "wide"), P()),
        out_specs=(P(("grp", "wide"), None, None), P(None, "grp", None, "wide")),
        check_vma=False,
    )
```

```python
import functools

import jax
import jax.numpy as jnp
from jax import lax
from jax.experimental import pallas as pl
from jax.experimental.layout import Layout, with_layout_constraint
from jax.experimental.pallas import tpu as pltpu
from jax.sharding import PartitionSpec as P


B = 16
LANES = 128
SUB = 8
HALO = 4
PAD = 8
GRANT = 24 << 20
PIECES = 8

VELOCITIES = (
    (0, 0, 0),
    (1, 0, 0),
    (-1, 0, 0),
    (0, 1, 0),
    (0, -1, 0),
    (0, 0, 1),
    (0, 0, -1),
    (1, 1, 0),
    (-1, -1, 0),
    (1, -1, 0),
    (-1, 1, 0),
    (1, 0, 1),
    (-1, 0, -1),
    (1, 0, -1),
    (-1, 0, 1),
    (0, 1, 1),
    (0, -1, -1),
    (0, 1, -1),
    (0, -1, 1),
)
Q = len(VELOCITIES)
WEIGHTS = (1.0 / 3.0,) + (1.0 / 18.0,) * 6 + (1.0 / 36.0,) * 12
W_DIAG = WEIGHTS[7]
COUPLING = -5.0
FINE_TAU = 1.1
COARSE_TAU = 0.8
TO_COARSE = 2.0 * COARSE_TAU / FINE_TAU
TO_FINE = FINE_TAU / (2.0 * COARSE_TAU)
UP = tuple(i for i in range(Q) if VELOCITIES[i][1] == 1)
DOWN = tuple(i for i in range(Q) if VELOCITIES[i][1] == -1)
NG = len(UP) + 1

VMEM = pl.BlockSpec(memory_space=pltpu.VMEM)
SMEM = pl.BlockSpec(memory_space=pltpu.SMEM)
HBM = pl.BlockSpec(memory_space=pl.ANY)


def call(body, outs, specs, scratch=(), flops=10**6, moved=10**6, place=VMEM):
    return pl.pallas_call(
        body,
        out_shape=outs,
        in_specs=specs,
        out_specs=jax.tree.map(lambda _: place, outs),
        scratch_shapes=list(scratch),
        cost_estimate=pl.CostEstimate(flops=flops, bytes_accessed=moved, transcendentals=0),
        compiler_params=pltpu.CompilerParams(vmem_limit_bytes=GRANT),
    )


def f32(*shape):
    return jax.ShapeDtypeStruct(shape, jnp.float32)


def moments(f):
    density = f[0]
    momentum = [None, None, None]
    for i in range(1, Q, 2):
        density = density + (f[i] + f[i + 1])
        odd = f[i] - f[i + 1]
        for j in range(3):
            c = VELOCITIES[i][j]
            if c:
                term = odd if c > 0 else -odd
                if momentum[j] is None:
                    momentum[j] = term
                else:
                    momentum[j] = momentum[j] + odd if c > 0 else momentum[j] - odd
    return density, momentum


def balances(density, flux, scale):
    w = density * (W_DIAG * scale)
    half = 1.5 / density
    v = [x * half for x in flux]
    g = [x * (3.0 * W_DIAG * scale) for x in flux]
    g2 = [x + x for x in g]
    h = [g[j] * v[j] for j in range(3)]
    total = h[0] + h[1] + h[2]
    base = w - total * (1.0 / 3.0)
    base2 = base + base
    yield 0, base2 * (0.5 * WEIGHTS[0] / W_DIAG)
    for j in range(3):
        even = base2 + (h[j] + h[j])
        yield 2 * j + 1, even + g2[j]
        yield 2 * j + 2, even - g2[j]
    all_h = base + total
    i = 7
    for a, b, c in ((0, 1, 2), (0, 2, 1), (1, 2, 0)):
        even = all_h - h[c]
        cross = g2[a] * v[b]
        for sign in (1, -1):
            side = even + cross if sign > 0 else even - cross
            odd = g[a] + g[b] if sign > 0 else g[a] - g[b]
            yield i, side + odd
            yield i + 1, side - odd
            i += 2


def rescaled(f, factor, wanted):
    density, momentum = moments(f)
    found = {}
    for i, balance in balances(density, momentum, 1.0):
        if i in wanted:
            found[i] = balance + factor * (f[i] - balance)
    return 1.0 - jnp.exp(-density), found


def gradient_parts(p, shift_y, shift_z):
    above = shift_y(p, -1, "p")
    below = shift_y(p, 1, "p")
    front = shift_z(p, -1)
    back = shift_z(p, 1)
    n = range(len(p))
    dy = [above[q] - below[q] for q in n]
    dz = [front[q] - back[q] for q in n]
    mixed = [(p[q] + p[q]) + (above[q] + below[q]) for q in n]
    tx = [mixed[q] + (front[q] + back[q]) for q in n]
    mixed_front = shift_z(mixed, -1)
    mixed_back = shift_z(mixed, 1)
    dy_front = shift_z(dy, -1)
    dy_back = shift_z(dy, 1)
    gy = [(dy[q] + dy[q]) + (dy_front[q] + dy_back[q]) for q in n]
    gz = [mixed_front[q] - mixed_back[q] for q in n]
    return tx, dy, dz, gy, gz


def flux_of(momentum, potential, pull, tau):
    force = (-tau * COUPLING * W_DIAG) * potential
    return [momentum[j] + force * pull[j] for j in range(3)]


def regroup_body(blocks, k_blocks, rows, target_ref, in_ref, out_ref):
    for b in range(blocks):
        source = (b // k_blocks) * (rows * k_blocks) + b % k_blocks
        out_ref[pl.ds(target_ref[b], rows, stride=k_blocks), :] = in_ref[
            pl.ds(source, rows, stride=k_blocks), :
        ]


def lane_ids():
    lane = lax.broadcasted_iota(jnp.int32, (SUB, LANES), 1)
    return lane % B, lane // B


def fine_shifts(ch_count, k_count, ghost):
    y, z = lane_ids()
    first_y, last_y = y == 0, y == B - 1
    first_z, last_z = z == 0, z == LANES // B - 1

    def shift_y(v, c, which):
        out = []
        for ch in range(ch_count):
            for k in range(k_count):
                q = ch * k_count + k
                if c > 0:
                    own = pltpu.roll(v[q], 1, 1)
                    carry = (
                        ghost(0, which, ch) if k == 0 else pltpu.roll(v[q - 1], LANES - (B - 1), 1)
                    )
                    out.append(jnp.where(first_y, carry, own))
                else:
                    own = pltpu.roll(v[q], LANES - 1, 1)
                    carry = (
                        ghost(1, which, ch)
                        if k == k_count - 1
                        else pltpu.roll(v[q + 1], B - 1, 1)
                    )
                    out.append(jnp.where(last_y, carry, own))
        return out

    def shift_z(v, c):
        rolled = [pltpu.roll(x, B if c > 0 else LANES - B, 1) for x in v]
        edge = first_z if c > 0 else last_z
        out = []
        for ch in range(ch_count):
            other = (ch - c) % ch_count
            for k in range(k_count):
                q = ch * k_count + k
                out.append(jnp.where(edge, rolled[other * k_count + k], rolled[q]))
        return out

    return shift_y, shift_z


def substep(load, store, ghosts, start, parts, ch_count, k_count, chunks, density_of=None):
    qs = range(ch_count * k_count)
    for chunk in range(chunks):
        r = chunk * SUB

        def ghost(side, which, ch, r=r):
            return ghosts[side, NG - 1, ch, pl.ds(start + r, SUB), :]

        moved = [moments([load(i, q, r) for i in range(Q)]) for q in qs]
        density = [moved[q][0] for q in qs]
        if density_of is not None:
            density = [density_of(q, r, density[q]) for q in qs]
        p = [1.0 - jnp.exp(-density[q]) for q in qs]
        shift_y, shift_z = fine_shifts(ch_count, k_count, ghost)
        tx, dy, dz, gy, gz = gradient_parts(p, shift_y, shift_z)
        for q in qs:
            values = (tx[q], dy[q], dz[q], gy[q], gz[q], p[q], density[q], *moved[q][1])
            for n, v in enumerate(values):
                parts[n, q, pl.ds(PAD + r, SUB), :] = v
    for chunk in range(chunks):
        r = chunk * SUB

        def ghost(side, which, ch, r=r):
            place = (UP if side == 0 else DOWN).index(which)
            return ghosts[side, place, ch, pl.ds(start + r, SUB), :]

        shift_y, shift_z = fine_shifts(ch_count, k_count, ghost)
        streams = []
        for q in qs:
            low = [parts[n, q, pl.ds(PAD + r - 1, SUB), :] for n in range(3)]
            high = [parts[n, q, pl.ds(PAD + r + 1, SUB), :] for n in range(3)]
            gy, gz, p, rho, mx, my, mz = (
                parts[n, q, pl.ds(PAD + r, SUB), :] for n in range(3, 10)
            )
            pull = [high[0] - low[0], gy + (high[1] + low[1]), gz + (high[2] + low[2])]
            flux = flux_of((mx, my, mz), p, pull, FINE_TAU)
            streams.append(balances(rho, flux, 1.0 / FINE_TAU))
        for i in range(Q):
            cx, cy, cz = VELOCITIES[i]
            post = []
            for q in qs:
                _, balance = next(streams[q])
                post.append(load(i, q, r) * (1.0 - 1.0 / FINE_TAU) + balance)
            if cy:
                post = shift_y(post, cy, i)
            if cz:
                post = shift_z(post, cz)
            for q in qs:
                store(i, q, r, cx, post[q])


CROSS = 5
FROM_DENSITY = Q
FROM_ENTER = Q + 1
FROM_PARTIAL = Q + 1 + CROSS
SENT = Q + 2 + CROSS


def edge_rows(nq):
    return SENT * nq + 2 * PLANES * (HALO // 2)


def sent_rows(nq):
    return -(-edge_rows(nq) // SUB) * SUB


def parts_of(count, pieces):
    cuts = [count * n // pieces for n in range(pieces + 1)]
    return list(zip(cuts[:-1], cuts[1:]))


def along(c):
    return [i for i in range(Q) if VELOCITIES[i][0] == c]


def restrict_body(ch_count, k_count, own, low, high):
    nq = ch_count * k_count

    def restricted(i, q, half):
        return own[pl.ds(i * (B * nq) + half * nq + q, SUB, stride=2 * nq), :]

    for side, out in enumerate((low, high)):
        for n, plane in enumerate(pack(restricted, ch_count, k_count, side)):
            out[n] = plane


def right_turn():
    return lax.axis_index("grp") % 2


def send_body(ch_count, k_count, own, ghosts, low, high, turn_0, turn_1, rim, moved, parts, sides):
    nq = ch_count * k_count
    per = B * nq
    edge = HALO // 2

    for i in range(Q):
        for q in range(nq):
            rim[i, q, pl.ds(0, HALO), :] = own[pl.ds(i * per + q, HALO, stride=nq), :]
            rim[i, q, pl.ds(HALO, HALO), :] = own[
                pl.ds(i * per + (B - HALO) * nq + q, HALO, stride=nq), :
            ]

    def load(i, q, r):
        return rim[i, q]

    def store(i, q, r, cx, v):
        moved[i, q, pl.ds(PAD + cx, SUB), :] = v

    substep(load, store, ghosts, 0, parts, ch_count, k_count, 1)

    right = right_turn()
    for c, out, outer in ((1, sides.at[right], B - 1), (-1, sides.at[1 - right], 0)):
        first = PAD + (SUB - 1 if c > 0 else 0)
        second = first - c
        for i in range(Q):
            out[pl.ds(i * nq, nq), :] = own[pl.ds(i * per + outer * nq, nq), :]
        for q in range(nq):
            out[pl.ds(FROM_DENSITY * nq + q, 1), :] = parts[6, q, pl.ds(second, 1), :]
            for n, i in enumerate(along(c)):
                out[pl.ds((FROM_ENTER + n) * nq + q, 1), :] = moved[i, q, pl.ds(first, 1), :]
            total = None
            for i in along(0) + along(c):
                v = moved[i, q, pl.ds(second, 1), :]
                total = v if total is None else total + v
            out[pl.ds(FROM_PARTIAL * nq + q, 1), :] = total
        x = SUB - edge if c > 0 else 0
        for place, ref in enumerate((low, high)):
            for n in range(PLANES):
                at = SENT * nq + (place * PLANES + n) * edge
                out[pl.ds(at, edge), :] = ref[n, pl.ds(x, edge), :]
        spare = sent_rows(nq) - edge_rows(nq)
        if spare:
            out[pl.ds(edge_rows(nq), spare), :] = jnp.zeros((spare, LANES), jnp.float32)
    turn_0[...] = sides[0]
    turn_1[...] = sides[1]


def inner_body(ch_count, k_count, own, ghosts, out, parts):
    nq = ch_count * k_count

    def load(i, q, r):
        return own[pl.ds(i * (B * nq) + r * nq + q, SUB, stride=nq), :]

    def store(i, q, r, cx, v):
        out[i, q, pl.ds(PAD + r + cx, SUB), :] = v

    substep(load, store, ghosts, HALO, parts, ch_count, k_count, B // SUB)


def fine_body(
    ch_count, k_count, own, turn_0, turn_1, inner, ghosts, rim_ghosts,
    out, rim, half, third, parts, held, sems, sides,
):
    nq = ch_count * k_count
    per = B * nq
    row = lax.broadcasted_iota(jnp.int32, (SUB, LANES), 0)
    origin = PAD + HALO
    sides[0] = turn_0[...]
    sides[1] = turn_1[...]
    left, right = sides.at[1 - right_turn()], sides.at[right_turn()]

    layers = Q * nq
    rim[pl.ds(1, layers, stride=SUB), :] = left[pl.ds(0, layers), :]
    rim[pl.ds(6, layers, stride=SUB), :] = right[pl.ds(0, layers), :]
    for i in range(Q):
        for sub, x in ((2, 0), (3, 1), (4, B - 2), (5, B - 1)):
            rim[pl.ds(i * (nq * SUB) + sub, nq, stride=SUB), :] = own[
                pl.ds(i * per + x * nq, nq), :
            ]

    def spread(ref, plane, q):
        return jnp.broadcast_to(ref[pl.ds(plane * nq + q, 1), :], (SUB, LANES))

    def load_rim(i, q, r):
        return rim[pl.ds((i * nq + q) * SUB, SUB), :]

    def rim_density(q, r, density):
        density = jnp.where(row == 0, spread(left, FROM_DENSITY, q), density)
        return jnp.where(row == SUB - 1, spread(right, FROM_DENSITY, q), density)

    outgoing = {(c, q): None for c in (-1, 1) for q in range(nq)}

    def store_rim(i, q, r, cx, v):
        half[i, q, pl.ds(origin - 2 + cx, SUB), :] = v
        half[i, q, pl.ds(origin + B - 6 + cx, SUB), :] = v
        if cx:
            seen = outgoing[cx, q]
            outgoing[cx, q] = v if seen is None else seen + v

    substep(load_rim, store_rim, rim_ghosts, 0, parts, ch_count, k_count, 1, rim_density)
    for i in range(Q):
        cx = VELOCITIES[i][0]
        for q in range(nq):
            half[i, q, pl.ds(origin + 1 + cx, B - 2), :] = inner[i, q, pl.ds(PAD + 1 + cx, B - 2), :]
            if cx:
                ref = left if cx > 0 else right
                at = origin - 1 if cx > 0 else origin + B
                place = FROM_ENTER + along(cx).index(i)
                half[i, q, pl.ds(at, 1), :] = ref[pl.ds(place * nq + q, 1), :]

    def load(i, q, r):
        return half[i, q, pl.ds(PAD + r, SUB), :]

    def store(i, q, r, cx, v):
        third[i, q, pl.ds(PAD + r + cx, SUB), :] = v

    chunks = (B + 2 * HALO) // SUB

    def density_of(q, r, density):
        if r == 0:
            value = spread(left, FROM_PARTIAL, q) + pltpu.roll(outgoing[-1, q], 1, 0)
            return jnp.where(row == HALO - 2, value, density)
        if r == (chunks - 1) * SUB:
            value = spread(right, FROM_PARTIAL, q) + pltpu.roll(outgoing[1, q], SUB - 1, 0)
            return jnp.where(row == SUB - HALO + 1, value, density)
        return density

    substep(load, store, ghosts, 0, parts, ch_count, k_count, chunks, density_of)

    copies = []
    for n, (i0, i1) in enumerate(parts_of(Q, PIECES)):
        for i in range(i0, i1):
            for q in range(nq):
                held[pl.ds(i * per + q, B, stride=nq), :] = third[i, q, pl.ds(origin, B), :]
        part = pl.ds(i0 * per, (i1 - i0) * per)
        copies.append(pltpu.make_async_copy(held.at[part], out.at[part], sems.at[n]))
        copies[-1].start()
    for copy in copies:
        copy.wait()


def fine_ghost_body(ch_count, rows, layers, spread, out, send_ghosts, rim_ghosts, wide):
    for side in range(2):
        wide[...] = jnp.dot(
            layers[side],
            spread[...],
            precision=lax.Precision.HIGHEST,
            preferred_element_type=jnp.float32,
        )
        wanted = UP if side == 0 else DOWN
        for ch in range(ch_count):
            for r in range(0, rows, SUB):
                f = [
                    wide[pl.ds(i * rows + r, SUB), pl.ds(ch * LANES, LANES)] for i in range(Q)
                ]
                potential, found = rescaled(f, TO_FINE, wanted)
                for n, i in enumerate(wanted):
                    out[side, n, ch, pl.ds(r, SUB), :] = found[i]
                out[side, NG - 1, ch, pl.ds(r, SUB), :] = potential
            for n in range(NG):
                for ref, lower, upper in (
                    (send_ghosts, HALO, rows - 2 * HALO),
                    (rim_ghosts, 2, rows - HALO - 2),
                ):
                    ref[side, n, ch, pl.ds(0, HALO), :] = out[side, n, ch, pl.ds(lower, HALO), :]
                    ref[side, n, ch, pl.ds(HALO, HALO), :] = out[
                        side, n, ch, pl.ds(upper, HALO), :
                    ]


GROUP = 16
STEP = 32
PLANES = -(-Q // GROUP)


def pack(load, ch_count, k_count, side):
    lane = lax.broadcasted_iota(jnp.int32, (SUB, LANES), 1)
    offset = B - 2 if side == 0 else 0
    kept = lane % STEP == offset
    k = k_count - 1 if side == 0 else 0
    planes = [None] * PLANES
    for i in range(Q):
        for ch in range(ch_count):
            q = ch * k_count + k
            v = load(i, q, 0) + load(i, q, 1)
            v = v + pltpu.roll(v, LANES - 1, 1)
            v = v + pltpu.roll(v, LANES - B, 1)
            v = jnp.where(kept, v, 0.0)
            shift = (2 * (i % GROUP) + ch - offset) % LANES
            if shift:
                v = pltpu.roll(v, shift, 1)
            n = i // GROUP
            planes[n] = v if planes[n] is None else planes[n] + v
    return planes


def coarse_body(planes, state, out, packed, near, parts, out_pad):
    lane = lax.broadcasted_iota(jnp.int32, (SUB, LANES), 1)

    def shift_y(v, c, which):
        return [pltpu.roll(v[0], 1 if c > 0 else LANES - 1, 1)]

    def shift_z(v, c):
        return [pltpu.roll(v[0], 1 if c > 0 else SUB - 1, 0)]

    def prepare(x, carry):
        density, momentum = moments([state[i, x] for i in range(Q)])
        p = 1.0 - jnp.exp(-density)
        values = gradient_parts([p], shift_y, shift_z)
        values = [v[0] for v in values] + [p, density, *momentum]
        for n, v in enumerate(values):
            parts[n, x] = v
        return carry

    lax.fori_loop(0, planes, prepare, 0, unroll=2)

    inner = planes - HALO
    base = HALO // 2

    def update(x, carry):
        lower = [parts[n, x - 1] for n in range(3)]
        upper = [parts[n, x + 1] for n in range(3)]
        gy, gz, p, rho, mx, my, mz = (parts[n, x] for n in range(3, 10))
        pull = [upper[0] - lower[0], gy + (upper[1] + lower[1]), gz + (upper[2] + lower[2])]
        flux = flux_of((mx, my, mz), p, pull, COARSE_TAU)
        for i, balance in balances(rho, flux, 1.0 / COARSE_TAU):
            cx, cy, cz = VELOCITIES[i]
            post = [state[i, x] * (1.0 - 1.0 / COARSE_TAU) + balance]
            if cy:
                post = shift_y(post, cy, i)
            if cz:
                post = shift_z(post, cz)
            inside = x + cx - base
            spare = jnp.where((inside >= 0) & (inside < inner), inside, inner)
            out_pad[i, spare] = post[0]
        return carry

    lax.fori_loop(base - 1, base + inner + 1, update, 0, unroll=2)
    out[...] = out_pad[:, :inner]

    def gather(i, carry):
        total = jnp.zeros((SUB, LANES), jnp.float32)
        for x in range(planes):
            here = (lane == 2 * x + 1) | (lane == 2 * x + 2)
            total = jnp.where(here, pltpu.roll(state[i, x], 2 * x + 2, 1), total)
        packed[i] = total
        return carry

    lax.fori_loop(0, Q, gather, 0)
    total = jnp.zeros((SUB, LANES), jnp.float32)
    for x in range(planes):
        p = parts[5, x]
        total = jnp.where(lane == 2 * x + 2, pltpu.roll(p, 2 * x + 1, 1), total)
        total = jnp.where(lane == 2 * x + 1, pltpu.roll(p, 2 * x + 3, 1), total)
    near[...] = total


def edges_body(
    ch_count, k_count, planes, turn_0, turn_1, low, high, packed, near, step,
    out, rows, columns, ghost, held, sems, sides,
):
    nq = ch_count * k_count
    edge = HALO // 2
    inner = planes - HALO
    lane = lax.broadcasted_iota(jnp.int32, (SUB, LANES), 1)
    sided = lane % 2 == 0
    tail = pl.ds(SENT * nq, PLANES * edge)
    sides[0] = turn_0[tail, :]
    sides[1] = turn_1[tail, :]
    left, right = sides.at[1 - right_turn()], sides.at[right_turn()]

    for n in range(PLANES):
        own_x = 2 * edge
        rows[n, pl.ds(2 + own_x, inner, stride=2), :] = low[n]
        beside = n * edge
        rows[n, pl.ds(2, edge, stride=2), :] = left[pl.ds(beside, edge), :]
        rows[n, pl.ds(2 + 2 * (edge + inner), edge, stride=2), :] = right[
            pl.ds(beside, edge), :
        ]
        rows[n, pl.ds(1 + own_x, inner, stride=2), :] = high[pl.ds(n * SUB, inner), :]
        turn = right_turn()
        for at, place in ((1, 1 - turn), (1 + 2 * (edge + inner), turn)):
            rows[n, pl.ds(at, edge, stride=2), :] = high[
                pl.ds(PLANES * SUB + (place * PLANES + n) * edge, edge), :
            ]
        columns[n, :, pl.ds(0, STEP)] = rows[n, pl.ds(0, STEP), :].T
    per = LANES // STEP
    for i in range(Q):
        for ch in range(ch_count):
            ghost[i, pl.ds(ch * per, per), :] = (
                0.125 * columns[i // GROUP, pl.ds(2 * (i % GROUP) + ch, per, stride=STEP), :]
            )

    beyond, entering = rescaled([ghost[i] for i in range(Q)], TO_COARSE, UP + DOWN)
    density, momentum = moments([packed[i] for i in range(Q)])
    p = 1.0 - jnp.exp(-density)
    inside = near[...]
    above = jnp.where(sided, inside, beyond)
    below = jnp.where(sided, beyond, inside)

    def shift_y(v, c, which):
        return [below if c > 0 else above]

    def shift_z(v, c):
        return [pltpu.roll(v[0], 1 if c > 0 else SUB - 1, 0)]

    def shift_x(v, c):
        return pltpu.roll(v, 2 if c > 0 else LANES - 2, 1) if c else v

    tx, dy, dz, gy, gz = (v[0] for v in gradient_parts([p], shift_y, shift_z))
    pull = [
        shift_x(tx, -1) - shift_x(tx, 1),
        gy + (shift_x(dy, -1) + shift_x(dy, 1)),
        gz + (shift_x(dz, -1) + shift_x(dz, 1)),
    ]
    flux = flux_of(momentum, p, pull, COARSE_TAU)
    copies = []
    for i, balance in balances(density, flux, 1.0 / COARSE_TAU):
        cx, cy, cz = VELOCITIES[i]
        v = packed[i] * (1.0 - 1.0 / COARSE_TAU) + balance
        if cy > 0:
            v = jnp.where(sided, entering[i], pltpu.roll(v, 1, 1))
            touched = lane < 2
        elif cy < 0:
            v = jnp.where(sided, pltpu.roll(v, LANES - 1, 1), entering[i])
            touched = lane >= LANES - 2
        else:
            touched = (lane == 0) | (lane == LANES - 1)
        v = shift_x(v, cx)
        if cz:
            v = shift_z([v], cz)[0]
        for x in range(inner):
            column = pltpu.roll(v, LANES - (2 * (x + edge) + 2), 1)
            held[i, x] = jnp.where(touched, column, step[i, x])
        for n, (i0, i1) in enumerate(parts_of(Q, PIECES)):
            if i == i1 - 1:
                part = pl.ds(i0, i1 - i0)
                copies.append(pltpu.make_async_copy(held.at[part], out.at[part], sems.at[n]))
                copies[-1].start()
    for copy in copies:
        copy.wait()


def ring(count, step):
    return [(i, (i + step) % count) for i in range(count)]


def slab_pairs(n_grp, n_wide, up, across):
    return [
        (g * n_wide + w, (g + across) % n_grp * n_wide + (w + up) % n_wide)
        for g in range(n_grp)
        for w in range(n_wide)
    ]


def local(fine_pop, coarse_pop, new_slot):
    k_count, q_count, cells = fine_pop.shape
    blocks = new_slot.shape[0]
    devices = blocks // k_count
    tiles = cells // LANES
    ch_count = tiles // B
    nq = ch_count * k_count
    axes = ("grp", "wide")
    n_grp, n_wide = lax.axis_size("grp"), lax.axis_size("wide")
    _, cx, cz, cy = coarse_pop.shape
    planes = cx + HALO
    fine_rows = B + 2 * HALO

    rows = pl.cdiv(Q * tiles, devices)
    pieces = fine_pop.reshape(k_count, Q, tiles, LANES)
    pieces = with_layout_constraint(pieces, Layout(major_to_minor=(1, 2, 0, 3)))
    pieces = pieces.transpose(1, 2, 0, 3)
    pieces = pieces.reshape(Q * tiles, k_count, LANES)
    if rows * devices != Q * tiles:
        pieces = jnp.pad(pieces, ((0, rows * devices - Q * tiles), (0, 0), (0, 0)))
    pieces = pieces.reshape(devices, rows, k_count, LANES)
    spread = lax.all_to_all(pieces, axes, 0, 0, tiled=True)
    edge = HALO // 2
    coarse_left = lax.ppermute(coarse_pop[:, cx - edge :], "grp", ring(n_grp, 1))
    coarse_right = lax.ppermute(coarse_pop[:, :edge], "grp", ring(n_grp, -1))
    last = coarse_pop[..., -1]
    below = []
    for part, across in ((last[:, cx - edge :], 1), (last, 0), (last[:, :edge], -1)):
        below.append(lax.ppermute(part, axes, slab_pairs(n_grp, n_wide, 1, across)))
    total = devices * rows * k_count
    regroup = call(
        functools.partial(regroup_body, blocks, k_count, rows),
        f32(total, LANES),
        [SMEM, VMEM],
        moved=8 * total * LANES,
    )
    targets = rows * new_slot - (rows - 1) * (new_slot % k_count)
    outgoing = regroup(targets, spread.reshape(total, LANES))
    arrived = lax.all_to_all(
        outgoing.reshape(devices, rows, k_count, LANES), axes, 0, 0, tiled=True
    )
    coarse = jnp.concatenate([coarse_left, coarse_pop, coarse_right], axis=1)
    below = jnp.concatenate(below, axis=1)
    layers = jnp.repeat(jnp.stack([below, coarse[..., 0]]), 2, axis=2)
    layers = layers.reshape(2, Q * fine_rows, cz)
    lane = jnp.arange(ch_count * LANES) // (2 * B)
    one_hot = (jnp.arange(cz)[:, None] == lane[None, :]).astype(jnp.float32)
    fine_ghosts, send_ghosts, rim_ghosts = call(
        functools.partial(fine_ghost_body, ch_count, fine_rows),
        [f32(2, NG, ch_count, n, LANES) for n in (fine_rows, SUB, SUB)],
        [VMEM, VMEM],
        [pltpu.VMEM((Q * fine_rows, ch_count * LANES), jnp.float32)],
    )(layers, one_hot)
    coarse_step, packed, near = call(
        functools.partial(coarse_body, planes),
        [f32(Q, cx, cz, cy), f32(Q, SUB, LANES), f32(SUB, LANES)],
        [VMEM],
        [
            pltpu.VMEM((10, planes, SUB, LANES), jnp.float32),
            pltpu.VMEM((Q, cx + 1, SUB, LANES), jnp.float32),
        ],
        flops=10**7,
    )(coarse)
    hidden = (fine_ghosts, send_ghosts, rim_ghosts, coarse_step, packed, near)
    arrived, hidden = lax.optimization_barrier((arrived, hidden))
    fine_ghosts, send_ghosts, rim_ghosts, coarse_step, packed, near = hidden
    own = arrived.reshape(total, LANES)[: Q * tiles * k_count]

    padded = PAD + fine_rows + PAD
    low, first = call(
        functools.partial(restrict_body, ch_count, k_count),
        [f32(PLANES, SUB, LANES)] * 2,
        [VMEM],
    )(own)
    turns = call(
        functools.partial(send_body, ch_count, k_count),
        [f32(sent_rows(nq), LANES)] * 2,
        [VMEM] * 4,
        [
            pltpu.VMEM((Q, nq, SUB, LANES), jnp.float32),
            pltpu.VMEM((Q, nq, 3 * PAD, LANES), jnp.float32),
            pltpu.VMEM((10, nq, 3 * PAD, LANES), jnp.float32),
            pltpu.VMEM((2, sent_rows(nq), LANES), jnp.float32),
        ],
    )(own, send_ghosts, low, first)
    assert n_grp % 2 == 0
    swaps = []
    for turn, values in enumerate(turns):
        ends = [((g + turn) % n_grp, (g + turn + 1) % n_grp) for g in range(0, n_grp, 2)]
        swaps.append(lax.ppermute(values, "grp", ends + [(j, i) for i, j in ends]))
    inner = call(
        functools.partial(inner_body, ch_count, k_count),
        f32(Q, nq, PAD + B + PAD, LANES),
        [VMEM] * 2,
        [pltpu.VMEM((10, nq, PAD + B + PAD, LANES), jnp.float32)],
        flops=10**7,
    )(own, fine_ghosts)
    tail = edge_rows(nq) - PLANES * edge
    widened = jnp.concatenate(
        [first.reshape(PLANES * SUB, LANES)]
        + [swap[tail : tail + PLANES * edge] for swap in swaps]
    )
    high = lax.ppermute(widened, "wide", ring(n_wide, -1))

    fine = call(
        functools.partial(fine_body, ch_count, k_count),
        f32(Q * B * nq, LANES),
        [VMEM] * 6,
        [
            pltpu.VMEM((Q * nq * SUB, LANES), jnp.float32),
            pltpu.VMEM((Q, nq, padded, LANES), jnp.float32),
            pltpu.VMEM((Q, nq, padded, LANES), jnp.float32),
            pltpu.VMEM((10, nq, padded, LANES), jnp.float32),
            pltpu.VMEM((Q * B * nq, LANES), jnp.float32),
            pltpu.SemaphoreType.DMA((PIECES,)),
            pltpu.VMEM((2, sent_rows(nq), LANES), jnp.float32),
        ],
        flops=10**7,
        place=HBM,
    )(own, *swaps, inner, fine_ghosts, rim_ghosts)

    coarse_out = call(
        functools.partial(edges_body, ch_count, k_count, planes),
        f32(Q, cx, cz, cy),
        [VMEM] * 7,
        [
            pltpu.VMEM((PLANES, LANES, LANES), jnp.float32),
            pltpu.VMEM((PLANES, LANES, LANES), jnp.float32),
            pltpu.VMEM((Q, SUB, LANES), jnp.float32),
            pltpu.VMEM((Q, cx, cz, cy), jnp.float32),
            pltpu.SemaphoreType.DMA((PIECES,)),
            pltpu.VMEM((2, PLANES * edge, LANES), jnp.float32),
        ],
        place=HBM,
    )(*swaps, low, high, packed, near, coarse_step)

    fine_out = fine.reshape(Q, tiles, k_count, LANES).transpose(2, 0, 1, 3)
    fine_out = fine_out.reshape(k_count, q_count, cells)
    return fine_out, coarse_out


def solution(mesh):
    return jax.shard_map(
        local,
        mesh=mesh,
        in_specs=(P(("grp", "wide"), None, None), P(None, "grp", None, "wide"), P()),
        out_specs=(P(("grp", "wide"), None, None), P(None, "grp", None, "wide")),
        check_vma=False,
    )
```

```python
import functools

import jax
import jax.numpy as jnp
from jax import lax
from jax.experimental import pallas as pl
from jax.experimental.layout import Layout, with_layout_constraint
from jax.experimental.pallas import tpu as pltpu
from jax.sharding import PartitionSpec as P


B = 16
LANES = 128
SUB = 8
HALO = 4
PAD = 8
GRANT = 24 << 20
PIECES = 8

VELOCITIES = (
    (0, 0, 0),
    (1, 0, 0),
    (-1, 0, 0),
    (0, 1, 0),
    (0, -1, 0),
    (0, 0, 1),
    (0, 0, -1),
    (1, 1, 0),
    (-1, -1, 0),
    (1, -1, 0),
    (-1, 1, 0),
    (1, 0, 1),
    (-1, 0, -1),
    (1, 0, -1),
    (-1, 0, 1),
    (0, 1, 1),
    (0, -1, -1),
    (0, 1, -1),
    (0, -1, 1),
)
Q = len(VELOCITIES)
WEIGHTS = (1.0 / 3.0,) + (1.0 / 18.0,) * 6 + (1.0 / 36.0,) * 12
W_DIAG = WEIGHTS[7]
COUPLING = -5.0
FINE_TAU = 1.1
COARSE_TAU = 0.8
TO_COARSE = 2.0 * COARSE_TAU / FINE_TAU
TO_FINE = FINE_TAU / (2.0 * COARSE_TAU)
UP = tuple(i for i in range(Q) if VELOCITIES[i][1] == 1)
DOWN = tuple(i for i in range(Q) if VELOCITIES[i][1] == -1)
NG = len(UP) + 1

VMEM = pl.BlockSpec(memory_space=pltpu.VMEM)
SMEM = pl.BlockSpec(memory_space=pltpu.SMEM)
HBM = pl.BlockSpec(memory_space=pl.ANY)


def call(body, outs, specs, scratch=(), flops=10**6, moved=10**6, place=VMEM):
    return pl.pallas_call(
        body,
        out_shape=outs,
        in_specs=specs,
        out_specs=jax.tree.map(lambda _: place, outs),
        scratch_shapes=list(scratch),
        cost_estimate=pl.CostEstimate(flops=flops, bytes_accessed=moved, transcendentals=0),
        compiler_params=pltpu.CompilerParams(vmem_limit_bytes=GRANT),
    )


def f32(*shape):
    return jax.ShapeDtypeStruct(shape, jnp.float32)


def moments(f):
    density = f[0]
    momentum = [None, None, None]
    for i in range(1, Q, 2):
        density = density + (f[i] + f[i + 1])
        odd = f[i] - f[i + 1]
        for j in range(3):
            c = VELOCITIES[i][j]
            if c:
                term = odd if c > 0 else -odd
                if momentum[j] is None:
                    momentum[j] = term
                else:
                    momentum[j] = momentum[j] + odd if c > 0 else momentum[j] - odd
    return density, momentum


def balances(density, flux, scale):
    w = density * (W_DIAG * scale)
    half = 1.5 / density
    v = [x * half for x in flux]
    g = [x * (3.0 * W_DIAG * scale) for x in flux]
    g2 = [x + x for x in g]
    h = [g[j] * v[j] for j in range(3)]
    total = h[0] + h[1] + h[2]
    base = w - total * (1.0 / 3.0)
    base2 = base + base
    yield 0, base2 * (0.5 * WEIGHTS[0] / W_DIAG)
    for j in range(3):
        even = base2 + (h[j] + h[j])
        yield 2 * j + 1, even + g2[j]
        yield 2 * j + 2, even - g2[j]
    all_h = base + total
    i = 7
    for a, b, c in ((0, 1, 2), (0, 2, 1), (1, 2, 0)):
        even = all_h - h[c]
        cross = g2[a] * v[b]
        for sign in (1, -1):
            side = even + cross if sign > 0 else even - cross
            odd = g[a] + g[b] if sign > 0 else g[a] - g[b]
            yield i, side + odd
            yield i + 1, side - odd
            i += 2


def rescaled(f, factor, wanted):
    density, momentum = moments(f)
    found = {}
    for i, balance in balances(density, momentum, 1.0):
        if i in wanted:
            found[i] = balance + factor * (f[i] - balance)
    return 1.0 - jnp.exp(-density), found


def gradient_parts(p, shift_y, shift_z):
    above = shift_y(p, -1, "p")
    below = shift_y(p, 1, "p")
    front = shift_z(p, -1)
    back = shift_z(p, 1)
    n = range(len(p))
    dy = [above[q] - below[q] for q in n]
    dz = [front[q] - back[q] for q in n]
    mixed = [(p[q] + p[q]) + (above[q] + below[q]) for q in n]
    tx = [mixed[q] + (front[q] + back[q]) for q in n]
    mixed_front = shift_z(mixed, -1)
    mixed_back = shift_z(mixed, 1)
    dy_front = shift_z(dy, -1)
    dy_back = shift_z(dy, 1)
    gy = [(dy[q] + dy[q]) + (dy_front[q] + dy_back[q]) for q in n]
    gz = [mixed_front[q] - mixed_back[q] for q in n]
    return tx, dy, dz, gy, gz


def flux_of(momentum, potential, pull, tau):
    force = (-tau * COUPLING * W_DIAG) * potential
    return [momentum[j] + force * pull[j] for j in range(3)]


def regroup_body(blocks, k_blocks, rows, target_ref, in_ref, out_ref):
    targets = target_ref[...]
    for b in range(blocks):
        source = (b // k_blocks) * (rows * k_blocks) + b % k_blocks
        out_ref[pl.ds(targets[0, b], rows, stride=k_blocks), :] = in_ref[
            pl.ds(source, rows, stride=k_blocks), :
        ]


def lane_ids():
    lane = lax.broadcasted_iota(jnp.int32, (SUB, LANES), 1)
    return lane % B, lane // B


def fine_shifts(ch_count, k_count, ghost):
    y, z = lane_ids()
    first_y, last_y = y == 0, y == B - 1
    first_z, last_z = z == 0, z == LANES // B - 1

    def shift_y(v, c, which):
        out = []
        for ch in range(ch_count):
            for k in range(k_count):
                q = ch * k_count + k
                if c > 0:
                    own = pltpu.roll(v[q], 1, 1)
                    carry = (
                        ghost(0, which, ch) if k == 0 else pltpu.roll(v[q - 1], LANES - (B - 1), 1)
                    )
                    out.append(jnp.where(first_y, carry, own))
                else:
                    own = pltpu.roll(v[q], LANES - 1, 1)
                    carry = (
                        ghost(1, which, ch)
                        if k == k_count - 1
                        else pltpu.roll(v[q + 1], B - 1, 1)
                    )
                    out.append(jnp.where(last_y, carry, own))
        return out

    def shift_z(v, c):
        rolled = [pltpu.roll(x, B if c > 0 else LANES - B, 1) for x in v]
        edge = first_z if c > 0 else last_z
        out = []
        for ch in range(ch_count):
            other = (ch - c) % ch_count
            for k in range(k_count):
                q = ch * k_count + k
                out.append(jnp.where(edge, rolled[other * k_count + k], rolled[q]))
        return out

    return shift_y, shift_z


def substep(load, store, ghosts, start, parts, ch_count, k_count, chunks, density_of=None):
    qs = range(ch_count * k_count)
    for chunk in range(chunks):
        r = chunk * SUB

        def ghost(side, which, ch, r=r):
            return ghosts[side, NG - 1, ch, pl.ds(start + r, SUB), :]

        moved = [moments([load(i, q, r) for i in range(Q)]) for q in qs]
        density = [moved[q][0] for q in qs]
        if density_of is not None:
            density = [density_of(q, r, density[q]) for q in qs]
        p = [1.0 - jnp.exp(-density[q]) for q in qs]
        shift_y, shift_z = fine_shifts(ch_count, k_count, ghost)
        tx, dy, dz, gy, gz = gradient_parts(p, shift_y, shift_z)
        for q in qs:
            values = (tx[q], dy[q], dz[q], gy[q], gz[q], p[q], density[q], *moved[q][1])
            for n, v in enumerate(values):
                parts[n, q, pl.ds(PAD + r, SUB), :] = v
    for chunk in range(chunks):
        r = chunk * SUB

        def ghost(side, which, ch, r=r):
            place = (UP if side == 0 else DOWN).index(which)
            return ghosts[side, place, ch, pl.ds(start + r, SUB), :]

        shift_y, shift_z = fine_shifts(ch_count, k_count, ghost)
        streams = []
        for q in qs:
            low = [parts[n, q, pl.ds(PAD + r - 1, SUB), :] for n in range(3)]
            high = [parts[n, q, pl.ds(PAD + r + 1, SUB), :] for n in range(3)]
            gy, gz, p, rho, mx, my, mz = (
                parts[n, q, pl.ds(PAD + r, SUB), :] for n in range(3, 10)
            )
            pull = [high[0] - low[0], gy + (high[1] + low[1]), gz + (high[2] + low[2])]
            flux = flux_of((mx, my, mz), p, pull, FINE_TAU)
            streams.append(balances(rho, flux, 1.0 / FINE_TAU))
        for i in range(Q):
            cx, cy, cz = VELOCITIES[i]
            post = []
            for q in qs:
                _, balance = next(streams[q])
                post.append(load(i, q, r) * (1.0 - 1.0 / FINE_TAU) + balance)
            if cy:
                post = shift_y(post, cy, i)
            if cz:
                post = shift_z(post, cz)
            for q in qs:
                store(i, q, r, cx, post[q])


CROSS = 5
FROM_DENSITY = Q
FROM_ENTER = Q + 1
FROM_PARTIAL = Q + 1 + CROSS
SENT = Q + 2 + CROSS


def edge_rows(nq):
    return SENT * nq + 2 * PLANES * (HALO // 2)


def sent_rows(nq):
    return -(-edge_rows(nq) // SUB) * SUB


def parts_of(count, pieces):
    cuts = [count * n // pieces for n in range(pieces + 1)]
    return list(zip(cuts[:-1], cuts[1:]))


def along(c):
    return [i for i in range(Q) if VELOCITIES[i][0] == c]


def restrict_body(ch_count, k_count, own, low, high):
    nq = ch_count * k_count

    def restricted(i, q, half):
        return own[pl.ds(i * (B * nq) + half * nq + q, SUB, stride=2 * nq), :]

    for side, out in enumerate((low, high)):
        for n, plane in enumerate(pack(restricted, ch_count, k_count, side)):
            out[n] = plane


def right_turn():
    return lax.axis_index("grp") % 2


def send_body(ch_count, k_count, own, ghosts, low, high, turn_0, turn_1, rim, moved, parts, sides):
    nq = ch_count * k_count
    per = B * nq
    edge = HALO // 2

    for i in range(Q):
        for q in range(nq):
            rim[i, q, pl.ds(0, HALO), :] = own[pl.ds(i * per + q, HALO, stride=nq), :]
            rim[i, q, pl.ds(HALO, HALO), :] = own[
                pl.ds(i * per + (B - HALO) * nq + q, HALO, stride=nq), :
            ]

    def load(i, q, r):
        return rim[i, q]

    def store(i, q, r, cx, v):
        moved[i, q, pl.ds(PAD + cx, SUB), :] = v

    substep(load, store, ghosts, 0, parts, ch_count, k_count, 1)

    right = right_turn()
    for c, out, outer in ((1, sides.at[right], B - 1), (-1, sides.at[1 - right], 0)):
        first = PAD + (SUB - 1 if c > 0 else 0)
        second = first - c
        for i in range(Q):
            out[pl.ds(i * nq, nq), :] = own[pl.ds(i * per + outer * nq, nq), :]
        for q in range(nq):
            out[pl.ds(FROM_DENSITY * nq + q, 1), :] = parts[6, q, pl.ds(second, 1), :]
            for n, i in enumerate(along(c)):
                out[pl.ds((FROM_ENTER + n) * nq + q, 1), :] = moved[i, q, pl.ds(first, 1), :]
            total = None
            for i in along(0) + along(c):
                v = moved[i, q, pl.ds(second, 1), :]
                total = v if total is None else total + v
            out[pl.ds(FROM_PARTIAL * nq + q, 1), :] = total
        x = SUB - edge if c > 0 else 0
        for place, ref in enumerate((low, high)):
            for n in range(PLANES):
                at = SENT * nq + (place * PLANES + n) * edge
                out[pl.ds(at, edge), :] = ref[n, pl.ds(x, edge), :]
        spare = sent_rows(nq) - edge_rows(nq)
        if spare:
            out[pl.ds(edge_rows(nq), spare), :] = jnp.zeros((spare, LANES), jnp.float32)
    turn_0[...] = sides[0]
    turn_1[...] = sides[1]


def inner_body(ch_count, k_count, own, ghosts, out, parts):
    nq = ch_count * k_count

    def load(i, q, r):
        return own[pl.ds(i * (B * nq) + r * nq + q, SUB, stride=nq), :]

    def store(i, q, r, cx, v):
        out[i, q, pl.ds(PAD + r + cx, SUB), :] = v

    substep(load, store, ghosts, HALO, parts, ch_count, k_count, B // SUB)


def fine_body(
    ch_count, k_count, own, turn_0, turn_1, inner, ghosts, rim_ghosts,
    out, rim, half, third, parts, held, sems, sides,
):
    nq = ch_count * k_count
    per = B * nq
    row = lax.broadcasted_iota(jnp.int32, (SUB, LANES), 0)
    origin = PAD + HALO
    sides[0] = turn_0[...]
    sides[1] = turn_1[...]
    left, right = sides.at[1 - right_turn()], sides.at[right_turn()]

    layers = Q * nq
    rim[pl.ds(1, layers, stride=SUB), :] = left[pl.ds(0, layers), :]
    rim[pl.ds(6, layers, stride=SUB), :] = right[pl.ds(0, layers), :]
    for i in range(Q):
        for sub, x in ((2, 0), (3, 1), (4, B - 2), (5, B - 1)):
            rim[pl.ds(i * (nq * SUB) + sub, nq, stride=SUB), :] = own[
                pl.ds(i * per + x * nq, nq), :
            ]

    def spread(ref, plane, q):
        return jnp.broadcast_to(ref[pl.ds(plane * nq + q, 1), :], (SUB, LANES))

    def load_rim(i, q, r):
        return rim[pl.ds((i * nq + q) * SUB, SUB), :]

    def rim_density(q, r, density):
        density = jnp.where(row == 0, spread(left, FROM_DENSITY, q), density)
        return jnp.where(row == SUB - 1, spread(right, FROM_DENSITY, q), density)

    outgoing = {(c, q): None for c in (-1, 1) for q in range(nq)}

    def store_rim(i, q, r, cx, v):
        half[i, q, pl.ds(origin - 2 + cx, SUB), :] = v
        half[i, q, pl.ds(origin + B - 6 + cx, SUB), :] = v
        if cx:
            seen = outgoing[cx, q]
            outgoing[cx, q] = v if seen is None else seen + v

    substep(load_rim, store_rim, rim_ghosts, 0, parts, ch_count, k_count, 1, rim_density)
    for i in range(Q):
        cx = VELOCITIES[i][0]
        for q in range(nq):
            half[i, q, pl.ds(origin + 1 + cx, B - 2), :] = inner[i, q, pl.ds(PAD + 1 + cx, B - 2), :]
            if cx:
                ref = left if cx > 0 else right
                at = origin - 1 if cx > 0 else origin + B
                place = FROM_ENTER + along(cx).index(i)
                half[i, q, pl.ds(at, 1), :] = ref[pl.ds(place * nq + q, 1), :]

    def load(i, q, r):
        return half[i, q, pl.ds(PAD + r, SUB), :]

    def store(i, q, r, cx, v):
        third[i, q, pl.ds(PAD + r + cx, SUB), :] = v

    chunks = (B + 2 * HALO) // SUB

    def density_of(q, r, density):
        if r == 0:
            value = spread(left, FROM_PARTIAL, q) + pltpu.roll(outgoing[-1, q], 1, 0)
            return jnp.where(row == HALO - 2, value, density)
        if r == (chunks - 1) * SUB:
            value = spread(right, FROM_PARTIAL, q) + pltpu.roll(outgoing[1, q], SUB - 1, 0)
            return jnp.where(row == SUB - HALO + 1, value, density)
        return density

    substep(load, store, ghosts, 0, parts, ch_count, k_count, chunks, density_of)

    copies = []
    for n, (i0, i1) in enumerate(parts_of(Q, PIECES)):
        for i in range(i0, i1):
            for q in range(nq):
                held[pl.ds(i * per + q, B, stride=nq), :] = third[i, q, pl.ds(origin, B), :]
        part = pl.ds(i0 * per, (i1 - i0) * per)
        copies.append(pltpu.make_async_copy(held.at[part], out.at[part], sems.at[n]))
        copies[-1].start()
    for copy in copies:
        copy.wait()


def fine_ghost_body(ch_count, rows, layers, spread, out, send_ghosts, rim_ghosts, wide):
    for side in range(2):
        wide[...] = jnp.dot(
            layers[side],
            spread[...],
            precision=lax.Precision.HIGHEST,
            preferred_element_type=jnp.float32,
        )
        wanted = UP if side == 0 else DOWN
        for ch in range(ch_count):
            for r in range(0, rows, SUB):
                f = [
                    wide[pl.ds(i * rows + r, SUB), pl.ds(ch * LANES, LANES)] for i in range(Q)
                ]
                potential, found = rescaled(f, TO_FINE, wanted)
                for n, i in enumerate(wanted):
                    out[side, n, ch, pl.ds(r, SUB), :] = found[i]
                out[side, NG - 1, ch, pl.ds(r, SUB), :] = potential
            for n in range(NG):
                for ref, lower, upper in (
                    (send_ghosts, HALO, rows - 2 * HALO),
                    (rim_ghosts, 2, rows - HALO - 2),
                ):
                    ref[side, n, ch, pl.ds(0, HALO), :] = out[side, n, ch, pl.ds(lower, HALO), :]
                    ref[side, n, ch, pl.ds(HALO, HALO), :] = out[
                        side, n, ch, pl.ds(upper, HALO), :
                    ]


STEP = 2 * B
GROUP = B // 2
PLANES = -(-2 * Q // STEP)


def place_of(i, ch):
    group, at = divmod(2 * i + ch, GROUP)
    plane, quarter = divmod(group, 4)
    return plane, 2 * at + quarter % 2 + B * (quarter // 2)


def pack(load, ch_count, k_count, side):
    lane = lax.broadcasted_iota(jnp.int32, (SUB, LANES), 1)
    offset = B - 2 if side == 0 else 0
    layers = lane % B // 2 == offset // 2
    kept = (lane % STEP < B) & (lane % 2 == 0)
    k = k_count - 1 if side == 0 else 0
    slots = [(i, ch) for i in range(Q) for ch in range(ch_count)]
    planes = [None] * PLANES
    for first in range(0, len(slots), GROUP):
        total = None
        for at, (i, ch) in enumerate(slots[first : first + GROUP]):
            q = ch * k_count + k
            v = jnp.where(layers, load(i, q, 0) + load(i, q, 1), 0.0)
            shift = (2 * at - offset) % LANES
            if shift:
                v = pltpu.roll(v, shift, 1)
            total = v if total is None else total + v
        total = total + pltpu.roll(total, LANES - 1, 1)
        total = total + pltpu.roll(total, LANES - B, 1)
        total = jnp.where(kept, total, 0.0)
        plane, shift = place_of(*slots[first])
        if shift:
            total = pltpu.roll(total, shift, 1)
        planes[plane] = total if planes[plane] is None else planes[plane] + total
    return planes


def coarse_body(planes, state, out, packed, near, parts, out_pad):
    lane = lax.broadcasted_iota(jnp.int32, (SUB, LANES), 1)

    def shift_y(v, c, which):
        return [pltpu.roll(v[0], 1 if c > 0 else LANES - 1, 1)]

    def shift_z(v, c):
        return [pltpu.roll(v[0], 1 if c > 0 else SUB - 1, 0)]

    def prepare(x, carry):
        density, momentum = moments([state[i, x] for i in range(Q)])
        p = 1.0 - jnp.exp(-density)
        values = gradient_parts([p], shift_y, shift_z)
        values = [v[0] for v in values] + [p, density, *momentum]
        for n, v in enumerate(values):
            parts[n, x] = v
        return carry

    lax.fori_loop(0, planes, prepare, 0, unroll=2)

    inner = planes - HALO
    base = HALO // 2

    def update(x, carry):
        lower = [parts[n, x - 1] for n in range(3)]
        upper = [parts[n, x + 1] for n in range(3)]
        gy, gz, p, rho, mx, my, mz = (parts[n, x] for n in range(3, 10))
        pull = [upper[0] - lower[0], gy + (upper[1] + lower[1]), gz + (upper[2] + lower[2])]
        flux = flux_of((mx, my, mz), p, pull, COARSE_TAU)
        for i, balance in balances(rho, flux, 1.0 / COARSE_TAU):
            cx, cy, cz = VELOCITIES[i]
            post = [state[i, x] * (1.0 - 1.0 / COARSE_TAU) + balance]
            if cy:
                post = shift_y(post, cy, i)
            if cz:
                post = shift_z(post, cz)
            inside = x + cx - base
            spare = jnp.where((inside >= 0) & (inside < inner), inside, inner)
            out_pad[i, spare] = post[0]
        return carry

    lax.fori_loop(base - 1, base + inner + 1, update, 0, unroll=2)
    out[...] = out_pad[:, :inner]

    def gather(i, carry):
        total = jnp.zeros((SUB, LANES), jnp.float32)
        for x in range(planes):
            here = (lane == 2 * x + 1) | (lane == 2 * x + 2)
            total = jnp.where(here, pltpu.roll(state[i, x], 2 * x + 2, 1), total)
        packed[i] = total
        return carry

    lax.fori_loop(0, Q, gather, 0)
    total = jnp.zeros((SUB, LANES), jnp.float32)
    for x in range(planes):
        p = parts[5, x]
        total = jnp.where(lane == 2 * x + 2, pltpu.roll(p, 2 * x + 1, 1), total)
        total = jnp.where(lane == 2 * x + 1, pltpu.roll(p, 2 * x + 3, 1), total)
    near[...] = total


def edges_body(
    ch_count, k_count, planes, turn_0, turn_1, low, high, packed, near, step,
    out, rows, columns, ghost, held, sems, sides,
):
    nq = ch_count * k_count
    edge = HALO // 2
    inner = planes - HALO
    lane = lax.broadcasted_iota(jnp.int32, (SUB, LANES), 1)
    sided = lane % 2 == 0
    tail = pl.ds(SENT * nq, PLANES * edge)
    sides[0] = turn_0[tail, :]
    sides[1] = turn_1[tail, :]
    left, right = sides.at[1 - right_turn()], sides.at[right_turn()]

    for n in range(PLANES):
        own_x = 2 * edge
        rows[n, pl.ds(2 + own_x, inner, stride=2), :] = low[n]
        beside = n * edge
        rows[n, pl.ds(2, edge, stride=2), :] = left[pl.ds(beside, edge), :]
        rows[n, pl.ds(2 + 2 * (edge + inner), edge, stride=2), :] = right[
            pl.ds(beside, edge), :
        ]
        rows[n, pl.ds(1 + own_x, inner, stride=2), :] = high[pl.ds(n * SUB, inner), :]
        turn = right_turn()
        for at, place in ((1, 1 - turn), (1 + 2 * (edge + inner), turn)):
            rows[n, pl.ds(at, edge, stride=2), :] = high[
                pl.ds(PLANES * SUB + (place * PLANES + n) * edge, edge), :
            ]
        columns[n, :, pl.ds(0, STEP)] = rows[n, pl.ds(0, STEP), :].T
    per = LANES // STEP
    for i in range(Q):
        for ch in range(ch_count):
            plane, at = place_of(i, ch)
            ghost[i, pl.ds(ch * per, per), :] = (
                0.125 * columns[plane, pl.ds(at, per, stride=STEP), :]
            )

    beyond, entering = rescaled([ghost[i] for i in range(Q)], TO_COARSE, UP + DOWN)
    density, momentum = moments([packed[i] for i in range(Q)])
    p = 1.0 - jnp.exp(-density)
    inside = near[...]
    above = jnp.where(sided, inside, beyond)
    below = jnp.where(sided, beyond, inside)

    def shift_y(v, c, which):
        return [below if c > 0 else above]

    def shift_z(v, c):
        return [pltpu.roll(v[0], 1 if c > 0 else SUB - 1, 0)]

    def shift_x(v, c):
        return pltpu.roll(v, 2 if c > 0 else LANES - 2, 1) if c else v

    tx, dy, dz, gy, gz = (v[0] for v in gradient_parts([p], shift_y, shift_z))
    pull = [
        shift_x(tx, -1) - shift_x(tx, 1),
        gy + (shift_x(dy, -1) + shift_x(dy, 1)),
        gz + (shift_x(dz, -1) + shift_x(dz, 1)),
    ]
    flux = flux_of(momentum, p, pull, COARSE_TAU)
    copies = []
    for i, balance in balances(density, flux, 1.0 / COARSE_TAU):
        cx, cy, cz = VELOCITIES[i]
        v = packed[i] * (1.0 - 1.0 / COARSE_TAU) + balance
        if cy > 0:
            v = jnp.where(sided, entering[i], pltpu.roll(v, 1, 1))
            touched = lane < 2
        elif cy < 0:
            v = jnp.where(sided, pltpu.roll(v, LANES - 1, 1), entering[i])
            touched = lane >= LANES - 2
        else:
            touched = (lane == 0) | (lane == LANES - 1)
        v = shift_x(v, cx)
        if cz:
            v = shift_z([v], cz)[0]
        for x in range(inner):
            column = pltpu.roll(v, LANES - (2 * (x + edge) + 2), 1)
            held[i, x] = jnp.where(touched, column, step[i, x])
        for n, (i0, i1) in enumerate(parts_of(Q, PIECES)):
            if i == i1 - 1:
                part = pl.ds(i0, i1 - i0)
                copies.append(pltpu.make_async_copy(held.at[part], out.at[part], sems.at[n]))
                copies[-1].start()
    for copy in copies:
        copy.wait()


def ring(count, step):
    return [(i, (i + step) % count) for i in range(count)]


def slab_pairs(n_grp, n_wide, up, across):
    return [
        (g * n_wide + w, (g + across) % n_grp * n_wide + (w + up) % n_wide)
        for g in range(n_grp)
        for w in range(n_wide)
    ]


def local(fine_pop, coarse_pop, new_slot):
    k_count, q_count, cells = fine_pop.shape
    blocks = new_slot.shape[0]
    devices = blocks // k_count
    tiles = cells // LANES
    ch_count = tiles // B
    nq = ch_count * k_count
    axes = ("grp", "wide")
    n_grp, n_wide = lax.axis_size("grp"), lax.axis_size("wide")
    _, cx, cz, cy = coarse_pop.shape
    planes = cx + HALO
    fine_rows = B + 2 * HALO

    rows = pl.cdiv(Q * tiles, devices)
    pieces = fine_pop.reshape(k_count, Q, tiles, LANES)
    pieces = with_layout_constraint(pieces, Layout(major_to_minor=(1, 2, 0, 3)))
    pieces = pieces.transpose(1, 2, 0, 3)
    pieces = pieces.reshape(Q * tiles, k_count, LANES)
    if rows * devices != Q * tiles:
        pieces = jnp.pad(pieces, ((0, rows * devices - Q * tiles), (0, 0), (0, 0)))
    pieces = pieces.reshape(devices, rows, k_count, LANES)
    spread = lax.all_to_all(pieces, axes, 0, 0, tiled=True)
    edge = HALO // 2
    coarse_left = lax.ppermute(coarse_pop[:, cx - edge :], "grp", ring(n_grp, 1))
    coarse_right = lax.ppermute(coarse_pop[:, :edge], "grp", ring(n_grp, -1))
    last = coarse_pop[..., -1]
    below = []
    for part, across in ((last[:, cx - edge :], 1), (last, 0), (last[:, :edge], -1)):
        below.append(lax.ppermute(part, axes, slab_pairs(n_grp, n_wide, 1, across)))
    total = devices * rows * k_count
    regroup = call(
        functools.partial(regroup_body, blocks, k_count, rows),
        f32(total, LANES),
        [VMEM, VMEM],
        moved=8 * total * LANES,
    )
    targets = rows * new_slot - (rows - 1) * (new_slot % k_count)
    outgoing = regroup(targets[None], spread.reshape(total, LANES))
    arrived = lax.all_to_all(
        outgoing.reshape(devices, rows, k_count, LANES), axes, 0, 0, tiled=True
    )
    coarse = jnp.concatenate([coarse_left, coarse_pop, coarse_right], axis=1)
    below = jnp.concatenate(below, axis=1)
    layers = jnp.repeat(jnp.stack([below, coarse[..., 0]]), 2, axis=2)
    layers = layers.reshape(2, Q * fine_rows, cz)
    lane = jnp.arange(ch_count * LANES) // (2 * B)
    one_hot = (jnp.arange(cz)[:, None] == lane[None, :]).astype(jnp.float32)
    fine_ghosts, send_ghosts, rim_ghosts = call(
        functools.partial(fine_ghost_body, ch_count, fine_rows),
        [f32(2, NG, ch_count, n, LANES) for n in (fine_rows, SUB, SUB)],
        [VMEM, VMEM],
        [pltpu.VMEM((Q * fine_rows, ch_count * LANES), jnp.float32)],
    )(layers, one_hot)
    coarse_step, packed, near = call(
        functools.partial(coarse_body, planes),
        [f32(Q, cx, cz, cy), f32(Q, SUB, LANES), f32(SUB, LANES)],
        [VMEM],
        [
            pltpu.VMEM((10, planes, SUB, LANES), jnp.float32),
            pltpu.VMEM((Q, cx + 1, SUB, LANES), jnp.float32),
        ],
        flops=10**7,
    )(coarse)
    hidden = (fine_ghosts, send_ghosts, rim_ghosts, coarse_step, packed, near)
    arrived, hidden = lax.optimization_barrier((arrived, hidden))
    fine_ghosts, send_ghosts, rim_ghosts, coarse_step, packed, near = hidden
    own = arrived.reshape(total, LANES)[: Q * tiles * k_count]

    padded = PAD + fine_rows + PAD
    low, first = call(
        functools.partial(restrict_body, ch_count, k_count),
        [f32(PLANES, SUB, LANES)] * 2,
        [VMEM],
    )(own)
    turns = call(
        functools.partial(send_body, ch_count, k_count),
        [f32(sent_rows(nq), LANES)] * 2,
        [VMEM] * 4,
        [
            pltpu.VMEM((Q, nq, SUB, LANES), jnp.float32),
            pltpu.VMEM((Q, nq, 3 * PAD, LANES), jnp.float32),
            pltpu.VMEM((10, nq, 3 * PAD, LANES), jnp.float32),
            pltpu.VMEM((2, sent_rows(nq), LANES), jnp.float32),
        ],
    )(own, send_ghosts, low, first)
    assert n_grp % 2 == 0
    swaps = []
    for turn, values in enumerate(turns):
        ends = [((g + turn) % n_grp, (g + turn + 1) % n_grp) for g in range(0, n_grp, 2)]
        swaps.append(lax.ppermute(values, "grp", ends + [(j, i) for i, j in ends]))
    inner = call(
        functools.partial(inner_body, ch_count, k_count),
        f32(Q, nq, PAD + B + PAD, LANES),
        [VMEM] * 2,
        [pltpu.VMEM((10, nq, PAD + B + PAD, LANES), jnp.float32)],
        flops=10**7,
    )(own, fine_ghosts)
    tail = edge_rows(nq) - PLANES * edge
    widened = jnp.concatenate(
        [first.reshape(PLANES * SUB, LANES)]
        + [swap[tail : tail + PLANES * edge] for swap in swaps]
    )
    high = lax.ppermute(widened, "wide", ring(n_wide, -1))

    fine = call(
        functools.partial(fine_body, ch_count, k_count),
        f32(Q * B * nq, LANES),
        [VMEM] * 6,
        [
            pltpu.VMEM((Q * nq * SUB, LANES), jnp.float32),
            pltpu.VMEM((Q, nq, padded, LANES), jnp.float32),
            pltpu.VMEM((Q, nq, padded, LANES), jnp.float32),
            pltpu.VMEM((10, nq, padded, LANES), jnp.float32),
            pltpu.VMEM((Q * B * nq, LANES), jnp.float32),
            pltpu.SemaphoreType.DMA((PIECES,)),
            pltpu.VMEM((2, sent_rows(nq), LANES), jnp.float32),
        ],
        flops=10**7,
        place=HBM,
    )(own, *swaps, inner, fine_ghosts, rim_ghosts)

    coarse_out = call(
        functools.partial(edges_body, ch_count, k_count, planes),
        f32(Q, cx, cz, cy),
        [VMEM] * 7,
        [
            pltpu.VMEM((PLANES, LANES, LANES), jnp.float32),
            pltpu.VMEM((PLANES, LANES, LANES), jnp.float32),
            pltpu.VMEM((Q, SUB, LANES), jnp.float32),
            pltpu.VMEM((Q, cx, cz, cy), jnp.float32),
            pltpu.SemaphoreType.DMA((PIECES,)),
            pltpu.VMEM((2, PLANES * edge, LANES), jnp.float32),
        ],
        place=HBM,
    )(*swaps, low, high, packed, near, coarse_step)

    fine_out = fine.reshape(Q, tiles, k_count, LANES).transpose(2, 0, 1, 3)
    fine_out = fine_out.reshape(k_count, q_count, cells)
    return fine_out, coarse_out


def solution(mesh):
    return jax.shard_map(
        local,
        mesh=mesh,
        in_specs=(P(("grp", "wide"), None, None), P(None, "grp", None, "wide"), P()),
        out_specs=(P(("grp", "wide"), None, None), P(None, "grp", None, "wide")),
        check_vma=False,
    )
```

```python
import functools

import jax
import jax.numpy as jnp
from jax import lax
from jax.experimental import pallas as pl
from jax.experimental.layout import Layout, with_layout_constraint
from jax.experimental.pallas import tpu as pltpu
from jax.sharding import PartitionSpec as P


B = 16
LANES = 128
SUB = 8
HALO = 4
PAD = 8
GRANT = 24 << 20
PIECES = 8

VELOCITIES = (
    (0, 0, 0),
    (1, 0, 0),
    (-1, 0, 0),
    (0, 1, 0),
    (0, -1, 0),
    (0, 0, 1),
    (0, 0, -1),
    (1, 1, 0),
    (-1, -1, 0),
    (1, -1, 0),
    (-1, 1, 0),
    (1, 0, 1),
    (-1, 0, -1),
    (1, 0, -1),
    (-1, 0, 1),
    (0, 1, 1),
    (0, -1, -1),
    (0, 1, -1),
    (0, -1, 1),
)
Q = len(VELOCITIES)
WEIGHTS = (1.0 / 3.0,) + (1.0 / 18.0,) * 6 + (1.0 / 36.0,) * 12
W_DIAG = WEIGHTS[7]
COUPLING = -5.0
FINE_TAU = 1.1
COARSE_TAU = 0.8
TO_COARSE = 2.0 * COARSE_TAU / FINE_TAU
TO_FINE = FINE_TAU / (2.0 * COARSE_TAU)
UP = tuple(i for i in range(Q) if VELOCITIES[i][1] == 1)
DOWN = tuple(i for i in range(Q) if VELOCITIES[i][1] == -1)
NG = len(UP) + 1

VMEM = pl.BlockSpec(memory_space=pltpu.VMEM)
HBM = pl.BlockSpec(memory_space=pl.ANY)


def call(body, outs, specs, scratch=(), flops=10**6, moved=10**6, place=VMEM):
    return pl.pallas_call(
        body,
        out_shape=outs,
        in_specs=specs,
        out_specs=jax.tree.map(lambda _: place, outs),
        scratch_shapes=list(scratch),
        cost_estimate=pl.CostEstimate(flops=flops, bytes_accessed=moved, transcendentals=0),
        compiler_params=pltpu.CompilerParams(vmem_limit_bytes=GRANT),
    )


def f32(*shape):
    return jax.ShapeDtypeStruct(shape, jnp.float32)


def moments(f):
    density = f[0]
    momentum = [None, None, None]
    for i in range(1, Q, 2):
        density = density + (f[i] + f[i + 1])
        odd = f[i] - f[i + 1]
        for j in range(3):
            c = VELOCITIES[i][j]
            if c:
                term = odd if c > 0 else -odd
                if momentum[j] is None:
                    momentum[j] = term
                else:
                    momentum[j] = momentum[j] + odd if c > 0 else momentum[j] - odd
    return density, momentum


def balances(density, flux, scale):
    w = density * (W_DIAG * scale)
    half = 1.5 / density
    v = [x * half for x in flux]
    g = [x * (3.0 * W_DIAG * scale) for x in flux]
    g2 = [x + x for x in g]
    h = [g[j] * v[j] for j in range(3)]
    total = h[0] + h[1] + h[2]
    base = w - total * (1.0 / 3.0)
    base2 = base + base
    yield 0, base2 * (0.5 * WEIGHTS[0] / W_DIAG)
    for j in range(3):
        even = base2 + (h[j] + h[j])
        yield 2 * j + 1, even + g2[j]
        yield 2 * j + 2, even - g2[j]
    all_h = base + total
    i = 7
    for a, b, c in ((0, 1, 2), (0, 2, 1), (1, 2, 0)):
        even = all_h - h[c]
        cross = g2[a] * v[b]
        for sign in (1, -1):
            side = even + cross if sign > 0 else even - cross
            odd = g[a] + g[b] if sign > 0 else g[a] - g[b]
            yield i, side + odd
            yield i + 1, side - odd
            i += 2


def rescaled(f, factor, wanted):
    density, momentum = moments(f)
    found = {}
    for i, balance in balances(density, momentum, 1.0):
        if i in wanted:
            found[i] = balance + factor * (f[i] - balance)
    return 1.0 - jnp.exp(-density), found


def gradient_parts(p, shift_y, shift_z):
    above = shift_y(p, -1, "p")
    below = shift_y(p, 1, "p")
    front = shift_z(p, -1)
    back = shift_z(p, 1)
    n = range(len(p))
    dy = [above[q] - below[q] for q in n]
    dz = [front[q] - back[q] for q in n]
    mixed = [(p[q] + p[q]) + (above[q] + below[q]) for q in n]
    tx = [mixed[q] + (front[q] + back[q]) for q in n]
    mixed_front = shift_z(mixed, -1)
    mixed_back = shift_z(mixed, 1)
    dy_front = shift_z(dy, -1)
    dy_back = shift_z(dy, 1)
    gy = [(dy[q] + dy[q]) + (dy_front[q] + dy_back[q]) for q in n]
    gz = [mixed_front[q] - mixed_back[q] for q in n]
    return tx, dy, dz, gy, gz


def flux_of(momentum, potential, pull, tau):
    force = (-tau * COUPLING * W_DIAG) * potential
    return [momentum[j] + force * pull[j] for j in range(3)]


def regroup_body(blocks, k_blocks, rows, target_ref, in_ref, out_ref):
    targets = target_ref[...]
    for b in range(blocks):
        source = (b // k_blocks) * (rows * k_blocks) + b % k_blocks
        out_ref[pl.ds(targets[0, b], rows, stride=k_blocks), :] = in_ref[
            pl.ds(source, rows, stride=k_blocks), :
        ]


def lane_ids():
    lane = lax.broadcasted_iota(jnp.int32, (SUB, LANES), 1)
    return lane % B, lane // B


def fine_shifts(ch_count, k_count, ghost):
    y, z = lane_ids()
    first_y, last_y = y == 0, y == B - 1
    first_z, last_z = z == 0, z == LANES // B - 1

    def shift_y(v, c, which):
        out = []
        for ch in range(ch_count):
            for k in range(k_count):
                q = ch * k_count + k
                if c > 0:
                    own = pltpu.roll(v[q], 1, 1)
                    carry = (
                        ghost(0, which, ch) if k == 0 else pltpu.roll(v[q - 1], LANES - (B - 1), 1)
                    )
                    out.append(jnp.where(first_y, carry, own))
                else:
                    own = pltpu.roll(v[q], LANES - 1, 1)
                    carry = (
                        ghost(1, which, ch)
                        if k == k_count - 1
                        else pltpu.roll(v[q + 1], B - 1, 1)
                    )
                    out.append(jnp.where(last_y, carry, own))
        return out

    def shift_z(v, c):
        rolled = [pltpu.roll(x, B if c > 0 else LANES - B, 1) for x in v]
        edge = first_z if c > 0 else last_z
        out = []
        for ch in range(ch_count):
            other = (ch - c) % ch_count
            for k in range(k_count):
                q = ch * k_count + k
                out.append(jnp.where(edge, rolled[other * k_count + k], rolled[q]))
        return out

    return shift_y, shift_z


def substep(load, store, ghosts, start, parts, ch_count, k_count, chunks, density_of=None):
    qs = range(ch_count * k_count)
    for chunk in range(chunks):
        r = chunk * SUB

        def ghost(side, which, ch, r=r):
            return ghosts[side, NG - 1, ch, pl.ds(start + r, SUB), :]

        moved = [moments([load(i, q, r) for i in range(Q)]) for q in qs]
        density = [moved[q][0] for q in qs]
        if density_of is not None:
            density = [density_of(q, r, density[q]) for q in qs]
        p = [1.0 - jnp.exp(-density[q]) for q in qs]
        shift_y, shift_z = fine_shifts(ch_count, k_count, ghost)
        tx, dy, dz, gy, gz = gradient_parts(p, shift_y, shift_z)
        for q in qs:
            values = (tx[q], dy[q], dz[q], gy[q], gz[q], p[q], density[q], *moved[q][1])
            for n, v in enumerate(values):
                parts[n, q, pl.ds(PAD + r, SUB), :] = v
    for chunk in range(chunks):
        r = chunk * SUB

        def ghost(side, which, ch, r=r):
            place = (UP if side == 0 else DOWN).index(which)
            return ghosts[side, place, ch, pl.ds(start + r, SUB), :]

        shift_y, shift_z = fine_shifts(ch_count, k_count, ghost)
        streams = []
        for q in qs:
            low = [parts[n, q, pl.ds(PAD + r - 1, SUB), :] for n in range(3)]
            high = [parts[n, q, pl.ds(PAD + r + 1, SUB), :] for n in range(3)]
            gy, gz, p, rho, mx, my, mz = (
                parts[n, q, pl.ds(PAD + r, SUB), :] for n in range(3, 10)
            )
            pull = [high[0] - low[0], gy + (high[1] + low[1]), gz + (high[2] + low[2])]
            flux = flux_of((mx, my, mz), p, pull, FINE_TAU)
            streams.append(balances(rho, flux, 1.0 / FINE_TAU))
        for i in range(Q):
            cx, cy, cz = VELOCITIES[i]
            post = []
            for q in qs:
                _, balance = next(streams[q])
                post.append(load(i, q, r) * (1.0 - 1.0 / FINE_TAU) + balance)
            if cy:
                post = shift_y(post, cy, i)
            if cz:
                post = shift_z(post, cz)
            for q in qs:
                store(i, q, r, cx, post[q])


CROSS = 5
FROM_DENSITY = Q
FROM_ENTER = Q + 1
FROM_PARTIAL = Q + 1 + CROSS
SENT = Q + 2 + CROSS


def edge_rows(nq):
    return SENT * nq + PLANES * (HALO // 2)


def sent_rows(nq):
    return -(-edge_rows(nq) // SUB) * SUB


def parts_of(count, pieces):
    cuts = [count * n // pieces for n in range(pieces + 1)]
    return list(zip(cuts[:-1], cuts[1:]))


def along(c):
    return [i for i in range(Q) if VELOCITIES[i][0] == c]


def restrict_body(ch_count, k_count, own, low, high):
    nq = ch_count * k_count

    def restricted(i, q, half):
        return own[pl.ds(i * (B * nq) + half * nq + q, SUB, stride=2 * nq), :]

    for side, out in enumerate((low, high)):
        for n, plane in enumerate(pack(restricted, ch_count, k_count, side)):
            out[n] = plane


def send_body(ch_count, k_count, own, ghosts, low, to_left, to_right, rim, moved, parts):
    nq = ch_count * k_count
    per = B * nq
    edge = HALO // 2

    for i in range(Q):
        for q in range(nq):
            rim[i, q, pl.ds(0, HALO), :] = own[pl.ds(i * per + q, HALO, stride=nq), :]
            rim[i, q, pl.ds(HALO, HALO), :] = own[
                pl.ds(i * per + (B - HALO) * nq + q, HALO, stride=nq), :
            ]

    def load(i, q, r):
        return rim[i, q]

    def store(i, q, r, cx, v):
        moved[i, q, pl.ds(PAD + cx, SUB), :] = v

    substep(load, store, ghosts, 0, parts, ch_count, k_count, 1)

    for c, out, outer in ((1, to_right, B - 1), (-1, to_left, 0)):
        first = PAD + (SUB - 1 if c > 0 else 0)
        second = first - c
        for i in range(Q):
            out[pl.ds(i * nq, nq), :] = own[pl.ds(i * per + outer * nq, nq), :]
        for q in range(nq):
            out[pl.ds(FROM_DENSITY * nq + q, 1), :] = parts[6, q, pl.ds(second, 1), :]
            for n, i in enumerate(along(c)):
                out[pl.ds((FROM_ENTER + n) * nq + q, 1), :] = moved[i, q, pl.ds(first, 1), :]
            total = None
            for i in along(0) + along(c):
                v = moved[i, q, pl.ds(second, 1), :]
                total = v if total is None else total + v
            out[pl.ds(FROM_PARTIAL * nq + q, 1), :] = total
        for n in range(PLANES):
            x = SUB - edge if c > 0 else 0
            out[pl.ds(SENT * nq + n * edge, edge), :] = low[n, pl.ds(x, edge), :]
        spare = sent_rows(nq) - edge_rows(nq)
        if spare:
            out[pl.ds(edge_rows(nq), spare), :] = jnp.zeros((spare, LANES), jnp.float32)


def inner_body(ch_count, k_count, own, ghosts, out, parts):
    nq = ch_count * k_count

    def load(i, q, r):
        return own[pl.ds(i * (B * nq) + r * nq + q, SUB, stride=nq), :]

    def store(i, q, r, cx, v):
        out[i, q, pl.ds(PAD + r + cx, SUB), :] = v

    substep(load, store, ghosts, HALO, parts, ch_count, k_count, B // SUB)


def fine_body(
    ch_count, k_count, own, left, right, inner, ghosts, rim_ghosts, out, rim, half, third, parts, held, sems
):
    nq = ch_count * k_count
    per = B * nq
    row = lax.broadcasted_iota(jnp.int32, (SUB, LANES), 0)
    origin = PAD + HALO

    layers = Q * nq
    rim[pl.ds(1, layers, stride=SUB), :] = left[pl.ds(0, layers), :]
    rim[pl.ds(6, layers, stride=SUB), :] = right[pl.ds(0, layers), :]
    for i in range(Q):
        for sub, x in ((2, 0), (3, 1), (4, B - 2), (5, B - 1)):
            rim[pl.ds(i * (nq * SUB) + sub, nq, stride=SUB), :] = own[
                pl.ds(i * per + x * nq, nq), :
            ]

    def spread(ref, plane, q):
        return jnp.broadcast_to(ref[pl.ds(plane * nq + q, 1), :], (SUB, LANES))

    def load_rim(i, q, r):
        return rim[pl.ds((i * nq + q) * SUB, SUB), :]

    def rim_density(q, r, density):
        density = jnp.where(row == 0, spread(left, FROM_DENSITY, q), density)
        return jnp.where(row == SUB - 1, spread(right, FROM_DENSITY, q), density)

    outgoing = {(c, q): None for c in (-1, 1) for q in range(nq)}

    def store_rim(i, q, r, cx, v):
        half[i, q, pl.ds(origin - 2 + cx, SUB), :] = v
        half[i, q, pl.ds(origin + B - 6 + cx, SUB), :] = v
        if cx:
            seen = outgoing[cx, q]
            outgoing[cx, q] = v if seen is None else seen + v

    substep(load_rim, store_rim, rim_ghosts, 0, parts, ch_count, k_count, 1, rim_density)
    for i in range(Q):
        cx = VELOCITIES[i][0]
        for q in range(nq):
            half[i, q, pl.ds(origin + 1 + cx, B - 2), :] = inner[i, q, pl.ds(PAD + 1 + cx, B - 2), :]
            if cx:
                ref = left if cx > 0 else right
                at = origin - 1 if cx > 0 else origin + B
                place = FROM_ENTER + along(cx).index(i)
                half[i, q, pl.ds(at, 1), :] = ref[pl.ds(place * nq + q, 1), :]

    def load(i, q, r):
        return half[i, q, pl.ds(PAD + r, SUB), :]

    def store(i, q, r, cx, v):
        third[i, q, pl.ds(PAD + r + cx, SUB), :] = v

    chunks = (B + 2 * HALO) // SUB

    def density_of(q, r, density):
        if r == 0:
            value = spread(left, FROM_PARTIAL, q) + pltpu.roll(outgoing[-1, q], 1, 0)
            return jnp.where(row == HALO - 2, value, density)
        if r == (chunks - 1) * SUB:
            value = spread(right, FROM_PARTIAL, q) + pltpu.roll(outgoing[1, q], SUB - 1, 0)
            return jnp.where(row == SUB - HALO + 1, value, density)
        return density

    substep(load, store, ghosts, 0, parts, ch_count, k_count, chunks, density_of)

    copies = []
    for n, (i0, i1) in enumerate(parts_of(Q, PIECES)):
        for i in range(i0, i1):
            for q in range(nq):
                held[pl.ds(i * per + q, B, stride=nq), :] = third[i, q, pl.ds(origin, B), :]
        part = pl.ds(i0 * per, (i1 - i0) * per)
        copies.append(pltpu.make_async_copy(held.at[part], out.at[part], sems.at[n]))
        copies[-1].start()
    for copy in copies:
        copy.wait()


def fine_ghost_body(ch_count, rows, layers, spread, out, send_ghosts, rim_ghosts, wide):
    for side in range(2):
        wide[...] = jnp.dot(
            layers[side],
            spread[...],
            precision=lax.Precision.HIGHEST,
            preferred_element_type=jnp.float32,
        )
        wanted = UP if side == 0 else DOWN
        for ch in range(ch_count):
            for r in range(0, rows, SUB):
                f = [
                    wide[pl.ds(i * rows + r, SUB), pl.ds(ch * LANES, LANES)] for i in range(Q)
                ]
                potential, found = rescaled(f, TO_FINE, wanted)
                for n, i in enumerate(wanted):
                    out[side, n, ch, pl.ds(r, SUB), :] = found[i]
                out[side, NG - 1, ch, pl.ds(r, SUB), :] = potential
            for n in range(NG):
                for ref, lower, upper in (
                    (send_ghosts, HALO, rows - 2 * HALO),
                    (rim_ghosts, 2, rows - HALO - 2),
                ):
                    ref[side, n, ch, pl.ds(0, HALO), :] = out[side, n, ch, pl.ds(lower, HALO), :]
                    ref[side, n, ch, pl.ds(HALO, HALO), :] = out[
                        side, n, ch, pl.ds(upper, HALO), :
                    ]


STEP = 2 * B
GROUP = B // 2
PLANES = -(-2 * Q // STEP)


def place_of(i, ch):
    group, at = divmod(2 * i + ch, GROUP)
    plane, quarter = divmod(group, 4)
    return plane, 2 * at + quarter % 2 + B * (quarter // 2)


def pack(load, ch_count, k_count, side):
    lane = lax.broadcasted_iota(jnp.int32, (SUB, LANES), 1)
    offset = B - 2 if side == 0 else 0
    layers = lane % B // 2 == offset // 2
    kept = (lane % STEP < B) & (lane % 2 == 0)
    k = k_count - 1 if side == 0 else 0
    slots = [(i, ch) for i in range(Q) for ch in range(ch_count)]
    planes = [None] * PLANES
    for first in range(0, len(slots), GROUP):
        total = None
        for at, (i, ch) in enumerate(slots[first : first + GROUP]):
            q = ch * k_count + k
            v = jnp.where(layers, load(i, q, 0) + load(i, q, 1), 0.0)
            shift = (2 * at - offset) % LANES
            if shift:
                v = pltpu.roll(v, shift, 1)
            total = v if total is None else total + v
        total = total + pltpu.roll(total, LANES - 1, 1)
        total = total + pltpu.roll(total, LANES - B, 1)
        total = jnp.where(kept, total, 0.0)
        plane, shift = place_of(*slots[first])
        if shift:
            total = pltpu.roll(total, shift, 1)
        planes[plane] = total if planes[plane] is None else planes[plane] + total
    return planes


def coarse_body(planes, state, out, packed, near, parts, out_pad):
    lane = lax.broadcasted_iota(jnp.int32, (SUB, LANES), 1)

    def shift_y(v, c, which):
        return [pltpu.roll(v[0], 1 if c > 0 else LANES - 1, 1)]

    def shift_z(v, c):
        return [pltpu.roll(v[0], 1 if c > 0 else SUB - 1, 0)]

    def prepare(x, carry):
        density, momentum = moments([state[i, x] for i in range(Q)])
        p = 1.0 - jnp.exp(-density)
        values = gradient_parts([p], shift_y, shift_z)
        values = [v[0] for v in values] + [p, density, *momentum]
        for n, v in enumerate(values):
            parts[n, x] = v
        return carry

    lax.fori_loop(0, planes, prepare, 0, unroll=2)

    inner = planes - HALO
    base = HALO // 2

    def update(x, carry):
        lower = [parts[n, x - 1] for n in range(3)]
        upper = [parts[n, x + 1] for n in range(3)]
        gy, gz, p, rho, mx, my, mz = (parts[n, x] for n in range(3, 10))
        pull = [upper[0] - lower[0], gy + (upper[1] + lower[1]), gz + (upper[2] + lower[2])]
        flux = flux_of((mx, my, mz), p, pull, COARSE_TAU)
        for i, balance in balances(rho, flux, 1.0 / COARSE_TAU):
            cx, cy, cz = VELOCITIES[i]
            post = [state[i, x] * (1.0 - 1.0 / COARSE_TAU) + balance]
            if cy:
                post = shift_y(post, cy, i)
            if cz:
                post = shift_z(post, cz)
            inside = x + cx - base
            spare = jnp.where((inside >= 0) & (inside < inner), inside, inner)
            out_pad[i, spare] = post[0]
        return carry

    lax.fori_loop(base - 1, base + inner + 1, update, 0, unroll=2)
    out[...] = out_pad[:, :inner]

    def gather(i, carry):
        total = jnp.zeros((SUB, LANES), jnp.float32)
        for x in range(planes):
            here = (lane == 2 * x + 1) | (lane == 2 * x + 2)
            total = jnp.where(here, pltpu.roll(state[i, x], 2 * x + 2, 1), total)
        packed[i] = total
        return carry

    lax.fori_loop(0, Q, gather, 0)
    total = jnp.zeros((SUB, LANES), jnp.float32)
    for x in range(planes):
        p = parts[5, x]
        total = jnp.where(lane == 2 * x + 2, pltpu.roll(p, 2 * x + 1, 1), total)
        total = jnp.where(lane == 2 * x + 1, pltpu.roll(p, 2 * x + 3, 1), total)
    near[...] = total


def edges_body(
    ch_count, k_count, planes, left, right, low, high, high_left, high_right, packed, near, step,
    out, rows, columns, ghost, held, sems,
):
    nq = ch_count * k_count
    edge = HALO // 2
    inner = planes - HALO
    lane = lax.broadcasted_iota(jnp.int32, (SUB, LANES), 1)
    sided = lane % 2 == 0

    for n in range(PLANES):
        own_x = 2 * edge
        rows[n, pl.ds(2 + own_x, inner, stride=2), :] = low[n]
        beside = SENT * nq + n * edge
        rows[n, pl.ds(2, edge, stride=2), :] = left[pl.ds(beside, edge), :]
        rows[n, pl.ds(2 + 2 * (edge + inner), edge, stride=2), :] = right[
            pl.ds(beside, edge), :
        ]
        rows[n, pl.ds(1 + own_x, inner, stride=2), :] = high[n]
        rows[n, pl.ds(1, edge, stride=2), :] = high_left[n, pl.ds(inner - edge, edge), :]
        rows[n, pl.ds(1 + 2 * (edge + inner), edge, stride=2), :] = high_right[
            n, pl.ds(0, edge), :
        ]
        columns[n, :, pl.ds(0, STEP)] = rows[n, pl.ds(0, STEP), :].T
    per = LANES // STEP
    for i in range(Q):
        for ch in range(ch_count):
            plane, at = place_of(i, ch)
            ghost[i, pl.ds(ch * per, per), :] = (
                0.125 * columns[plane, pl.ds(at, per, stride=STEP), :]
            )

    beyond, entering = rescaled([ghost[i] for i in range(Q)], TO_COARSE, UP + DOWN)
    density, momentum = moments([packed[i] for i in range(Q)])
    p = 1.0 - jnp.exp(-density)
    inside = near[...]
    above = jnp.where(sided, inside, beyond)
    below = jnp.where(sided, beyond, inside)

    def shift_y(v, c, which):
        return [below if c > 0 else above]

    def shift_z(v, c):
        return [pltpu.roll(v[0], 1 if c > 0 else SUB - 1, 0)]

    def shift_x(v, c):
        return pltpu.roll(v, 2 if c > 0 else LANES - 2, 1) if c else v

    tx, dy, dz, gy, gz = (v[0] for v in gradient_parts([p], shift_y, shift_z))
    pull = [
        shift_x(tx, -1) - shift_x(tx, 1),
        gy + (shift_x(dy, -1) + shift_x(dy, 1)),
        gz + (shift_x(dz, -1) + shift_x(dz, 1)),
    ]
    flux = flux_of(momentum, p, pull, COARSE_TAU)
    copies = []
    for i, balance in balances(density, flux, 1.0 / COARSE_TAU):
        cx, cy, cz = VELOCITIES[i]
        v = packed[i] * (1.0 - 1.0 / COARSE_TAU) + balance
        if cy > 0:
            v = jnp.where(sided, entering[i], pltpu.roll(v, 1, 1))
            touched = lane < 2
        elif cy < 0:
            v = jnp.where(sided, pltpu.roll(v, LANES - 1, 1), entering[i])
            touched = lane >= LANES - 2
        else:
            touched = (lane == 0) | (lane == LANES - 1)
        v = shift_x(v, cx)
        if cz:
            v = shift_z([v], cz)[0]
        for x in range(inner):
            column = pltpu.roll(v, LANES - (2 * (x + edge) + 2), 1)
            held[i, x] = jnp.where(touched, column, step[i, x])
        for n, (i0, i1) in enumerate(parts_of(Q, PIECES)):
            if i == i1 - 1:
                part = pl.ds(i0, i1 - i0)
                copies.append(pltpu.make_async_copy(held.at[part], out.at[part], sems.at[n]))
                copies[-1].start()
    for copy in copies:
        copy.wait()


def ring(count, step):
    return [(i, (i + step) % count) for i in range(count)]


def slab_pairs(n_grp, n_wide, up, across):
    return [
        (g * n_wide + w, (g + across) % n_grp * n_wide + (w + up) % n_wide)
        for g in range(n_grp)
        for w in range(n_wide)
    ]


def local(fine_pop, coarse_pop, new_slot):
    k_count, q_count, cells = fine_pop.shape
    blocks = new_slot.shape[0]
    devices = blocks // k_count
    tiles = cells // LANES
    ch_count = tiles // B
    nq = ch_count * k_count
    axes = ("grp", "wide")
    n_grp, n_wide = lax.axis_size("grp"), lax.axis_size("wide")
    _, cx, cz, cy = coarse_pop.shape
    planes = cx + HALO
    fine_rows = B + 2 * HALO

    rows = pl.cdiv(Q * tiles, devices)
    pieces = fine_pop.reshape(k_count, Q, tiles, LANES)
    pieces = with_layout_constraint(pieces, Layout(major_to_minor=(1, 2, 0, 3)))
    pieces = pieces.transpose(1, 2, 0, 3)
    pieces = pieces.reshape(Q * tiles, k_count, LANES)
    if rows * devices != Q * tiles:
        pieces = jnp.pad(pieces, ((0, rows * devices - Q * tiles), (0, 0), (0, 0)))
    pieces = pieces.reshape(devices, rows, k_count, LANES)
    spread = lax.all_to_all(pieces, axes, 0, 0, tiled=True)
    edge = HALO // 2
    coarse_left = lax.ppermute(coarse_pop[:, cx - edge :], "grp", ring(n_grp, 1))
    coarse_right = lax.ppermute(coarse_pop[:, :edge], "grp", ring(n_grp, -1))
    last = coarse_pop[..., -1]
    below = []
    for part, across in ((last[:, cx - edge :], 1), (last, 0), (last[:, :edge], -1)):
        below.append(lax.ppermute(part, axes, slab_pairs(n_grp, n_wide, 1, across)))
    total = devices * rows * k_count
    regroup = call(
        functools.partial(regroup_body, blocks, k_count, rows),
        f32(total, LANES),
        [VMEM, VMEM],
        moved=8 * total * LANES,
    )
    targets = rows * new_slot - (rows - 1) * (new_slot % k_count)
    outgoing = regroup(targets[None], spread.reshape(total, LANES))
    arrived = lax.all_to_all(
        outgoing.reshape(devices, rows, k_count, LANES), axes, 0, 0, tiled=True
    )
    coarse = jnp.concatenate([coarse_left, coarse_pop, coarse_right], axis=1)
    below = jnp.concatenate(below, axis=1)
    layers = jnp.repeat(jnp.stack([below, coarse[..., 0]]), 2, axis=2)
    layers = layers.reshape(2, Q * fine_rows, cz)
    lane = jnp.arange(ch_count * LANES) // (2 * B)
    one_hot = (jnp.arange(cz)[:, None] == lane[None, :]).astype(jnp.float32)
    fine_ghosts, send_ghosts, rim_ghosts = call(
        functools.partial(fine_ghost_body, ch_count, fine_rows),
        [f32(2, NG, ch_count, n, LANES) for n in (fine_rows, SUB, SUB)],
        [VMEM, VMEM],
        [pltpu.VMEM((Q * fine_rows, ch_count * LANES), jnp.float32)],
    )(layers, one_hot)
    coarse_step, packed, near = call(
        functools.partial(coarse_body, planes),
        [f32(Q, cx, cz, cy), f32(Q, SUB, LANES), f32(SUB, LANES)],
        [VMEM],
        [
            pltpu.VMEM((10, planes, SUB, LANES), jnp.float32),
            pltpu.VMEM((Q, cx + 1, SUB, LANES), jnp.float32),
        ],
        flops=10**7,
    )(coarse)
    hidden = (fine_ghosts, send_ghosts, rim_ghosts, coarse_step, packed, near)
    arrived, hidden = lax.optimization_barrier((arrived, hidden))
    fine_ghosts, send_ghosts, rim_ghosts, coarse_step, packed, near = hidden
    own = arrived.reshape(total, LANES)[: Q * tiles * k_count]

    padded = PAD + fine_rows + PAD
    low, first = call(
        functools.partial(restrict_body, ch_count, k_count),
        [f32(PLANES, SUB, LANES)] * 2,
        [VMEM],
    )(own)
    to_left, to_right = call(
        functools.partial(send_body, ch_count, k_count),
        [f32(sent_rows(nq), LANES)] * 2,
        [VMEM] * 3,
        [
            pltpu.VMEM((Q, nq, SUB, LANES), jnp.float32),
            pltpu.VMEM((Q, nq, 3 * PAD, LANES), jnp.float32),
            pltpu.VMEM((10, nq, 3 * PAD, LANES), jnp.float32),
        ],
    )(own, send_ghosts, low)
    left = lax.ppermute(to_right, "grp", ring(n_grp, 1))
    right = lax.ppermute(to_left, "grp", ring(n_grp, -1))
    inner = call(
        functools.partial(inner_body, ch_count, k_count),
        f32(Q, nq, PAD + B + PAD, LANES),
        [VMEM] * 2,
        [pltpu.VMEM((10, nq, PAD + B + PAD, LANES), jnp.float32)],
        flops=10**7,
    )(own, fine_ghosts)
    highs = []
    for across in (0, 1, -1):
        highs.append(lax.ppermute(first, axes, slab_pairs(n_grp, n_wide, -1, across)))

    fine = call(
        functools.partial(fine_body, ch_count, k_count),
        f32(Q * B * nq, LANES),
        [VMEM] * 6,
        [
            pltpu.VMEM((Q * nq * SUB, LANES), jnp.float32),
            pltpu.VMEM((Q, nq, padded, LANES), jnp.float32),
            pltpu.VMEM((Q, nq, padded, LANES), jnp.float32),
            pltpu.VMEM((10, nq, padded, LANES), jnp.float32),
            pltpu.VMEM((Q * B * nq, LANES), jnp.float32),
            pltpu.SemaphoreType.DMA((PIECES,)),
        ],
        flops=10**7,
        place=HBM,
    )(own, left, right, inner, fine_ghosts, rim_ghosts)

    coarse_out = call(
        functools.partial(edges_body, ch_count, k_count, planes),
        f32(Q, cx, cz, cy),
        [VMEM] * 9,
        [
            pltpu.VMEM((PLANES, LANES, LANES), jnp.float32),
            pltpu.VMEM((PLANES, LANES, LANES), jnp.float32),
            pltpu.VMEM((Q, SUB, LANES), jnp.float32),
            pltpu.VMEM((Q, cx, cz, cy), jnp.float32),
            pltpu.SemaphoreType.DMA((PIECES,)),
        ],
        place=HBM,
    )(left, right, low, *highs, packed, near, coarse_step)

    fine_out = fine.reshape(Q, tiles, k_count, LANES).transpose(2, 0, 1, 3)
    fine_out = fine_out.reshape(k_count, q_count, cells)
    return fine_out, coarse_out


def solution(mesh):
    return jax.shard_map(
        local,
        mesh=mesh,
        in_specs=(P(("grp", "wide"), None, None), P(None, "grp", None, "wide"), P()),
        out_specs=(P(("grp", "wide"), None, None), P(None, "grp", None, "wide")),
        check_vma=False,
    )
```

```python
import functools

import jax
import jax.numpy as jnp
from jax import lax
from jax.experimental import pallas as pl
from jax.experimental.layout import Layout, with_layout_constraint
from jax.experimental.pallas import tpu as pltpu
from jax.sharding import PartitionSpec as P


B = 16
LANES = 128
SUB = 8
HALO = 4
PAD = 8
GRANT = 24 << 20
PIECES = 8

VELOCITIES = (
    (0, 0, 0),
    (1, 0, 0),
    (-1, 0, 0),
    (0, 1, 0),
    (0, -1, 0),
    (0, 0, 1),
    (0, 0, -1),
    (1, 1, 0),
    (-1, -1, 0),
    (1, -1, 0),
    (-1, 1, 0),
    (1, 0, 1),
    (-1, 0, -1),
    (1, 0, -1),
    (-1, 0, 1),
    (0, 1, 1),
    (0, -1, -1),
    (0, 1, -1),
    (0, -1, 1),
)
Q = len(VELOCITIES)
WEIGHTS = (1.0 / 3.0,) + (1.0 / 18.0,) * 6 + (1.0 / 36.0,) * 12
W_DIAG = WEIGHTS[7]
COUPLING = -5.0
FINE_TAU = 1.1
COARSE_TAU = 0.8
TO_COARSE = 2.0 * COARSE_TAU / FINE_TAU
TO_FINE = FINE_TAU / (2.0 * COARSE_TAU)
UP = tuple(i for i in range(Q) if VELOCITIES[i][1] == 1)
DOWN = tuple(i for i in range(Q) if VELOCITIES[i][1] == -1)
NG = len(UP) + 1

VMEM = pl.BlockSpec(memory_space=pltpu.VMEM)
HBM = pl.BlockSpec(memory_space=pl.ANY)


def call(body, outs, specs, scratch=(), flops=10**6, moved=10**6, place=VMEM):
    return pl.pallas_call(
        body,
        out_shape=outs,
        in_specs=specs,
        out_specs=jax.tree.map(lambda _: place, outs),
        scratch_shapes=list(scratch),
        cost_estimate=pl.CostEstimate(flops=flops, bytes_accessed=moved, transcendentals=0),
        compiler_params=pltpu.CompilerParams(vmem_limit_bytes=GRANT),
    )


def f32(*shape):
    return jax.ShapeDtypeStruct(shape, jnp.float32)


def moments(f):
    density = f[0]
    momentum = [None, None, None]
    for i in range(1, Q, 2):
        density = density + (f[i] + f[i + 1])
        odd = f[i] - f[i + 1]
        for j in range(3):
            c = VELOCITIES[i][j]
            if c:
                term = odd if c > 0 else -odd
                if momentum[j] is None:
                    momentum[j] = term
                else:
                    momentum[j] = momentum[j] + odd if c > 0 else momentum[j] - odd
    return density, momentum


def balances(density, flux, scale):
    w = density * (W_DIAG * scale)
    half = 1.5 / density
    v = [x * half for x in flux]
    g = [x * (3.0 * W_DIAG * scale) for x in flux]
    g2 = [x + x for x in g]
    h = [g[j] * v[j] for j in range(3)]
    total = h[0] + h[1] + h[2]
    base = w - total * (1.0 / 3.0)
    base2 = base + base
    yield 0, base2 * (0.5 * WEIGHTS[0] / W_DIAG)
    for j in range(3):
        even = base2 + (h[j] + h[j])
        yield 2 * j + 1, even + g2[j]
        yield 2 * j + 2, even - g2[j]
    all_h = base + total
    i = 7
    for a, b, c in ((0, 1, 2), (0, 2, 1), (1, 2, 0)):
        even = all_h - h[c]
        cross = g2[a] * v[b]
        for sign in (1, -1):
            side = even + cross if sign > 0 else even - cross
            odd = g[a] + g[b] if sign > 0 else g[a] - g[b]
            yield i, side + odd
            yield i + 1, side - odd
            i += 2


def rescaled(f, factor, wanted):
    density, momentum = moments(f)
    found = {}
    for i, balance in balances(density, momentum, 1.0):
        if i in wanted:
            found[i] = balance + factor * (f[i] - balance)
    return 1.0 - jnp.exp(-density), found


def gradient_parts(p, shift_y, shift_z):
    above = shift_y(p, -1, "p")
    below = shift_y(p, 1, "p")
    front = shift_z(p, -1)
    back = shift_z(p, 1)
    n = range(len(p))
    dy = [above[q] - below[q] for q in n]
    dz = [front[q] - back[q] for q in n]
    mixed = [(p[q] + p[q]) + (above[q] + below[q]) for q in n]
    tx = [mixed[q] + (front[q] + back[q]) for q in n]
    mixed_front = shift_z(mixed, -1)
    mixed_back = shift_z(mixed, 1)
    dy_front = shift_z(dy, -1)
    dy_back = shift_z(dy, 1)
    gy = [(dy[q] + dy[q]) + (dy_front[q] + dy_back[q]) for q in n]
    gz = [mixed_front[q] - mixed_back[q] for q in n]
    return tx, dy, dz, gy, gz


def flux_of(momentum, potential, pull, tau):
    force = (-tau * COUPLING * W_DIAG) * potential
    return [momentum[j] + force * pull[j] for j in range(3)]


def regroup_body(blocks, k_blocks, rows, target_ref, in_ref, out_ref):
    targets = target_ref[...]
    for b in range(blocks):
        source = (b // k_blocks) * (rows * k_blocks) + b % k_blocks
        out_ref[pl.ds(targets[0, b], rows, stride=k_blocks), :] = in_ref[
            pl.ds(source, rows, stride=k_blocks), :
        ]


def lane_ids():
    lane = lax.broadcasted_iota(jnp.int32, (SUB, LANES), 1)
    return lane % B, lane // B


def fine_shifts(ch_count, k_count, ghost):
    y, z = lane_ids()
    first_y, last_y = y == 0, y == B - 1
    first_z, last_z = z == 0, z == LANES // B - 1

    def shift_y(v, c, which):
        out = []
        for ch in range(ch_count):
            for k in range(k_count):
                q = ch * k_count + k
                if c > 0:
                    own = pltpu.roll(v[q], 1, 1)
                    carry = (
                        ghost(0, which, ch) if k == 0 else pltpu.roll(v[q - 1], LANES - (B - 1), 1)
                    )
                    out.append(jnp.where(first_y, carry, own))
                else:
                    own = pltpu.roll(v[q], LANES - 1, 1)
                    carry = (
                        ghost(1, which, ch)
                        if k == k_count - 1
                        else pltpu.roll(v[q + 1], B - 1, 1)
                    )
                    out.append(jnp.where(last_y, carry, own))
        return out

    def shift_z(v, c):
        rolled = [pltpu.roll(x, B if c > 0 else LANES - B, 1) for x in v]
        edge = first_z if c > 0 else last_z
        out = []
        for ch in range(ch_count):
            other = (ch - c) % ch_count
            for k in range(k_count):
                q = ch * k_count + k
                out.append(jnp.where(edge, rolled[other * k_count + k], rolled[q]))
        return out

    return shift_y, shift_z


def substep(load, store, ghosts, start, parts, ch_count, k_count, chunks, density_of=None):
    qs = range(ch_count * k_count)
    for chunk in range(chunks):
        r = chunk * SUB

        def ghost(side, which, ch, r=r):
            return ghosts[side, NG - 1, ch, pl.ds(start + r, SUB), :]

        moved = [moments([load(i, q, r) for i in range(Q)]) for q in qs]
        density = [moved[q][0] for q in qs]
        if density_of is not None:
            density = [density_of(q, r, density[q]) for q in qs]
        p = [1.0 - jnp.exp(-density[q]) for q in qs]
        shift_y, shift_z = fine_shifts(ch_count, k_count, ghost)
        tx, dy, dz, gy, gz = gradient_parts(p, shift_y, shift_z)
        for q in qs:
            values = (tx[q], dy[q], dz[q], gy[q], gz[q], p[q], density[q], *moved[q][1])
            for n, v in enumerate(values):
                parts[n, q, pl.ds(PAD + r, SUB), :] = v
    for chunk in range(chunks):
        r = chunk * SUB

        def ghost(side, which, ch, r=r):
            place = (UP if side == 0 else DOWN).index(which)
            return ghosts[side, place, ch, pl.ds(start + r, SUB), :]

        shift_y, shift_z = fine_shifts(ch_count, k_count, ghost)
        streams = []
        for q in qs:
            low = [parts[n, q, pl.ds(PAD + r - 1, SUB), :] for n in range(3)]
            high = [parts[n, q, pl.ds(PAD + r + 1, SUB), :] for n in range(3)]
            gy, gz, p, rho, mx, my, mz = (
                parts[n, q, pl.ds(PAD + r, SUB), :] for n in range(3, 10)
            )
            pull = [high[0] - low[0], gy + (high[1] + low[1]), gz + (high[2] + low[2])]
            flux = flux_of((mx, my, mz), p, pull, FINE_TAU)
            streams.append(balances(rho, flux, 1.0 / FINE_TAU))
        for i in range(Q):
            cx, cy, cz = VELOCITIES[i]
            post = []
            for q in qs:
                _, balance = next(streams[q])
                post.append(load(i, q, r) * (1.0 - 1.0 / FINE_TAU) + balance)
            if cy:
                post = shift_y(post, cy, i)
            if cz:
                post = shift_z(post, cz)
            for q in qs:
                store(i, q, r, cx, post[q])


CROSS = 5
FROM_DENSITY = Q
FROM_ENTER = Q + 1
FROM_PARTIAL = Q + 1 + CROSS
SENT = Q + 2 + CROSS


def edge_rows(nq):
    return SENT * nq + PLANES * (HALO // 2)


def sent_rows(nq):
    return -(-edge_rows(nq) // SUB) * SUB


def parts_of(count, pieces):
    cuts = [count * n // pieces for n in range(pieces + 1)]
    return list(zip(cuts[:-1], cuts[1:]))


def along(c):
    return [i for i in range(Q) if VELOCITIES[i][0] == c]


def restrict_body(ch_count, k_count, own, low, high):
    nq = ch_count * k_count

    def restricted(i, q, half):
        return own[pl.ds(i * (B * nq) + half * nq + q, SUB, stride=2 * nq), :]

    for side, out in enumerate((low, high)):
        for n, plane in enumerate(pack(restricted, ch_count, k_count, side)):
            out[n] = plane


def send_body(ch_count, k_count, own, ghosts, to_left, to_right, low, high, rim, moved, parts):
    nq = ch_count * k_count
    per = B * nq
    edge = HALO // 2

    for i in range(Q):
        for q in range(nq):
            rim[i, q, pl.ds(0, HALO), :] = own[pl.ds(i * per + q, HALO, stride=nq), :]
            rim[i, q, pl.ds(HALO, HALO), :] = own[
                pl.ds(i * per + (B - HALO) * nq + q, HALO, stride=nq), :
            ]

    def load(i, q, r):
        return rim[i, q]

    def store(i, q, r, cx, v):
        moved[i, q, pl.ds(PAD + cx, SUB), :] = v

    substep(load, store, ghosts, 0, parts, ch_count, k_count, 1)

    @pl.loop(0, 1)
    def _(_):
        restrict_body(ch_count, k_count, own, low, high)

    for c, out, outer in ((1, to_right, B - 1), (-1, to_left, 0)):
        first = PAD + (SUB - 1 if c > 0 else 0)
        second = first - c
        for i in range(Q):
            out[pl.ds(i * nq, nq), :] = own[pl.ds(i * per + outer * nq, nq), :]
        for q in range(nq):
            out[pl.ds(FROM_DENSITY * nq + q, 1), :] = parts[6, q, pl.ds(second, 1), :]
            for n, i in enumerate(along(c)):
                out[pl.ds((FROM_ENTER + n) * nq + q, 1), :] = moved[i, q, pl.ds(first, 1), :]
            total = None
            for i in along(0) + along(c):
                v = moved[i, q, pl.ds(second, 1), :]
                total = v if total is None else total + v
            out[pl.ds(FROM_PARTIAL * nq + q, 1), :] = total
        for n in range(PLANES):
            x = SUB - edge if c > 0 else 0
            out[pl.ds(SENT * nq + n * edge, edge), :] = low[n, pl.ds(x, edge), :]
        spare = sent_rows(nq) - edge_rows(nq)
        if spare:
            out[pl.ds(edge_rows(nq), spare), :] = jnp.zeros((spare, LANES), jnp.float32)


def inner_body(ch_count, k_count, own, ghosts, out, parts):
    nq = ch_count * k_count

    def load(i, q, r):
        return own[pl.ds(i * (B * nq) + r * nq + q, SUB, stride=nq), :]

    def store(i, q, r, cx, v):
        out[i, q, pl.ds(PAD + r + cx, SUB), :] = v

    substep(load, store, ghosts, HALO, parts, ch_count, k_count, B // SUB)


def fine_body(
    ch_count, k_count, own, left, right, inner, ghosts, rim_ghosts, out, rim, half, third, parts, held, sems
):
    nq = ch_count * k_count
    per = B * nq
    row = lax.broadcasted_iota(jnp.int32, (SUB, LANES), 0)
    origin = PAD + HALO

    layers = Q * nq
    rim[pl.ds(1, layers, stride=SUB), :] = left[pl.ds(0, layers), :]
    rim[pl.ds(6, layers, stride=SUB), :] = right[pl.ds(0, layers), :]
    for i in range(Q):
        for sub, x in ((2, 0), (3, 1), (4, B - 2), (5, B - 1)):
            rim[pl.ds(i * (nq * SUB) + sub, nq, stride=SUB), :] = own[
                pl.ds(i * per + x * nq, nq), :
            ]

    def spread(ref, plane, q):
        return jnp.broadcast_to(ref[pl.ds(plane * nq + q, 1), :], (SUB, LANES))

    def load_rim(i, q, r):
        return rim[pl.ds((i * nq + q) * SUB, SUB), :]

    def rim_density(q, r, density):
        density = jnp.where(row == 0, spread(left, FROM_DENSITY, q), density)
        return jnp.where(row == SUB - 1, spread(right, FROM_DENSITY, q), density)

    outgoing = {(c, q): None for c in (-1, 1) for q in range(nq)}

    def store_rim(i, q, r, cx, v):
        half[i, q, pl.ds(origin - 2 + cx, SUB), :] = v
        half[i, q, pl.ds(origin + B - 6 + cx, SUB), :] = v
        if cx:
            seen = outgoing[cx, q]
            outgoing[cx, q] = v if seen is None else seen + v

    substep(load_rim, store_rim, rim_ghosts, 0, parts, ch_count, k_count, 1, rim_density)
    for i in range(Q):
        cx = VELOCITIES[i][0]
        for q in range(nq):
            half[i, q, pl.ds(origin + 1 + cx, B - 2), :] = inner[i, q, pl.ds(PAD + 1 + cx, B - 2), :]
            if cx:
                ref = left if cx > 0 else right
                at = origin - 1 if cx > 0 else origin + B
                place = FROM_ENTER + along(cx).index(i)
                half[i, q, pl.ds(at, 1), :] = ref[pl.ds(place * nq + q, 1), :]

    def load(i, q, r):
        return half[i, q, pl.ds(PAD + r, SUB), :]

    def store(i, q, r, cx, v):
        third[i, q, pl.ds(PAD + r + cx, SUB), :] = v

    chunks = (B + 2 * HALO) // SUB

    def density_of(q, r, density):
        if r == 0:
            value = spread(left, FROM_PARTIAL, q) + pltpu.roll(outgoing[-1, q], 1, 0)
            return jnp.where(row == HALO - 2, value, density)
        if r == (chunks - 1) * SUB:
            value = spread(right, FROM_PARTIAL, q) + pltpu.roll(outgoing[1, q], SUB - 1, 0)
            return jnp.where(row == SUB - HALO + 1, value, density)
        return density

    substep(load, store, ghosts, 0, parts, ch_count, k_count, chunks, density_of)

    copies = []
    for n, (i0, i1) in enumerate(parts_of(Q, PIECES)):
        for i in range(i0, i1):
            for q in range(nq):
                held[pl.ds(i * per + q, B, stride=nq), :] = third[i, q, pl.ds(origin, B), :]
        part = pl.ds(i0 * per, (i1 - i0) * per)
        copies.append(pltpu.make_async_copy(held.at[part], out.at[part], sems.at[n]))
        copies[-1].start()
    for copy in copies:
        copy.wait()


def fine_ghost_body(ch_count, rows, layers, spread, out, send_ghosts, rim_ghosts, wide):
    for side in range(2):
        wide[...] = jnp.dot(
            layers[side],
            spread[...],
            precision=lax.Precision.HIGHEST,
            preferred_element_type=jnp.float32,
        )
        wanted = UP if side == 0 else DOWN
        for ch in range(ch_count):
            for r in range(0, rows, SUB):
                f = [
                    wide[pl.ds(i * rows + r, SUB), pl.ds(ch * LANES, LANES)] for i in range(Q)
                ]
                potential, found = rescaled(f, TO_FINE, wanted)
                for n, i in enumerate(wanted):
                    out[side, n, ch, pl.ds(r, SUB), :] = found[i]
                out[side, NG - 1, ch, pl.ds(r, SUB), :] = potential
            for n in range(NG):
                for ref, lower, upper in (
                    (send_ghosts, HALO, rows - 2 * HALO),
                    (rim_ghosts, 2, rows - HALO - 2),
                ):
                    ref[side, n, ch, pl.ds(0, HALO), :] = out[side, n, ch, pl.ds(lower, HALO), :]
                    ref[side, n, ch, pl.ds(HALO, HALO), :] = out[
                        side, n, ch, pl.ds(upper, HALO), :
                    ]


STEP = 2 * B
GROUP = B // 2
PLANES = -(-2 * Q // STEP)


def place_of(i, ch):
    group, at = divmod(2 * i + ch, GROUP)
    plane, quarter = divmod(group, 4)
    return plane, 2 * at + quarter % 2 + B * (quarter // 2)


def pack(load, ch_count, k_count, side):
    lane = lax.broadcasted_iota(jnp.int32, (SUB, LANES), 1)
    offset = B - 2 if side == 0 else 0
    layers = lane % B // 2 == offset // 2
    kept = (lane % STEP < B) & (lane % 2 == 0)
    k = k_count - 1 if side == 0 else 0
    slots = [(i, ch) for i in range(Q) for ch in range(ch_count)]
    planes = [None] * PLANES
    for first in range(0, len(slots), GROUP):
        total = None
        for at, (i, ch) in enumerate(slots[first : first + GROUP]):
            q = ch * k_count + k
            v = jnp.where(layers, load(i, q, 0) + load(i, q, 1), 0.0)
            shift = (2 * at - offset) % LANES
            if shift:
                v = pltpu.roll(v, shift, 1)
            total = v if total is None else total + v
        total = total + pltpu.roll(total, LANES - 1, 1)
        total = total + pltpu.roll(total, LANES - B, 1)
        total = jnp.where(kept, total, 0.0)
        plane, shift = place_of(*slots[first])
        if shift:
            total = pltpu.roll(total, shift, 1)
        planes[plane] = total if planes[plane] is None else planes[plane] + total
    return planes


def coarse_body(planes, state, out, packed, near, parts, out_pad):
    lane = lax.broadcasted_iota(jnp.int32, (SUB, LANES), 1)

    def shift_y(v, c, which):
        return [pltpu.roll(v[0], 1 if c > 0 else LANES - 1, 1)]

    def shift_z(v, c):
        return [pltpu.roll(v[0], 1 if c > 0 else SUB - 1, 0)]

    def prepare(x, carry):
        density, momentum = moments([state[i, x] for i in range(Q)])
        p = 1.0 - jnp.exp(-density)
        values = gradient_parts([p], shift_y, shift_z)
        values = [v[0] for v in values] + [p, density, *momentum]
        for n, v in enumerate(values):
            parts[n, x] = v
        return carry

    lax.fori_loop(0, planes, prepare, 0, unroll=2)

    inner = planes - HALO
    base = HALO // 2

    def update(x, carry):
        lower = [parts[n, x - 1] for n in range(3)]
        upper = [parts[n, x + 1] for n in range(3)]
        gy, gz, p, rho, mx, my, mz = (parts[n, x] for n in range(3, 10))
        pull = [upper[0] - lower[0], gy + (upper[1] + lower[1]), gz + (upper[2] + lower[2])]
        flux = flux_of((mx, my, mz), p, pull, COARSE_TAU)
        for i, balance in balances(rho, flux, 1.0 / COARSE_TAU):
            cx, cy, cz = VELOCITIES[i]
            post = [state[i, x] * (1.0 - 1.0 / COARSE_TAU) + balance]
            if cy:
                post = shift_y(post, cy, i)
            if cz:
                post = shift_z(post, cz)
            inside = x + cx - base
            spare = jnp.where((inside >= 0) & (inside < inner), inside, inner)
            out_pad[i, spare] = post[0]
        return carry

    lax.fori_loop(base - 1, base + inner + 1, update, 0, unroll=2)
    out[...] = out_pad[:, :inner]

    def gather(i, carry):
        total = jnp.zeros((SUB, LANES), jnp.float32)
        for x in range(planes):
            here = (lane == 2 * x + 1) | (lane == 2 * x + 2)
            total = jnp.where(here, pltpu.roll(state[i, x], 2 * x + 2, 1), total)
        packed[i] = total
        return carry

    lax.fori_loop(0, Q, gather, 0)
    total = jnp.zeros((SUB, LANES), jnp.float32)
    for x in range(planes):
        p = parts[5, x]
        total = jnp.where(lane == 2 * x + 2, pltpu.roll(p, 2 * x + 1, 1), total)
        total = jnp.where(lane == 2 * x + 1, pltpu.roll(p, 2 * x + 3, 1), total)
    near[...] = total


def edges_body(
    ch_count, k_count, planes, left, right, low, high, high_left, high_right, packed, near, step,
    out, rows, columns, ghost, held, sems,
):
    nq = ch_count * k_count
    edge = HALO // 2
    inner = planes - HALO
    lane = lax.broadcasted_iota(jnp.int32, (SUB, LANES), 1)
    sided = lane % 2 == 0

    for n in range(PLANES):
        own_x = 2 * edge
        rows[n, pl.ds(2 + own_x, inner, stride=2), :] = low[n]
        beside = SENT * nq + n * edge
        rows[n, pl.ds(2, edge, stride=2), :] = left[pl.ds(beside, edge), :]
        rows[n, pl.ds(2 + 2 * (edge + inner), edge, stride=2), :] = right[
            pl.ds(beside, edge), :
        ]
        rows[n, pl.ds(1 + own_x, inner, stride=2), :] = high[n]
        rows[n, pl.ds(1, edge, stride=2), :] = high_left[n, pl.ds(inner - edge, edge), :]
        rows[n, pl.ds(1 + 2 * (edge + inner), edge, stride=2), :] = high_right[
            n, pl.ds(0, edge), :
        ]
        columns[n, :, pl.ds(0, STEP)] = rows[n, pl.ds(0, STEP), :].T
    per = LANES // STEP
    for i in range(Q):
        for ch in range(ch_count):
            plane, at = place_of(i, ch)
            ghost[i, pl.ds(ch * per, per), :] = (
                0.125 * columns[plane, pl.ds(at, per, stride=STEP), :]
            )

    beyond, entering = rescaled([ghost[i] for i in range(Q)], TO_COARSE, UP + DOWN)
    density, momentum = moments([packed[i] for i in range(Q)])
    p = 1.0 - jnp.exp(-density)
    inside = near[...]
    above = jnp.where(sided, inside, beyond)
    below = jnp.where(sided, beyond, inside)

    def shift_y(v, c, which):
        return [below if c > 0 else above]

    def shift_z(v, c):
        return [pltpu.roll(v[0], 1 if c > 0 else SUB - 1, 0)]

    def shift_x(v, c):
        return pltpu.roll(v, 2 if c > 0 else LANES - 2, 1) if c else v

    tx, dy, dz, gy, gz = (v[0] for v in gradient_parts([p], shift_y, shift_z))
    pull = [
        shift_x(tx, -1) - shift_x(tx, 1),
        gy + (shift_x(dy, -1) + shift_x(dy, 1)),
        gz + (shift_x(dz, -1) + shift_x(dz, 1)),
    ]
    flux = flux_of(momentum, p, pull, COARSE_TAU)
    copies = []
    for i, balance in balances(density, flux, 1.0 / COARSE_TAU):
        cx, cy, cz = VELOCITIES[i]
        v = packed[i] * (1.0 - 1.0 / COARSE_TAU) + balance
        if cy > 0:
            v = jnp.where(sided, entering[i], pltpu.roll(v, 1, 1))
            touched = lane < 2
        elif cy < 0:
            v = jnp.where(sided, pltpu.roll(v, LANES - 1, 1), entering[i])
            touched = lane >= LANES - 2
        else:
            touched = (lane == 0) | (lane == LANES - 1)
        v = shift_x(v, cx)
        if cz:
            v = shift_z([v], cz)[0]
        for x in range(inner):
            column = pltpu.roll(v, LANES - (2 * (x + edge) + 2), 1)
            held[i, x] = jnp.where(touched, column, step[i, x])
        for n, (i0, i1) in enumerate(parts_of(Q, PIECES)):
            if i == i1 - 1:
                part = pl.ds(i0, i1 - i0)
                copies.append(pltpu.make_async_copy(held.at[part], out.at[part], sems.at[n]))
                copies[-1].start()
    for copy in copies:
        copy.wait()


def ring(count, step):
    return [(i, (i + step) % count) for i in range(count)]


def slab_pairs(n_grp, n_wide, up, across):
    return [
        (g * n_wide + w, (g + across) % n_grp * n_wide + (w + up) % n_wide)
        for g in range(n_grp)
        for w in range(n_wide)
    ]


def local(fine_pop, coarse_pop, new_slot):
    k_count, q_count, cells = fine_pop.shape
    blocks = new_slot.shape[0]
    devices = blocks // k_count
    tiles = cells // LANES
    ch_count = tiles // B
    nq = ch_count * k_count
    axes = ("grp", "wide")
    n_grp, n_wide = lax.axis_size("grp"), lax.axis_size("wide")
    _, cx, cz, cy = coarse_pop.shape
    planes = cx + HALO
    fine_rows = B + 2 * HALO

    rows = pl.cdiv(Q * tiles, devices)
    pieces = fine_pop.reshape(k_count, Q, tiles, LANES)
    pieces = with_layout_constraint(pieces, Layout(major_to_minor=(1, 2, 0, 3)))
    pieces = pieces.transpose(1, 2, 0, 3)
    pieces = pieces.reshape(Q * tiles, k_count, LANES)
    if rows * devices != Q * tiles:
        pieces = jnp.pad(pieces, ((0, rows * devices - Q * tiles), (0, 0), (0, 0)))
    pieces = pieces.reshape(devices, rows, k_count, LANES)
    spread = lax.all_to_all(pieces, axes, 0, 0, tiled=True)
    edge = HALO // 2
    coarse_left = lax.ppermute(coarse_pop[:, cx - edge :], "grp", ring(n_grp, 1))
    coarse_right = lax.ppermute(coarse_pop[:, :edge], "grp", ring(n_grp, -1))
    last = coarse_pop[..., -1]
    below = []
    for part, across in ((last[:, cx - edge :], 1), (last, 0), (last[:, :edge], -1)):
        below.append(lax.ppermute(part, axes, slab_pairs(n_grp, n_wide, 1, across)))
    total = devices * rows * k_count
    regroup = call(
        functools.partial(regroup_body, blocks, k_count, rows),
        f32(total, LANES),
        [VMEM, VMEM],
        moved=8 * total * LANES,
    )
    targets = rows * new_slot - (rows - 1) * (new_slot % k_count)
    outgoing = regroup(targets[None], spread.reshape(total, LANES))
    arrived = lax.all_to_all(
        outgoing.reshape(devices, rows, k_count, LANES), axes, 0, 0, tiled=True
    )
    coarse = jnp.concatenate([coarse_left, coarse_pop, coarse_right], axis=1)
    below = jnp.concatenate(below, axis=1)
    layers = jnp.repeat(jnp.stack([below, coarse[..., 0]]), 2, axis=2)
    layers = layers.reshape(2, Q * fine_rows, cz)
    lane = jnp.arange(ch_count * LANES) // (2 * B)
    one_hot = (jnp.arange(cz)[:, None] == lane[None, :]).astype(jnp.float32)
    fine_ghosts, send_ghosts, rim_ghosts = call(
        functools.partial(fine_ghost_body, ch_count, fine_rows),
        [f32(2, NG, ch_count, n, LANES) for n in (fine_rows, SUB, SUB)],
        [VMEM, VMEM],
        [pltpu.VMEM((Q * fine_rows, ch_count * LANES), jnp.float32)],
    )(layers, one_hot)
    coarse_step, packed, near = call(
        functools.partial(coarse_body, planes),
        [f32(Q, cx, cz, cy), f32(Q, SUB, LANES), f32(SUB, LANES)],
        [VMEM],
        [
            pltpu.VMEM((10, planes, SUB, LANES), jnp.float32),
            pltpu.VMEM((Q, cx + 1, SUB, LANES), jnp.float32),
        ],
        flops=10**7,
    )(coarse)
    hidden = (fine_ghosts, send_ghosts, rim_ghosts, coarse_step, packed, near)
    arrived, hidden = lax.optimization_barrier((arrived, hidden))
    fine_ghosts, send_ghosts, rim_ghosts, coarse_step, packed, near = hidden
    own = arrived.reshape(total, LANES)[: Q * tiles * k_count]

    padded = PAD + fine_rows + PAD
    to_left, to_right, low, first = call(
        functools.partial(send_body, ch_count, k_count),
        [f32(sent_rows(nq), LANES)] * 2 + [f32(PLANES, SUB, LANES)] * 2,
        [VMEM] * 2,
        [
            pltpu.VMEM((Q, nq, SUB, LANES), jnp.float32),
            pltpu.VMEM((Q, nq, 3 * PAD, LANES), jnp.float32),
            pltpu.VMEM((10, nq, 3 * PAD, LANES), jnp.float32),
        ],
    )(own, send_ghosts)
    left = lax.ppermute(to_right, "grp", ring(n_grp, 1))
    right = lax.ppermute(to_left, "grp", ring(n_grp, -1))
    inner = call(
        functools.partial(inner_body, ch_count, k_count),
        f32(Q, nq, PAD + B + PAD, LANES),
        [VMEM] * 2,
        [pltpu.VMEM((10, nq, PAD + B + PAD, LANES), jnp.float32)],
        flops=10**7,
    )(own, fine_ghosts)
    highs = []
    for across in (0, 1, -1):
        highs.append(lax.ppermute(first, axes, slab_pairs(n_grp, n_wide, -1, across)))

    fine = call(
        functools.partial(fine_body, ch_count, k_count),
        f32(Q * B * nq, LANES),
        [VMEM] * 6,
        [
            pltpu.VMEM((Q * nq * SUB, LANES), jnp.float32),
            pltpu.VMEM((Q, nq, padded, LANES), jnp.float32),
            pltpu.VMEM((Q, nq, padded, LANES), jnp.float32),
            pltpu.VMEM((10, nq, padded, LANES), jnp.float32),
            pltpu.VMEM((Q * B * nq, LANES), jnp.float32),
            pltpu.SemaphoreType.DMA((PIECES,)),
        ],
        flops=10**7,
        place=HBM,
    )(own, left, right, inner, fine_ghosts, rim_ghosts)

    coarse_out = call(
        functools.partial(edges_body, ch_count, k_count, planes),
        f32(Q, cx, cz, cy),
        [VMEM] * 9,
        [
            pltpu.VMEM((PLANES, LANES, LANES), jnp.float32),
            pltpu.VMEM((PLANES, LANES, LANES), jnp.float32),
            pltpu.VMEM((Q, SUB, LANES), jnp.float32),
            pltpu.VMEM((Q, cx, cz, cy), jnp.float32),
            pltpu.SemaphoreType.DMA((PIECES,)),
        ],
        place=HBM,
    )(left, right, low, *highs, packed, near, coarse_step)

    fine_out = fine.reshape(Q, tiles, k_count, LANES).transpose(2, 0, 1, 3)
    fine_out = fine_out.reshape(k_count, q_count, cells)
    return fine_out, coarse_out


def solution(mesh):
    return jax.shard_map(
        local,
        mesh=mesh,
        in_specs=(P(("grp", "wide"), None, None), P(None, "grp", None, "wide"), P()),
        out_specs=(P(("grp", "wide"), None, None), P(None, "grp", None, "wide")),
        check_vma=False,
    )
```

```python
import functools

import jax
import jax.numpy as jnp
from jax import lax
from jax.experimental import pallas as pl
from jax.experimental.layout import Layout, with_layout_constraint
from jax.experimental.pallas import tpu as pltpu
from jax.sharding import PartitionSpec as P


B = 16
LANES = 128
SUB = 8
HALO = 4
PAD = 8
GRANT = 24 << 20
PIECES = 8

VELOCITIES = (
    (0, 0, 0),
    (1, 0, 0),
    (-1, 0, 0),
    (0, 1, 0),
    (0, -1, 0),
    (0, 0, 1),
    (0, 0, -1),
    (1, 1, 0),
    (-1, -1, 0),
    (1, -1, 0),
    (-1, 1, 0),
    (1, 0, 1),
    (-1, 0, -1),
    (1, 0, -1),
    (-1, 0, 1),
    (0, 1, 1),
    (0, -1, -1),
    (0, 1, -1),
    (0, -1, 1),
)
Q = len(VELOCITIES)
WEIGHTS = (1.0 / 3.0,) + (1.0 / 18.0,) * 6 + (1.0 / 36.0,) * 12
W_DIAG = WEIGHTS[7]
COUPLING = -5.0
FINE_TAU = 1.1
COARSE_TAU = 0.8
TO_COARSE = 2.0 * COARSE_TAU / FINE_TAU
TO_FINE = FINE_TAU / (2.0 * COARSE_TAU)
UP = tuple(i for i in range(Q) if VELOCITIES[i][1] == 1)
DOWN = tuple(i for i in range(Q) if VELOCITIES[i][1] == -1)
NG = len(UP) + 1

VMEM = pl.BlockSpec(memory_space=pltpu.VMEM)
HBM = pl.BlockSpec(memory_space=pl.ANY)


def call(body, outs, specs, scratch=(), flops=10**6, moved=10**6, place=VMEM):
    return pl.pallas_call(
        body,
        out_shape=outs,
        in_specs=specs,
        out_specs=jax.tree.map(lambda _: place, outs),
        scratch_shapes=list(scratch),
        cost_estimate=pl.CostEstimate(flops=flops, bytes_accessed=moved, transcendentals=0),
        compiler_params=pltpu.CompilerParams(vmem_limit_bytes=GRANT),
    )


def f32(*shape):
    return jax.ShapeDtypeStruct(shape, jnp.float32)


def moments(f):
    density = f[0]
    momentum = [None, None, None]
    for i in range(1, Q, 2):
        density = density + (f[i] + f[i + 1])
        odd = f[i] - f[i + 1]
        for j in range(3):
            c = VELOCITIES[i][j]
            if c:
                term = odd if c > 0 else -odd
                if momentum[j] is None:
                    momentum[j] = term
                else:
                    momentum[j] = momentum[j] + odd if c > 0 else momentum[j] - odd
    return density, momentum


def balances(density, flux, scale):
    w = density * (W_DIAG * scale)
    half = 1.5 / density
    v = [x * half for x in flux]
    g = [x * (3.0 * W_DIAG * scale) for x in flux]
    g2 = [x + x for x in g]
    h = [g[j] * v[j] for j in range(3)]
    total = h[0] + h[1] + h[2]
    base = w - total * (1.0 / 3.0)
    base2 = base + base
    yield 0, base2 * (0.5 * WEIGHTS[0] / W_DIAG)
    for j in range(3):
        even = base2 + (h[j] + h[j])
        yield 2 * j + 1, even + g2[j]
        yield 2 * j + 2, even - g2[j]
    all_h = base + total
    i = 7
    for a, b, c in ((0, 1, 2), (0, 2, 1), (1, 2, 0)):
        even = all_h - h[c]
        cross = g2[a] * v[b]
        for sign in (1, -1):
            side = even + cross if sign > 0 else even - cross
            odd = g[a] + g[b] if sign > 0 else g[a] - g[b]
            yield i, side + odd
            yield i + 1, side - odd
            i += 2


def rescaled(f, factor, wanted):
    density, momentum = moments(f)
    found = {}
    for i, balance in balances(density, momentum, 1.0):
        if i in wanted:
            found[i] = balance + factor * (f[i] - balance)
    return 1.0 - jnp.exp(-density), found


def gradient_parts(p, shift_y, shift_z):
    above = shift_y(p, -1, "p")
    below = shift_y(p, 1, "p")
    front = shift_z(p, -1)
    back = shift_z(p, 1)
    n = range(len(p))
    dy = [above[q] - below[q] for q in n]
    dz = [front[q] - back[q] for q in n]
    mixed = [(p[q] + p[q]) + (above[q] + below[q]) for q in n]
    tx = [mixed[q] + (front[q] + back[q]) for q in n]
    mixed_front = shift_z(mixed, -1)
    mixed_back = shift_z(mixed, 1)
    dy_front = shift_z(dy, -1)
    dy_back = shift_z(dy, 1)
    gy = [(dy[q] + dy[q]) + (dy_front[q] + dy_back[q]) for q in n]
    gz = [mixed_front[q] - mixed_back[q] for q in n]
    return tx, dy, dz, gy, gz


def flux_of(momentum, potential, pull, tau):
    force = (-tau * COUPLING * W_DIAG) * potential
    return [momentum[j] + force * pull[j] for j in range(3)]


def regroup_body(blocks, k_blocks, rows, target_ref, in_ref, out_ref):
    targets = target_ref[...]
    for b in range(blocks):
        source = (b // k_blocks) * (rows * k_blocks) + b % k_blocks
        out_ref[pl.ds(targets[0, b], rows, stride=k_blocks), :] = in_ref[
            pl.ds(source, rows, stride=k_blocks), :
        ]


def lane_ids():
    lane = lax.broadcasted_iota(jnp.int32, (SUB, LANES), 1)
    return lane % B, lane // B


def fine_shifts(ch_count, k_count, ghost):
    y, z = lane_ids()
    first_y, last_y = y == 0, y == B - 1
    first_z, last_z = z == 0, z == LANES // B - 1

    def shift_y(v, c, which):
        out = []
        for ch in range(ch_count):
            for k in range(k_count):
                q = ch * k_count + k
                if c > 0:
                    own = pltpu.roll(v[q], 1, 1)
                    carry = (
                        ghost(0, which, ch) if k == 0 else pltpu.roll(v[q - 1], LANES - (B - 1), 1)
                    )
                    out.append(jnp.where(first_y, carry, own))
                else:
                    own = pltpu.roll(v[q], LANES - 1, 1)
                    carry = (
                        ghost(1, which, ch)
                        if k == k_count - 1
                        else pltpu.roll(v[q + 1], B - 1, 1)
                    )
                    out.append(jnp.where(last_y, carry, own))
        return out

    def shift_z(v, c):
        rolled = [pltpu.roll(x, B if c > 0 else LANES - B, 1) for x in v]
        edge = first_z if c > 0 else last_z
        out = []
        for ch in range(ch_count):
            other = (ch - c) % ch_count
            for k in range(k_count):
                q = ch * k_count + k
                out.append(jnp.where(edge, rolled[other * k_count + k], rolled[q]))
        return out

    def shift_both(v, cy, cz, which):
        edge_y = first_y if cy > 0 else last_y
        edge_z = first_z if cz > 0 else last_z
        turn = B * cz
        moved = []
        for ch in range(ch_count):
            for k in range(k_count):
                q = ch * k_count + k
                own = pltpu.roll(v[q], (turn + cy) % LANES, 1)
                if k == (0 if cy > 0 else k_count - 1):
                    carry = pltpu.roll(ghost(0 if cy > 0 else 1, which, ch), turn % LANES, 1)
                else:
                    carry = pltpu.roll(v[q - cy], (turn - cy * (B - 1)) % LANES, 1)
                moved.append(jnp.where(edge_y, carry, own))
        return [
            jnp.where(edge_z, moved[(ch - cz) % ch_count * k_count + k], moved[ch * k_count + k])
            for ch in range(ch_count)
            for k in range(k_count)
        ]

    return shift_y, shift_z, shift_both


def substep(load, store, ghosts, start, parts, ch_count, k_count, chunks, density_of=None):
    qs = range(ch_count * k_count)
    for chunk in range(chunks):
        r = chunk * SUB

        def ghost(side, which, ch, r=r):
            return ghosts[side, NG - 1, ch, pl.ds(start + r, SUB), :]

        moved = [moments([load(i, q, r) for i in range(Q)]) for q in qs]
        density = [moved[q][0] for q in qs]
        if density_of is not None:
            density = [density_of(q, r, density[q]) for q in qs]
        p = [1.0 - jnp.exp(-density[q]) for q in qs]
        shift_y, shift_z, shift_both = fine_shifts(ch_count, k_count, ghost)
        tx, dy, dz, gy, gz = gradient_parts(p, shift_y, shift_z)
        for q in qs:
            values = (tx[q], dy[q], dz[q], gy[q], gz[q], p[q], density[q], *moved[q][1])
            for n, v in enumerate(values):
                parts[n, q, pl.ds(PAD + r, SUB), :] = v
    for chunk in range(chunks):
        r = chunk * SUB

        def ghost(side, which, ch, r=r):
            place = (UP if side == 0 else DOWN).index(which)
            return ghosts[side, place, ch, pl.ds(start + r, SUB), :]

        shift_y, shift_z, shift_both = fine_shifts(ch_count, k_count, ghost)
        streams = []
        for q in qs:
            low = [parts[n, q, pl.ds(PAD + r - 1, SUB), :] for n in range(3)]
            high = [parts[n, q, pl.ds(PAD + r + 1, SUB), :] for n in range(3)]
            gy, gz, p, rho, mx, my, mz = (
                parts[n, q, pl.ds(PAD + r, SUB), :] for n in range(3, 10)
            )
            pull = [high[0] - low[0], gy + (high[1] + low[1]), gz + (high[2] + low[2])]
            flux = flux_of((mx, my, mz), p, pull, FINE_TAU)
            streams.append(balances(rho, flux, 1.0 / FINE_TAU))
        for i in range(Q):
            cx, cy, cz = VELOCITIES[i]
            post = []
            for q in qs:
                _, balance = next(streams[q])
                post.append(load(i, q, r) * (1.0 - 1.0 / FINE_TAU) + balance)
            if cy and cz:
                post = shift_both(post, cy, cz, i)
            elif cy:
                post = shift_y(post, cy, i)
            elif cz:
                post = shift_z(post, cz)
            for q in qs:
                store(i, q, r, cx, post[q])


CROSS = 5
FROM_DENSITY = Q
FROM_ENTER = Q + 1
FROM_PARTIAL = Q + 1 + CROSS
SENT = Q + 2 + CROSS


def edge_rows(nq):
    return SENT * nq + PLANES * (HALO // 2)


def sent_rows(nq):
    return -(-edge_rows(nq) // SUB) * SUB


def parts_of(count, pieces):
    cuts = [count * n // pieces for n in range(pieces + 1)]
    return list(zip(cuts[:-1], cuts[1:]))


def along(c):
    return [i for i in range(Q) if VELOCITIES[i][0] == c]


def restrict_body(ch_count, k_count, own, low, high):
    nq = ch_count * k_count

    def restricted(i, q, half):
        return own[pl.ds(i * (B * nq) + half * nq + q, SUB, stride=2 * nq), :]

    for side, out in enumerate((low, high)):
        for n, plane in enumerate(pack(restricted, ch_count, k_count, side)):
            out[n] = plane


def send_body(ch_count, k_count, own, ghosts, to_left, to_right, low, high, rim, moved, parts):
    nq = ch_count * k_count
    per = B * nq
    edge = HALO // 2

    for i in range(Q):
        for q in range(nq):
            rim[i, q, pl.ds(0, HALO), :] = own[pl.ds(i * per + q, HALO, stride=nq), :]
            rim[i, q, pl.ds(HALO, HALO), :] = own[
                pl.ds(i * per + (B - HALO) * nq + q, HALO, stride=nq), :
            ]

    def load(i, q, r):
        return rim[i, q]

    def store(i, q, r, cx, v):
        moved[i, q, pl.ds(PAD + cx, SUB), :] = v

    substep(load, store, ghosts, 0, parts, ch_count, k_count, 1)

    @pl.loop(0, 1)
    def _(_):
        restrict_body(ch_count, k_count, own, low, high)

    for c, out, outer in ((1, to_right, B - 1), (-1, to_left, 0)):
        first = PAD + (SUB - 1 if c > 0 else 0)
        second = first - c
        for i in range(Q):
            out[pl.ds(i * nq, nq), :] = own[pl.ds(i * per + outer * nq, nq), :]
        for q in range(nq):
            out[pl.ds(FROM_DENSITY * nq + q, 1), :] = parts[6, q, pl.ds(second, 1), :]
            for n, i in enumerate(along(c)):
                out[pl.ds((FROM_ENTER + n) * nq + q, 1), :] = moved[i, q, pl.ds(first, 1), :]
            total = None
            for i in along(0) + along(c):
                v = moved[i, q, pl.ds(second, 1), :]
                total = v if total is None else total + v
            out[pl.ds(FROM_PARTIAL * nq + q, 1), :] = total
        for n in range(PLANES):
            x = SUB - edge if c > 0 else 0
            out[pl.ds(SENT * nq + n * edge, edge), :] = low[n, pl.ds(x, edge), :]
        spare = sent_rows(nq) - edge_rows(nq)
        if spare:
            out[pl.ds(edge_rows(nq), spare), :] = jnp.zeros((spare, LANES), jnp.float32)


def inner_body(ch_count, k_count, own, ghosts, out, parts):
    nq = ch_count * k_count

    def load(i, q, r):
        return own[pl.ds(i * (B * nq) + r * nq + q, SUB, stride=nq), :]

    def store(i, q, r, cx, v):
        out[i, q, pl.ds(PAD + r + cx, SUB), :] = v

    substep(load, store, ghosts, HALO, parts, ch_count, k_count, B // SUB)


def fine_body(
    ch_count, k_count, own, left, right, inner, ghosts, rim_ghosts, out, rim, half, third, parts, held, sems
):
    nq = ch_count * k_count
    per = B * nq
    row = lax.broadcasted_iota(jnp.int32, (SUB, LANES), 0)
    origin = PAD + HALO

    layers = Q * nq
    rim[pl.ds(1, layers, stride=SUB), :] = left[pl.ds(0, layers), :]
    rim[pl.ds(6, layers, stride=SUB), :] = right[pl.ds(0, layers), :]
    for i in range(Q):
        for sub, x in ((2, 0), (3, 1), (4, B - 2), (5, B - 1)):
            rim[pl.ds(i * (nq * SUB) + sub, nq, stride=SUB), :] = own[
                pl.ds(i * per + x * nq, nq), :
            ]

    def spread(ref, plane, q):
        return jnp.broadcast_to(ref[pl.ds(plane * nq + q, 1), :], (SUB, LANES))

    def load_rim(i, q, r):
        return rim[pl.ds((i * nq + q) * SUB, SUB), :]

    def rim_density(q, r, density):
        density = jnp.where(row == 0, spread(left, FROM_DENSITY, q), density)
        return jnp.where(row == SUB - 1, spread(right, FROM_DENSITY, q), density)

    outgoing = {(c, q): None for c in (-1, 1) for q in range(nq)}

    def store_rim(i, q, r, cx, v):
        half[i, q, pl.ds(origin - 2 + cx, SUB), :] = v
        half[i, q, pl.ds(origin + B - 6 + cx, SUB), :] = v
        if cx:
            seen = outgoing[cx, q]
            outgoing[cx, q] = v if seen is None else seen + v

    substep(load_rim, store_rim, rim_ghosts, 0, parts, ch_count, k_count, 1, rim_density)
    for i in range(Q):
        cx = VELOCITIES[i][0]
        for q in range(nq):
            half[i, q, pl.ds(origin + 1 + cx, B - 2), :] = inner[i, q, pl.ds(PAD + 1 + cx, B - 2), :]
            if cx:
                ref = left if cx > 0 else right
                at = origin - 1 if cx > 0 else origin + B
                place = FROM_ENTER + along(cx).index(i)
                half[i, q, pl.ds(at, 1), :] = ref[pl.ds(place * nq + q, 1), :]

    def load(i, q, r):
        return half[i, q, pl.ds(PAD + r, SUB), :]

    def store(i, q, r, cx, v):
        third[i, q, pl.ds(PAD + r + cx, SUB), :] = v

    chunks = (B + 2 * HALO) // SUB

    def density_of(q, r, density):
        if r == 0:
            value = spread(left, FROM_PARTIAL, q) + pltpu.roll(outgoing[-1, q], 1, 0)
            return jnp.where(row == HALO - 2, value, density)
        if r == (chunks - 1) * SUB:
            value = spread(right, FROM_PARTIAL, q) + pltpu.roll(outgoing[1, q], SUB - 1, 0)
            return jnp.where(row == SUB - HALO + 1, value, density)
        return density

    substep(load, store, ghosts, 0, parts, ch_count, k_count, chunks, density_of)

    copies = []
    for n, (i0, i1) in enumerate(parts_of(Q, PIECES)):
        for i in range(i0, i1):
            for q in range(nq):
                held[pl.ds(i * per + q, B, stride=nq), :] = third[i, q, pl.ds(origin, B), :]
        part = pl.ds(i0 * per, (i1 - i0) * per)
        copies.append(pltpu.make_async_copy(held.at[part], out.at[part], sems.at[n]))
        copies[-1].start()
    for copy in copies:
        copy.wait()


def fine_ghost_body(ch_count, rows, layers, spread, out, send_ghosts, rim_ghosts, wide):
    for side in range(2):
        wide[...] = jnp.dot(
            layers[side],
            spread[...],
            precision=lax.Precision.HIGHEST,
            preferred_element_type=jnp.float32,
        )
        wanted = UP if side == 0 else DOWN
        for ch in range(ch_count):
            for r in range(0, rows, SUB):
                f = [
                    wide[pl.ds(i * rows + r, SUB), pl.ds(ch * LANES, LANES)] for i in range(Q)
                ]
                potential, found = rescaled(f, TO_FINE, wanted)
                for n, i in enumerate(wanted):
                    out[side, n, ch, pl.ds(r, SUB), :] = found[i]
                out[side, NG - 1, ch, pl.ds(r, SUB), :] = potential
            for n in range(NG):
                for ref, lower, upper in (
                    (send_ghosts, HALO, rows - 2 * HALO),
                    (rim_ghosts, 2, rows - HALO - 2),
                ):
                    ref[side, n, ch, pl.ds(0, HALO), :] = out[side, n, ch, pl.ds(lower, HALO), :]
                    ref[side, n, ch, pl.ds(HALO, HALO), :] = out[
                        side, n, ch, pl.ds(upper, HALO), :
                    ]


STEP = 2 * B
GROUP = B // 2
PLANES = -(-2 * Q // STEP)


def place_of(i, ch):
    group, at = divmod(2 * i + ch, GROUP)
    plane, quarter = divmod(group, 4)
    return plane, 2 * at + quarter % 2 + B * (quarter // 2)


def pack(load, ch_count, k_count, side):
    lane = lax.broadcasted_iota(jnp.int32, (SUB, LANES), 1)
    offset = B - 2 if side == 0 else 0
    layers = lane % B // 2 == offset // 2
    kept = (lane % STEP < B) & (lane % 2 == 0)
    k = k_count - 1 if side == 0 else 0
    slots = [(i, ch) for i in range(Q) for ch in range(ch_count)]
    planes = [None] * PLANES
    for first in range(0, len(slots), GROUP):
        total = None
        for at, (i, ch) in enumerate(slots[first : first + GROUP]):
            q = ch * k_count + k
            v = jnp.where(layers, load(i, q, 0) + load(i, q, 1), 0.0)
            shift = (2 * at - offset) % LANES
            if shift:
                v = pltpu.roll(v, shift, 1)
            total = v if total is None else total + v
        total = total + pltpu.roll(total, LANES - 1, 1)
        total = total + pltpu.roll(total, LANES - B, 1)
        total = jnp.where(kept, total, 0.0)
        plane, shift = place_of(*slots[first])
        if shift:
            total = pltpu.roll(total, shift, 1)
        planes[plane] = total if planes[plane] is None else planes[plane] + total
    return planes


def coarse_body(planes, state, out, packed, near, parts, out_pad):
    lane = lax.broadcasted_iota(jnp.int32, (SUB, LANES), 1)

    def shift_y(v, c, which):
        return [pltpu.roll(v[0], 1 if c > 0 else LANES - 1, 1)]

    def shift_z(v, c):
        return [pltpu.roll(v[0], 1 if c > 0 else SUB - 1, 0)]

    def prepare(x, carry):
        density, momentum = moments([state[i, x] for i in range(Q)])
        p = 1.0 - jnp.exp(-density)
        values = gradient_parts([p], shift_y, shift_z)
        values = [v[0] for v in values] + [p, density, *momentum]
        for n, v in enumerate(values):
            parts[n, x] = v
        return carry

    lax.fori_loop(0, planes, prepare, 0, unroll=2)

    inner = planes - HALO
    base = HALO // 2

    def update(x, carry):
        lower = [parts[n, x - 1] for n in range(3)]
        upper = [parts[n, x + 1] for n in range(3)]
        gy, gz, p, rho, mx, my, mz = (parts[n, x] for n in range(3, 10))
        pull = [upper[0] - lower[0], gy + (upper[1] + lower[1]), gz + (upper[2] + lower[2])]
        flux = flux_of((mx, my, mz), p, pull, COARSE_TAU)
        for i, balance in balances(rho, flux, 1.0 / COARSE_TAU):
            cx, cy, cz = VELOCITIES[i]
            post = [state[i, x] * (1.0 - 1.0 / COARSE_TAU) + balance]
            if cy:
                post = shift_y(post, cy, i)
            if cz:
                post = shift_z(post, cz)
            inside = x + cx - base
            spare = jnp.where((inside >= 0) & (inside < inner), inside, inner)
            out_pad[i, spare] = post[0]
        return carry

    lax.fori_loop(base - 1, base + inner + 1, update, 0, unroll=2)
    out[...] = out_pad[:, :inner]

    def gather(i, carry):
        total = jnp.zeros((SUB, LANES), jnp.float32)
        for x in range(planes):
            here = (lane == 2 * x + 1) | (lane == 2 * x + 2)
            total = jnp.where(here, pltpu.roll(state[i, x], 2 * x + 2, 1), total)
        packed[i] = total
        return carry

    lax.fori_loop(0, Q, gather, 0)
    total = jnp.zeros((SUB, LANES), jnp.float32)
    for x in range(planes):
        p = parts[5, x]
        total = jnp.where(lane == 2 * x + 2, pltpu.roll(p, 2 * x + 1, 1), total)
        total = jnp.where(lane == 2 * x + 1, pltpu.roll(p, 2 * x + 3, 1), total)
    near[...] = total


def edges_body(
    ch_count, k_count, planes, left, right, low, high, high_left, high_right, packed, near, step,
    out, rows, columns, ghost, held, sems,
):
    nq = ch_count * k_count
    edge = HALO // 2
    inner = planes - HALO
    lane = lax.broadcasted_iota(jnp.int32, (SUB, LANES), 1)
    sided = lane % 2 == 0

    for n in range(PLANES):
        own_x = 2 * edge
        rows[n, pl.ds(2 + own_x, inner, stride=2), :] = low[n]
        beside = SENT * nq + n * edge
        rows[n, pl.ds(2, edge, stride=2), :] = left[pl.ds(beside, edge), :]
        rows[n, pl.ds(2 + 2 * (edge + inner), edge, stride=2), :] = right[
            pl.ds(beside, edge), :
        ]
        rows[n, pl.ds(1 + own_x, inner, stride=2), :] = high[n]
        rows[n, pl.ds(1, edge, stride=2), :] = high_left[n, pl.ds(inner - edge, edge), :]
        rows[n, pl.ds(1 + 2 * (edge + inner), edge, stride=2), :] = high_right[
            n, pl.ds(0, edge), :
        ]
        columns[n, :, pl.ds(0, STEP)] = rows[n, pl.ds(0, STEP), :].T
    per = LANES // STEP
    for i in range(Q):
        for ch in range(ch_count):
            plane, at = place_of(i, ch)
            ghost[i, pl.ds(ch * per, per), :] = (
                0.125 * columns[plane, pl.ds(at, per, stride=STEP), :]
            )

    beyond, entering = rescaled([ghost[i] for i in range(Q)], TO_COARSE, UP + DOWN)
    density, momentum = moments([packed[i] for i in range(Q)])
    p = 1.0 - jnp.exp(-density)
    inside = near[...]
    above = jnp.where(sided, inside, beyond)
    below = jnp.where(sided, beyond, inside)

    def shift_y(v, c, which):
        return [below if c > 0 else above]

    def shift_z(v, c):
        return [pltpu.roll(v[0], 1 if c > 0 else SUB - 1, 0)]

    def shift_x(v, c):
        return pltpu.roll(v, 2 if c > 0 else LANES - 2, 1) if c else v

    tx, dy, dz, gy, gz = (v[0] for v in gradient_parts([p], shift_y, shift_z))
    pull = [
        shift_x(tx, -1) - shift_x(tx, 1),
        gy + (shift_x(dy, -1) + shift_x(dy, 1)),
        gz + (shift_x(dz, -1) + shift_x(dz, 1)),
    ]
    flux = flux_of(momentum, p, pull, COARSE_TAU)
    copies = []
    for i, balance in balances(density, flux, 1.0 / COARSE_TAU):
        cx, cy, cz = VELOCITIES[i]
        v = packed[i] * (1.0 - 1.0 / COARSE_TAU) + balance
        if cy > 0:
            v = jnp.where(sided, entering[i], pltpu.roll(v, 1, 1))
            touched = lane < 2
        elif cy < 0:
            v = jnp.where(sided, pltpu.roll(v, LANES - 1, 1), entering[i])
            touched = lane >= LANES - 2
        else:
            touched = (lane == 0) | (lane == LANES - 1)
        v = shift_x(v, cx)
        if cz:
            v = shift_z([v], cz)[0]
        for x in range(inner):
            column = pltpu.roll(v, LANES - (2 * (x + edge) + 2), 1)
            held[i, x] = jnp.where(touched, column, step[i, x])
        for n, (i0, i1) in enumerate(parts_of(Q, PIECES)):
            if i == i1 - 1:
                part = pl.ds(i0, i1 - i0)
                copies.append(pltpu.make_async_copy(held.at[part], out.at[part], sems.at[n]))
                copies[-1].start()
    for copy in copies:
        copy.wait()


def ring(count, step):
    return [(i, (i + step) % count) for i in range(count)]


def slab_pairs(n_grp, n_wide, up, across):
    return [
        (g * n_wide + w, (g + across) % n_grp * n_wide + (w + up) % n_wide)
        for g in range(n_grp)
        for w in range(n_wide)
    ]


def local(fine_pop, coarse_pop, new_slot):
    k_count, q_count, cells = fine_pop.shape
    blocks = new_slot.shape[0]
    devices = blocks // k_count
    tiles = cells // LANES
    ch_count = tiles // B
    nq = ch_count * k_count
    axes = ("grp", "wide")
    n_grp, n_wide = lax.axis_size("grp"), lax.axis_size("wide")
    _, cx, cz, cy = coarse_pop.shape
    planes = cx + HALO
    fine_rows = B + 2 * HALO

    rows = pl.cdiv(Q * tiles, devices)
    pieces = fine_pop.reshape(k_count, Q, tiles, LANES)
    pieces = with_layout_constraint(pieces, Layout(major_to_minor=(1, 2, 0, 3)))
    pieces = pieces.transpose(1, 2, 0, 3)
    pieces = pieces.reshape(Q * tiles, k_count, LANES)
    if rows * devices != Q * tiles:
        pieces = jnp.pad(pieces, ((0, rows * devices - Q * tiles), (0, 0), (0, 0)))
    pieces = pieces.reshape(devices, rows, k_count, LANES)
    spread = lax.all_to_all(pieces, axes, 0, 0, tiled=True)
    edge = HALO // 2
    coarse_left = lax.ppermute(coarse_pop[:, cx - edge :], "grp", ring(n_grp, 1))
    coarse_right = lax.ppermute(coarse_pop[:, :edge], "grp", ring(n_grp, -1))
    last = coarse_pop[..., -1]
    below = []
    for part, across in ((last[:, cx - edge :], 1), (last, 0), (last[:, :edge], -1)):
        below.append(lax.ppermute(part, axes, slab_pairs(n_grp, n_wide, 1, across)))
    total = devices * rows * k_count
    regroup = call(
        functools.partial(regroup_body, blocks, k_count, rows),
        f32(total, LANES),
        [VMEM, VMEM],
        moved=8 * total * LANES,
    )
    targets = rows * new_slot - (rows - 1) * (new_slot % k_count)
    outgoing = regroup(targets[None], spread.reshape(total, LANES))
    arrived = lax.all_to_all(
        outgoing.reshape(devices, rows, k_count, LANES), axes, 0, 0, tiled=True
    )
    coarse = jnp.concatenate([coarse_left, coarse_pop, coarse_right], axis=1)
    below = jnp.concatenate(below, axis=1)
    layers = jnp.repeat(jnp.stack([below, coarse[..., 0]]), 2, axis=2)
    layers = layers.reshape(2, Q * fine_rows, cz)
    lane = jnp.arange(ch_count * LANES) // (2 * B)
    one_hot = (jnp.arange(cz)[:, None] == lane[None, :]).astype(jnp.float32)
    fine_ghosts, send_ghosts, rim_ghosts = call(
        functools.partial(fine_ghost_body, ch_count, fine_rows),
        [f32(2, NG, ch_count, n, LANES) for n in (fine_rows, SUB, SUB)],
        [VMEM, VMEM],
        [pltpu.VMEM((Q * fine_rows, ch_count * LANES), jnp.float32)],
    )(layers, one_hot)
    coarse_step, packed, near = call(
        functools.partial(coarse_body, planes),
        [f32(Q, cx, cz, cy), f32(Q, SUB, LANES), f32(SUB, LANES)],
        [VMEM],
        [
            pltpu.VMEM((10, planes, SUB, LANES), jnp.float32),
            pltpu.VMEM((Q, cx + 1, SUB, LANES), jnp.float32),
        ],
        flops=10**7,
    )(coarse)
    hidden = (fine_ghosts, send_ghosts, rim_ghosts, coarse_step, packed, near)
    arrived, hidden = lax.optimization_barrier((arrived, hidden))
    fine_ghosts, send_ghosts, rim_ghosts, coarse_step, packed, near = hidden
    own = arrived.reshape(total, LANES)[: Q * tiles * k_count]

    padded = PAD + fine_rows + PAD
    to_left, to_right, low, first = call(
        functools.partial(send_body, ch_count, k_count),
        [f32(sent_rows(nq), LANES)] * 2 + [f32(PLANES, SUB, LANES)] * 2,
        [VMEM] * 2,
        [
            pltpu.VMEM((Q, nq, SUB, LANES), jnp.float32),
            pltpu.VMEM((Q, nq, 3 * PAD, LANES), jnp.float32),
            pltpu.VMEM((10, nq, 3 * PAD, LANES), jnp.float32),
        ],
    )(own, send_ghosts)
    left = lax.ppermute(to_right, "grp", ring(n_grp, 1))
    right = lax.ppermute(to_left, "grp", ring(n_grp, -1))
    inner = call(
        functools.partial(inner_body, ch_count, k_count),
        f32(Q, nq, PAD + B + PAD, LANES),
        [VMEM] * 2,
        [pltpu.VMEM((10, nq, PAD + B + PAD, LANES), jnp.float32)],
        flops=10**7,
    )(own, fine_ghosts)
    highs = []
    for across in (0, 1, -1):
        highs.append(lax.ppermute(first, axes, slab_pairs(n_grp, n_wide, -1, across)))

    fine = call(
        functools.partial(fine_body, ch_count, k_count),
        f32(Q * B * nq, LANES),
        [VMEM] * 6,
        [
            pltpu.VMEM((Q * nq * SUB, LANES), jnp.float32),
            pltpu.VMEM((Q, nq, padded, LANES), jnp.float32),
            pltpu.VMEM((Q, nq, padded, LANES), jnp.float32),
            pltpu.VMEM((10, nq, padded, LANES), jnp.float32),
            pltpu.VMEM((Q * B * nq, LANES), jnp.float32),
            pltpu.SemaphoreType.DMA((PIECES,)),
        ],
        flops=10**7,
        place=HBM,
    )(own, left, right, inner, fine_ghosts, rim_ghosts)

    coarse_out = call(
        functools.partial(edges_body, ch_count, k_count, planes),
        f32(Q, cx, cz, cy),
        [VMEM] * 9,
        [
            pltpu.VMEM((PLANES, LANES, LANES), jnp.float32),
            pltpu.VMEM((PLANES, LANES, LANES), jnp.float32),
            pltpu.VMEM((Q, SUB, LANES), jnp.float32),
            pltpu.VMEM((Q, cx, cz, cy), jnp.float32),
            pltpu.SemaphoreType.DMA((PIECES,)),
        ],
        place=HBM,
    )(left, right, low, *highs, packed, near, coarse_step)

    fine_out = fine.reshape(Q, tiles, k_count, LANES).transpose(2, 0, 1, 3)
    fine_out = fine_out.reshape(k_count, q_count, cells)
    return fine_out, coarse_out


def solution(mesh):
    return jax.shard_map(
        local,
        mesh=mesh,
        in_specs=(P(("grp", "wide"), None, None), P(None, "grp", None, "wide"), P()),
        out_specs=(P(("grp", "wide"), None, None), P(None, "grp", None, "wide")),
        check_vma=False,
    )
```

```python
import functools

import jax
import jax.numpy as jnp
from jax import lax
from jax.experimental import pallas as pl
from jax.experimental.layout import Layout, with_layout_constraint
from jax.experimental.pallas import tpu as pltpu
from jax.sharding import PartitionSpec as P


B = 16
LANES = 128
SUB = 8
HALO = 4
PAD = 8
GRANT = 24 << 20
PIECES = 4

VELOCITIES = (
    (0, 0, 0),
    (1, 0, 0),
    (-1, 0, 0),
    (0, 1, 0),
    (0, -1, 0),
    (0, 0, 1),
    (0, 0, -1),
    (1, 1, 0),
    (-1, -1, 0),
    (1, -1, 0),
    (-1, 1, 0),
    (1, 0, 1),
    (-1, 0, -1),
    (1, 0, -1),
    (-1, 0, 1),
    (0, 1, 1),
    (0, -1, -1),
    (0, 1, -1),
    (0, -1, 1),
)
Q = len(VELOCITIES)
WEIGHTS = (1.0 / 3.0,) + (1.0 / 18.0,) * 6 + (1.0 / 36.0,) * 12
W_DIAG = WEIGHTS[7]
COUPLING = -5.0
FINE_TAU = 1.1
COARSE_TAU = 0.8
TO_COARSE = 2.0 * COARSE_TAU / FINE_TAU
TO_FINE = FINE_TAU / (2.0 * COARSE_TAU)
UP = tuple(i for i in range(Q) if VELOCITIES[i][1] == 1)
DOWN = tuple(i for i in range(Q) if VELOCITIES[i][1] == -1)
NG = len(UP) + 1

VMEM = pl.BlockSpec(memory_space=pltpu.VMEM)
HBM = pl.BlockSpec(memory_space=pl.ANY)


def call(body, outs, specs, scratch=(), flops=10**6, moved=10**6, place=VMEM):
    return pl.pallas_call(
        body,
        out_shape=outs,
        in_specs=specs,
        out_specs=jax.tree.map(lambda _: place, outs),
        scratch_shapes=list(scratch),
        cost_estimate=pl.CostEstimate(flops=flops, bytes_accessed=moved, transcendentals=0),
        compiler_params=pltpu.CompilerParams(vmem_limit_bytes=GRANT),
    )


def f32(*shape):
    return jax.ShapeDtypeStruct(shape, jnp.float32)


def moments(f):
    density = f[0]
    momentum = [None, None, None]
    for i in range(1, Q, 2):
        density = density + (f[i] + f[i + 1])
        odd = f[i] - f[i + 1]
        for j in range(3):
            c = VELOCITIES[i][j]
            if c:
                term = odd if c > 0 else -odd
                if momentum[j] is None:
                    momentum[j] = term
                else:
                    momentum[j] = momentum[j] + odd if c > 0 else momentum[j] - odd
    return density, momentum


def balances(density, flux, scale):
    w = density * (W_DIAG * scale)
    half = 1.5 / density
    v = [x * half for x in flux]
    g = [x * (3.0 * W_DIAG * scale) for x in flux]
    g2 = [x + x for x in g]
    h = [g[j] * v[j] for j in range(3)]
    total = h[0] + h[1] + h[2]
    base = w - total * (1.0 / 3.0)
    base2 = base + base
    yield 0, base2 * (0.5 * WEIGHTS[0] / W_DIAG)
    for j in range(3):
        even = base2 + (h[j] + h[j])
        yield 2 * j + 1, even + g2[j]
        yield 2 * j + 2, even - g2[j]
    all_h = base + total
    i = 7
    for a, b, c in ((0, 1, 2), (0, 2, 1), (1, 2, 0)):
        even = all_h - h[c]
        cross = g2[a] * v[b]
        for sign in (1, -1):
            side = even + cross if sign > 0 else even - cross
            odd = g[a] + g[b] if sign > 0 else g[a] - g[b]
            yield i, side + odd
            yield i + 1, side - odd
            i += 2


def rescaled(f, factor, wanted):
    density, momentum = moments(f)
    found = {}
    for i, balance in balances(density, momentum, 1.0):
        if i in wanted:
            found[i] = balance + factor * (f[i] - balance)
    return 1.0 - jnp.exp(-density), found


def gradient_parts(p, shift_y, shift_z):
    above = shift_y(p, -1, "p")
    below = shift_y(p, 1, "p")
    front = shift_z(p, -1)
    back = shift_z(p, 1)
    n = range(len(p))
    dy = [above[q] - below[q] for q in n]
    dz = [front[q] - back[q] for q in n]
    mixed = [(p[q] + p[q]) + (above[q] + below[q]) for q in n]
    tx = [mixed[q] + (front[q] + back[q]) for q in n]
    mixed_front = shift_z(mixed, -1)
    mixed_back = shift_z(mixed, 1)
    dy_front = shift_z(dy, -1)
    dy_back = shift_z(dy, 1)
    gy = [(dy[q] + dy[q]) + (dy_front[q] + dy_back[q]) for q in n]
    gz = [mixed_front[q] - mixed_back[q] for q in n]
    return tx, dy, dz, gy, gz


def flux_of(momentum, potential, pull, tau):
    force = (-tau * COUPLING * W_DIAG) * potential
    return [momentum[j] + force * pull[j] for j in range(3)]


def regroup_body(blocks, k_blocks, rows, target_ref, in_ref, out_ref):
    targets = target_ref[...]
    for b in range(blocks):
        source = (b // k_blocks) * (rows * k_blocks) + b % k_blocks
        out_ref[pl.ds(targets[0, b], rows, stride=k_blocks), :] = in_ref[
            pl.ds(source, rows, stride=k_blocks), :
        ]


def lane_ids():
    lane = lax.broadcasted_iota(jnp.int32, (SUB, LANES), 1)
    return lane % B, lane // B


def fine_shifts(ch_count, k_count, ghost):
    y, z = lane_ids()
    first_y, last_y = y == 0, y == B - 1
    first_z, last_z = z == 0, z == LANES // B - 1

    def shift_y(v, c, which):
        out = []
        for ch in range(ch_count):
            for k in range(k_count):
                q = ch * k_count + k
                if c > 0:
                    own = pltpu.roll(v[q], 1, 1)
                    carry = (
                        ghost(0, which, ch) if k == 0 else pltpu.roll(v[q - 1], LANES - (B - 1), 1)
                    )
                    out.append(jnp.where(first_y, carry, own))
                else:
                    own = pltpu.roll(v[q], LANES - 1, 1)
                    carry = (
                        ghost(1, which, ch)
                        if k == k_count - 1
                        else pltpu.roll(v[q + 1], B - 1, 1)
                    )
                    out.append(jnp.where(last_y, carry, own))
        return out

    def shift_z(v, c):
        rolled = [pltpu.roll(x, B if c > 0 else LANES - B, 1) for x in v]
        edge = first_z if c > 0 else last_z
        out = []
        for ch in range(ch_count):
            other = (ch - c) % ch_count
            for k in range(k_count):
                q = ch * k_count + k
                out.append(jnp.where(edge, rolled[other * k_count + k], rolled[q]))
        return out

    def shift_both(v, cy, cz, which):
        edge_y = first_y if cy > 0 else last_y
        edge_z = first_z if cz > 0 else last_z
        turn = B * cz
        moved = []
        for ch in range(ch_count):
            for k in range(k_count):
                q = ch * k_count + k
                own = pltpu.roll(v[q], (turn + cy) % LANES, 1)
                if k == (0 if cy > 0 else k_count - 1):
                    carry = ghost(0 if cy > 0 else 1, which, ch)
                else:
                    carry = pltpu.roll(v[q - cy], (turn - cy * (B - 1)) % LANES, 1)
                moved.append(jnp.where(edge_y, carry, own))
        return [
            jnp.where(edge_z, moved[(ch - cz) % ch_count * k_count + k], moved[ch * k_count + k])
            for ch in range(ch_count)
            for k in range(k_count)
        ]

    return shift_y, shift_z, shift_both


def substep(load, store, ghosts, start, parts, ch_count, k_count, chunks, density_of=None):
    qs = range(ch_count * k_count)
    for chunk in range(chunks):
        r = chunk * SUB

        def ghost(side, which, ch, r=r):
            return ghosts[side, NG - 1, ch, pl.ds(start + r, SUB), :]

        moved = [moments([load(i, q, r) for i in range(Q)]) for q in qs]
        density = [moved[q][0] for q in qs]
        if density_of is not None:
            density = [density_of(q, r, density[q]) for q in qs]
        p = [1.0 - jnp.exp(-density[q]) for q in qs]
        shift_y, shift_z, shift_both = fine_shifts(ch_count, k_count, ghost)
        tx, dy, dz, gy, gz = gradient_parts(p, shift_y, shift_z)
        for q in qs:
            values = (tx[q], dy[q], dz[q], gy[q], gz[q], p[q], density[q], *moved[q][1])
            for n, v in enumerate(values):
                parts[n, q, pl.ds(PAD + r, SUB), :] = v
    for chunk in range(chunks):
        r = chunk * SUB

        def ghost(side, which, ch, r=r):
            place = (UP if side == 0 else DOWN).index(which)
            return ghosts[side, place, ch, pl.ds(start + r, SUB), :]

        shift_y, shift_z, shift_both = fine_shifts(ch_count, k_count, ghost)
        streams = []
        for q in qs:
            low = [parts[n, q, pl.ds(PAD + r - 1, SUB), :] for n in range(3)]
            high = [parts[n, q, pl.ds(PAD + r + 1, SUB), :] for n in range(3)]
            gy, gz, p, rho, mx, my, mz = (
                parts[n, q, pl.ds(PAD + r, SUB), :] for n in range(3, 10)
            )
            pull = [high[0] - low[0], gy + (high[1] + low[1]), gz + (high[2] + low[2])]
            flux = flux_of((mx, my, mz), p, pull, FINE_TAU)
            streams.append(balances(rho, flux, 1.0 / FINE_TAU))
        for i in range(Q):
            cx, cy, cz = VELOCITIES[i]
            post = []
            for q in qs:
                _, balance = next(streams[q])
                post.append(load(i, q, r) * (1.0 - 1.0 / FINE_TAU) + balance)
            if cy and cz:
                post = shift_both(post, cy, cz, i)
            elif cy:
                post = shift_y(post, cy, i)
            elif cz:
                post = shift_z(post, cz)
            for q in qs:
                store(i, q, r, cx, post[q])


CROSS = 5
FROM_DENSITY = Q
FROM_ENTER = Q + 1
FROM_PARTIAL = Q + 1 + CROSS
SENT = Q + 2 + CROSS


def edge_rows(nq):
    return SENT * nq + PLANES * (HALO // 2)


def sent_rows(nq):
    return -(-edge_rows(nq) // SUB) * SUB


def parts_of(count, pieces):
    cuts = [count * n // pieces for n in range(pieces + 1)]
    return list(zip(cuts[:-1], cuts[1:]))


def along(c):
    return [i for i in range(Q) if VELOCITIES[i][0] == c]


def restrict_body(ch_count, k_count, own, low, high):
    nq = ch_count * k_count

    def restricted(i, q, half):
        return own[pl.ds(i * (B * nq) + half * nq + q, SUB, stride=2 * nq), :]

    for side, out in enumerate((low, high)):
        for n, plane in enumerate(pack(restricted, ch_count, k_count, side)):
            out[n] = plane


def send_body(ch_count, k_count, own, ghosts, to_left, to_right, low, high, rim, moved, parts):
    nq = ch_count * k_count
    per = B * nq
    edge = HALO // 2

    for i in range(Q):
        for q in range(nq):
            rim[i, q, pl.ds(0, HALO), :] = own[pl.ds(i * per + q, HALO, stride=nq), :]
            rim[i, q, pl.ds(HALO, HALO), :] = own[
                pl.ds(i * per + (B - HALO) * nq + q, HALO, stride=nq), :
            ]

    def load(i, q, r):
        return rim[i, q]

    def store(i, q, r, cx, v):
        moved[i, q, pl.ds(PAD + cx, SUB), :] = v

    substep(load, store, ghosts, 0, parts, ch_count, k_count, 1)

    @pl.loop(0, 1)
    def _(_):
        restrict_body(ch_count, k_count, own, low, high)

    for c, out, outer in ((1, to_right, B - 1), (-1, to_left, 0)):
        first = PAD + (SUB - 1 if c > 0 else 0)
        second = first - c
        for i in range(Q):
            out[pl.ds(i * nq, nq), :] = own[pl.ds(i * per + outer * nq, nq), :]
        for q in range(nq):
            out[pl.ds(FROM_DENSITY * nq + q, 1), :] = parts[6, q, pl.ds(second, 1), :]
            for n, i in enumerate(along(c)):
                out[pl.ds((FROM_ENTER + n) * nq + q, 1), :] = moved[i, q, pl.ds(first, 1), :]
            total = None
            for i in along(0) + along(c):
                v = moved[i, q, pl.ds(second, 1), :]
                total = v if total is None else total + v
            out[pl.ds(FROM_PARTIAL * nq + q, 1), :] = total
        for n in range(PLANES):
            x = SUB - edge if c > 0 else 0
            out[pl.ds(SENT * nq + n * edge, edge), :] = low[n, pl.ds(x, edge), :]
        spare = sent_rows(nq) - edge_rows(nq)
        if spare:
            out[pl.ds(edge_rows(nq), spare), :] = jnp.zeros((spare, LANES), jnp.float32)


def inner_body(ch_count, k_count, own, ghosts, out, parts):
    nq = ch_count * k_count

    def load(i, q, r):
        return own[pl.ds(i * (B * nq) + r * nq + q, SUB, stride=nq), :]

    def store(i, q, r, cx, v):
        out[i, q, pl.ds(PAD + r + cx, SUB), :] = v

    substep(load, store, ghosts, HALO, parts, ch_count, k_count, B // SUB)


def fine_body(
    ch_count, k_count, own, left, right, inner, ghosts, rim_ghosts, out, rim, half, third, parts, held, sems
):
    nq = ch_count * k_count
    per = B * nq
    row = lax.broadcasted_iota(jnp.int32, (SUB, LANES), 0)
    origin = PAD + HALO

    layers = Q * nq
    rim[pl.ds(1, layers, stride=SUB), :] = left[pl.ds(0, layers), :]
    rim[pl.ds(6, layers, stride=SUB), :] = right[pl.ds(0, layers), :]
    for i in range(Q):
        for sub, x in ((2, 0), (3, 1), (4, B - 2), (5, B - 1)):
            rim[pl.ds(i * (nq * SUB) + sub, nq, stride=SUB), :] = own[
                pl.ds(i * per + x * nq, nq), :
            ]

    def spread(ref, plane, q):
        return jnp.broadcast_to(ref[pl.ds(plane * nq + q, 1), :], (SUB, LANES))

    def load_rim(i, q, r):
        return rim[pl.ds((i * nq + q) * SUB, SUB), :]

    def rim_density(q, r, density):
        density = jnp.where(row == 0, spread(left, FROM_DENSITY, q), density)
        return jnp.where(row == SUB - 1, spread(right, FROM_DENSITY, q), density)

    outgoing = {(c, q): None for c in (-1, 1) for q in range(nq)}

    def store_rim(i, q, r, cx, v):
        half[i, q, pl.ds(origin - 2 + cx, SUB), :] = v
        half[i, q, pl.ds(origin + B - 6 + cx, SUB), :] = v
        if cx:
            seen = outgoing[cx, q]
            outgoing[cx, q] = v if seen is None else seen + v

    substep(load_rim, store_rim, rim_ghosts, 0, parts, ch_count, k_count, 1, rim_density)
    for i in range(Q):
        cx = VELOCITIES[i][0]
        for q in range(nq):
            half[i, q, pl.ds(origin + 1 + cx, B - 2), :] = inner[i, q, pl.ds(PAD + 1 + cx, B - 2), :]
            if cx:
                ref = left if cx > 0 else right
                at = origin - 1 if cx > 0 else origin + B
                place = FROM_ENTER + along(cx).index(i)
                half[i, q, pl.ds(at, 1), :] = ref[pl.ds(place * nq + q, 1), :]

    def load(i, q, r):
        return half[i, q, pl.ds(PAD + r, SUB), :]

    def store(i, q, r, cx, v):
        third[i, q, pl.ds(PAD + r + cx, SUB), :] = v

    chunks = (B + 2 * HALO) // SUB

    def density_of(q, r, density):
        if r == 0:
            value = spread(left, FROM_PARTIAL, q) + pltpu.roll(outgoing[-1, q], 1, 0)
            return jnp.where(row == HALO - 2, value, density)
        if r == (chunks - 1) * SUB:
            value = spread(right, FROM_PARTIAL, q) + pltpu.roll(outgoing[1, q], SUB - 1, 0)
            return jnp.where(row == SUB - HALO + 1, value, density)
        return density

    substep(load, store, ghosts, 0, parts, ch_count, k_count, chunks, density_of)

    copies = []
    for n, (i0, i1) in enumerate(parts_of(Q, PIECES)):
        for i in range(i0, i1):
            for q in range(nq):
                held[pl.ds(i * per + q, B, stride=nq), :] = third[i, q, pl.ds(origin, B), :]
        part = pl.ds(i0 * per, (i1 - i0) * per)
        copies.append(pltpu.make_async_copy(held.at[part], out.at[part], sems.at[n]))
        copies[-1].start()
    for copy in copies:
        copy.wait()


def fine_ghost_body(ch_count, rows, layers, spread, out, send_ghosts, rim_ghosts, wide):
    for side in range(2):
        wide[...] = jnp.dot(
            layers[side],
            spread[...],
            precision=lax.Precision.HIGHEST,
            preferred_element_type=jnp.float32,
        )
        wanted = UP if side == 0 else DOWN
        for ch in range(ch_count):
            for r in range(0, rows, SUB):
                f = [
                    wide[pl.ds(i * rows + r, SUB), pl.ds(ch * LANES, LANES)] for i in range(Q)
                ]
                potential, found = rescaled(f, TO_FINE, wanted)
                for n, i in enumerate(wanted):
                    v, cz = found[i], VELOCITIES[i][2]
                    if cz:
                        v = pltpu.roll(v, B * cz % LANES, 1)
                    out[side, n, ch, pl.ds(r, SUB), :] = v
                out[side, NG - 1, ch, pl.ds(r, SUB), :] = potential
            for n in range(NG):
                for ref, lower, upper in (
                    (send_ghosts, HALO, rows - 2 * HALO),
                    (rim_ghosts, 2, rows - HALO - 2),
                ):
                    ref[side, n, ch, pl.ds(0, HALO), :] = out[side, n, ch, pl.ds(lower, HALO), :]
                    ref[side, n, ch, pl.ds(HALO, HALO), :] = out[
                        side, n, ch, pl.ds(upper, HALO), :
                    ]


STEP = 2 * B
GROUP = B // 2
PLANES = -(-2 * Q // STEP)


def place_of(i, ch):
    group, at = divmod(2 * i + ch, GROUP)
    plane, quarter = divmod(group, 4)
    return plane, 2 * at + quarter % 2 + B * (quarter // 2)


def pack(load, ch_count, k_count, side):
    lane = lax.broadcasted_iota(jnp.int32, (SUB, LANES), 1)
    offset = B - 2 if side == 0 else 0
    layers = lane % B // 2 == offset // 2
    kept = (lane % STEP < B) & (lane % 2 == 0)
    k = k_count - 1 if side == 0 else 0
    slots = [(i, ch) for i in range(Q) for ch in range(ch_count)]
    planes = [None] * PLANES
    for first in range(0, len(slots), GROUP):
        total = None
        for at, (i, ch) in enumerate(slots[first : first + GROUP]):
            q = ch * k_count + k
            v = jnp.where(layers, load(i, q, 0) + load(i, q, 1), 0.0)
            shift = (2 * at - offset) % LANES
            if shift:
                v = pltpu.roll(v, shift, 1)
            total = v if total is None else total + v
        total = total + pltpu.roll(total, LANES - 1, 1)
        total = total + pltpu.roll(total, LANES - B, 1)
        total = jnp.where(kept, total, 0.0)
        plane, shift = place_of(*slots[first])
        if shift:
            total = pltpu.roll(total, shift, 1)
        planes[plane] = total if planes[plane] is None else planes[plane] + total
    return planes


def coarse_body(planes, state, out, packed, near, parts, out_pad):
    lane = lax.broadcasted_iota(jnp.int32, (SUB, LANES), 1)

    def shift_y(v, c, which):
        return [pltpu.roll(v[0], 1 if c > 0 else LANES - 1, 1)]

    def shift_z(v, c):
        return [pltpu.roll(v[0], 1 if c > 0 else SUB - 1, 0)]

    def prepare(x, carry):
        density, momentum = moments([state[i, x] for i in range(Q)])
        p = 1.0 - jnp.exp(-density)
        values = gradient_parts([p], shift_y, shift_z)
        values = [v[0] for v in values] + [p, density, *momentum]
        for n, v in enumerate(values):
            parts[n, x] = v
        return carry

    lax.fori_loop(0, planes, prepare, 0, unroll=2)

    inner = planes - HALO
    base = HALO // 2

    def update(x, carry):
        lower = [parts[n, x - 1] for n in range(3)]
        upper = [parts[n, x + 1] for n in range(3)]
        gy, gz, p, rho, mx, my, mz = (parts[n, x] for n in range(3, 10))
        pull = [upper[0] - lower[0], gy + (upper[1] + lower[1]), gz + (upper[2] + lower[2])]
        flux = flux_of((mx, my, mz), p, pull, COARSE_TAU)
        for i, balance in balances(rho, flux, 1.0 / COARSE_TAU):
            cx, cy, cz = VELOCITIES[i]
            post = [state[i, x] * (1.0 - 1.0 / COARSE_TAU) + balance]
            if cy:
                post = shift_y(post, cy, i)
            if cz:
                post = shift_z(post, cz)
            inside = x + cx - base
            spare = jnp.where((inside >= 0) & (inside < inner), inside, inner)
            out_pad[i, spare] = post[0]
        return carry

    lax.fori_loop(base - 1, base + inner + 1, update, 0, unroll=2)
    out[...] = out_pad[:, :inner]

    def gather(i, carry):
        total = jnp.zeros((SUB, LANES), jnp.float32)
        for x in range(planes):
            here = (lane == 2 * x + 1) | (lane == 2 * x + 2)
            total = jnp.where(here, pltpu.roll(state[i, x], 2 * x + 2, 1), total)
        packed[i] = total
        return carry

    lax.fori_loop(0, Q, gather, 0)
    total = jnp.zeros((SUB, LANES), jnp.float32)
    for x in range(planes):
        p = parts[5, x]
        total = jnp.where(lane == 2 * x + 2, pltpu.roll(p, 2 * x + 1, 1), total)
        total = jnp.where(lane == 2 * x + 1, pltpu.roll(p, 2 * x + 3, 1), total)
    near[...] = total


def edges_body(
    ch_count, k_count, planes, left, right, low, high, high_left, high_right, packed, near, step,
    out, rows, columns, ghost, held, sems,
):
    nq = ch_count * k_count
    edge = HALO // 2
    inner = planes - HALO
    lane = lax.broadcasted_iota(jnp.int32, (SUB, LANES), 1)
    sided = lane % 2 == 0

    for n in range(PLANES):
        own_x = 2 * edge
        rows[n, pl.ds(2 + own_x, inner, stride=2), :] = low[n]
        beside = SENT * nq + n * edge
        rows[n, pl.ds(2, edge, stride=2), :] = left[pl.ds(beside, edge), :]
        rows[n, pl.ds(2 + 2 * (edge + inner), edge, stride=2), :] = right[
            pl.ds(beside, edge), :
        ]
        rows[n, pl.ds(1 + own_x, inner, stride=2), :] = high[n]
        rows[n, pl.ds(1, edge, stride=2), :] = high_left[n, pl.ds(inner - edge, edge), :]
        rows[n, pl.ds(1 + 2 * (edge + inner), edge, stride=2), :] = high_right[
            n, pl.ds(0, edge), :
        ]
        columns[n, :, pl.ds(0, STEP)] = rows[n, pl.ds(0, STEP), :].T
    per = LANES // STEP
    for i in range(Q):
        for ch in range(ch_count):
            plane, at = place_of(i, ch)
            ghost[i, pl.ds(ch * per, per), :] = (
                0.125 * columns[plane, pl.ds(at, per, stride=STEP), :]
            )

    beyond, entering = rescaled([ghost[i] for i in range(Q)], TO_COARSE, UP + DOWN)
    density, momentum = moments([packed[i] for i in range(Q)])
    p = 1.0 - jnp.exp(-density)
    inside = near[...]
    above = jnp.where(sided, inside, beyond)
    below = jnp.where(sided, beyond, inside)

    def shift_y(v, c, which):
        return [below if c > 0 else above]

    def shift_z(v, c):
        return [pltpu.roll(v[0], 1 if c > 0 else SUB - 1, 0)]

    def shift_x(v, c):
        return pltpu.roll(v, 2 if c > 0 else LANES - 2, 1) if c else v

    tx, dy, dz, gy, gz = (v[0] for v in gradient_parts([p], shift_y, shift_z))
    pull = [
        shift_x(tx, -1) - shift_x(tx, 1),
        gy + (shift_x(dy, -1) + shift_x(dy, 1)),
        gz + (shift_x(dz, -1) + shift_x(dz, 1)),
    ]
    flux = flux_of(momentum, p, pull, COARSE_TAU)
    copies = []
    for i, balance in balances(density, flux, 1.0 / COARSE_TAU):
        cx, cy, cz = VELOCITIES[i]
        v = packed[i] * (1.0 - 1.0 / COARSE_TAU) + balance
        if cy > 0:
            v = jnp.where(sided, entering[i], pltpu.roll(v, 1, 1))
            touched = lane < 2
        elif cy < 0:
            v = jnp.where(sided, pltpu.roll(v, LANES - 1, 1), entering[i])
            touched = lane >= LANES - 2
        else:
            touched = (lane == 0) | (lane == LANES - 1)
        v = shift_x(v, cx)
        if cz:
            v = shift_z([v], cz)[0]
        for x in range(inner):
            column = pltpu.roll(v, LANES - (2 * (x + edge) + 2), 1)
            held[i, x] = jnp.where(touched, column, step[i, x])
        for n, (i0, i1) in enumerate(parts_of(Q, PIECES)):
            if i == i1 - 1:
                part = pl.ds(i0, i1 - i0)
                copies.append(pltpu.make_async_copy(held.at[part], out.at[part], sems.at[n]))
                copies[-1].start()
    for copy in copies:
        copy.wait()


def ring(count, step):
    return [(i, (i + step) % count) for i in range(count)]


def slab_pairs(n_grp, n_wide, up, across):
    return [
        (g * n_wide + w, (g + across) % n_grp * n_wide + (w + up) % n_wide)
        for g in range(n_grp)
        for w in range(n_wide)
    ]


def local(fine_pop, coarse_pop, new_slot):
    k_count, q_count, cells = fine_pop.shape
    blocks = new_slot.shape[0]
    devices = blocks // k_count
    tiles = cells // LANES
    ch_count = tiles // B
    nq = ch_count * k_count
    axes = ("grp", "wide")
    n_grp, n_wide = lax.axis_size("grp"), lax.axis_size("wide")
    _, cx, cz, cy = coarse_pop.shape
    planes = cx + HALO
    fine_rows = B + 2 * HALO

    rows = pl.cdiv(Q * tiles, devices)
    pieces = fine_pop.reshape(k_count, Q, tiles, LANES)
    pieces = with_layout_constraint(pieces, Layout(major_to_minor=(1, 2, 0, 3)))
    pieces = pieces.transpose(1, 2, 0, 3)
    pieces = pieces.reshape(Q * tiles, k_count, LANES)
    if rows * devices != Q * tiles:
        pieces = jnp.pad(pieces, ((0, rows * devices - Q * tiles), (0, 0), (0, 0)))
    pieces = pieces.reshape(devices, rows, k_count, LANES)
    spread = lax.all_to_all(pieces, axes, 0, 0, tiled=True)
    edge = HALO // 2
    coarse_left = lax.ppermute(coarse_pop[:, cx - edge :], "grp", ring(n_grp, 1))
    coarse_right = lax.ppermute(coarse_pop[:, :edge], "grp", ring(n_grp, -1))
    last = coarse_pop[..., -1]
    below = []
    for part, across in ((last[:, cx - edge :], 1), (last, 0), (last[:, :edge], -1)):
        below.append(lax.ppermute(part, axes, slab_pairs(n_grp, n_wide, 1, across)))
    total = devices * rows * k_count
    regroup = call(
        functools.partial(regroup_body, blocks, k_count, rows),
        f32(total, LANES),
        [VMEM, VMEM],
        moved=8 * total * LANES,
    )
    targets = rows * new_slot - (rows - 1) * (new_slot % k_count)
    outgoing = regroup(targets[None], spread.reshape(total, LANES))
    arrived = lax.all_to_all(
        outgoing.reshape(devices, rows, k_count, LANES), axes, 0, 0, tiled=True
    )
    coarse = jnp.concatenate([coarse_left, coarse_pop, coarse_right], axis=1)
    below = jnp.concatenate(below, axis=1)
    layers = jnp.repeat(jnp.stack([below, coarse[..., 0]]), 2, axis=2)
    layers = layers.reshape(2, Q * fine_rows, cz)
    lane = jnp.arange(ch_count * LANES) // (2 * B)
    one_hot = (jnp.arange(cz)[:, None] == lane[None, :]).astype(jnp.float32)
    fine_ghosts, send_ghosts, rim_ghosts = call(
        functools.partial(fine_ghost_body, ch_count, fine_rows),
        [f32(2, NG, ch_count, n, LANES) for n in (fine_rows, SUB, SUB)],
        [VMEM, VMEM],
        [pltpu.VMEM((Q * fine_rows, ch_count * LANES), jnp.float32)],
    )(layers, one_hot)
    coarse_step, packed, near = call(
        functools.partial(coarse_body, planes),
        [f32(Q, cx, cz, cy), f32(Q, SUB, LANES), f32(SUB, LANES)],
        [VMEM],
        [
            pltpu.VMEM((10, planes, SUB, LANES), jnp.float32),
            pltpu.VMEM((Q, cx + 1, SUB, LANES), jnp.float32),
        ],
        flops=10**7,
    )(coarse)
    hidden = (fine_ghosts, send_ghosts, rim_ghosts, coarse_step, packed, near)
    arrived, hidden = lax.optimization_barrier((arrived, hidden))
    fine_ghosts, send_ghosts, rim_ghosts, coarse_step, packed, near = hidden
    own = arrived.reshape(total, LANES)[: Q * tiles * k_count]

    padded = PAD + fine_rows + PAD
    to_left, to_right, low, first = call(
        functools.partial(send_body, ch_count, k_count),
        [f32(sent_rows(nq), LANES)] * 2 + [f32(PLANES, SUB, LANES)] * 2,
        [VMEM] * 2,
        [
            pltpu.VMEM((Q, nq, SUB, LANES), jnp.float32),
            pltpu.VMEM((Q, nq, 3 * PAD, LANES), jnp.float32),
            pltpu.VMEM((10, nq, 3 * PAD, LANES), jnp.float32),
        ],
    )(own, send_ghosts)
    left = lax.ppermute(to_right, "grp", ring(n_grp, 1))
    right = lax.ppermute(to_left, "grp", ring(n_grp, -1))
    inner = call(
        functools.partial(inner_body, ch_count, k_count),
        f32(Q, nq, PAD + B + PAD, LANES),
        [VMEM] * 2,
        [pltpu.VMEM((10, nq, PAD + B + PAD, LANES), jnp.float32)],
        flops=10**7,
    )(own, fine_ghosts)
    highs = []
    for across in (0, 1, -1):
        highs.append(lax.ppermute(first, axes, slab_pairs(n_grp, n_wide, -1, across)))

    fine = call(
        functools.partial(fine_body, ch_count, k_count),
        f32(Q * B * nq, LANES),
        [VMEM] * 6,
        [
            pltpu.VMEM((Q * nq * SUB, LANES), jnp.float32),
            pltpu.VMEM((Q, nq, padded, LANES), jnp.float32),
            pltpu.VMEM((Q, nq, padded, LANES), jnp.float32),
            pltpu.VMEM((10, nq, padded, LANES), jnp.float32),
            pltpu.VMEM((Q * B * nq, LANES), jnp.float32),
            pltpu.SemaphoreType.DMA((PIECES,)),
        ],
        flops=10**7,
        place=HBM,
    )(own, left, right, inner, fine_ghosts, rim_ghosts)

    coarse_out = call(
        functools.partial(edges_body, ch_count, k_count, planes),
        f32(Q, cx, cz, cy),
        [VMEM] * 9,
        [
            pltpu.VMEM((PLANES, LANES, LANES), jnp.float32),
            pltpu.VMEM((PLANES, LANES, LANES), jnp.float32),
            pltpu.VMEM((Q, SUB, LANES), jnp.float32),
            pltpu.VMEM((Q, cx, cz, cy), jnp.float32),
            pltpu.SemaphoreType.DMA((PIECES,)),
        ],
        place=HBM,
    )(left, right, low, *highs, packed, near, coarse_step)

    fine_out = fine.reshape(Q, tiles, k_count, LANES).transpose(2, 0, 1, 3)
    fine_out = fine_out.reshape(k_count, q_count, cells)
    return fine_out, coarse_out


def solution(mesh):
    return jax.shard_map(
        local,
        mesh=mesh,
        in_specs=(P(("grp", "wide"), None, None), P(None, "grp", None, "wide"), P()),
        out_specs=(P(("grp", "wide"), None, None), P(None, "grp", None, "wide")),
        check_vma=False,
    )
```
